32 devices in a mesh: shard: 2 (over y), context: 4 (over x, core), tensor: 4 (over z).
Axes of the slice: x: 2, y: 2, z: 4, core: 2. Of those that a mesh axis runs over, the one named last changes fastest.
Arguments:
- tokens: bfloat16 [5120, 1088], P(('shard', 'context', 'tensor')), may hold values from -6 to 6
- segments: int32 [2, 2560], P('shard', ('context', 'tensor')), may hold values from 0 to 5, never falling along the last dimension, each value on 1 to 1920 neighbouring positions
- w_qkv: bfloat16 [1088, 3264], P('shard'), may hold values from -0.1875 to 0.1875
- w_out: bfloat16 [1088, 1088], P('shard'), may hold values from -1.5 to 1.5
- ln1_gain: bfloat16 [1088], P('shard'), may hold values from 0.5 to 1.5
- ln1_bias: bfloat16 [1088], P('shard'), may hold values from -3 to 3
- ln2_gain: bfloat16 [1088], P('shard'), may hold values from 0.5 to 1.5
- ln2_bias: bfloat16 [1088], P('shard'), may hold values from -3 to 3
- w_up: bfloat16 [1088, 4352], P('shard', 'tensor'), may hold values from -0.1875 to 0.1875
- w_down: bfloat16 [4352, 1088], P('tensor', 'shard'), may hold values from -0.09375 to 0.09375
- out_grad: bfloat16 [5120, 1088], P(('shard', 'context', 'tensor')), may hold values from -6 to 6
Outputs:
- result: bfloat16 [5120, 1088], P(('shard', 'context', 'tensor'))
- input_grad: bfloat16 [5120, 1088], P(('shard', 'context', 'tensor'))
- grad_w_qkv: float32 [1088, 3264], P('shard')
- grad_w_out: float32 [1088, 1088], P('shard')
- grad_ln1_gain: float32 [1088], P('shard')
- grad_ln1_bias: float32 [1088], P('shard')
- grad_ln2_gain: float32 [1088], P('shard')
- grad_ln2_bias: float32 [1088], P('shard')
- grad_w_up: float32 [1088, 4352], P('shard', 'tensor')
- grad_w_down: float32 [4352, 1088], P('tensor', 'shard')
The draws below stay inside these ranges and needn't reach their ends.
Inputs may be any that keep to these rules, and one draw needn't show every extreme that they name: `segments`: row s lists the sequence numbers of the 2560 tokens of shard index s in order; they never fall, each of the 6 sequences has 1 to 1920 tokens, and one has exactly 1920.
All inputs are finite; a program needn't handle non-finite values.
Results may differ from the reference program's by a relative error of at most 0.012.
Values may be sent and summed in bfloat16 or wider, within the bound.
No kernel may reach another device: no remote copies, remote signals or barrier semaphores. Data moves between devices by JAX's collectives and lax.ppermute only.
A program may use at most 192 MiB of HBM per device.

```python
import math
import jax
import jax.numpy as jnp
import numpy as np
from jax import lax

D = 1088
HEADS = 17
FF = 4352
HEAD_DIM = 64
GROUP_TOK = 2560
SEQ_MAX = 1920
SEQS = 6
TOKENS = 5120
N_SHARD = 2


def level_of(key, extent, pieces, smallest, top_value):
    level = 1.0
    for axis_at, shards_of in pieces:
        heights = jax.random.uniform(jax.random.fold_in(jax.random.fold_in(key, 6), axis_at), (shards_of,), jnp.float32, smallest / len(pieces), top_value / len(pieces))
        level = level * jnp.repeat(jnp.exp(heights), extent[axis_at] // shards_of).reshape((-1,) + (1,) * (len(extent) - 1 - axis_at))
    return level


def length_profile(count, total, reach, skew):
    loads = [(1 << 20) // math.isqrt(grade ** skew) + 1 for grade in range(2, count + 1)]
    spare, counts = total - reach - (count - 1), [1] * (count - 1)
    while spare > 0:
        movable = [i for i in range(count - 1) if counts[i] < reach]
        pool, left = sum([loads[i] for i in movable]), spare
        for i in movable:
            more = min(reach - counts[i], max(1, left * loads[i] // pool), spare)
            counts[i] = counts[i] + more
            spare = spare - more
    return np.array([reach] + counts)


def uneven(stream_key, count, total, bound, slope):
    if count == 2:
        one = jax.random.randint(stream_key, (), max(1, total - bound), min(bound, total - 1) + 1)
        return jnp.stack([one, total - one])
    sizes = jnp.asarray(length_profile(count, total, bound, slope), jnp.int32)
    couples = (count - 1) // 2
    giver, taker = sizes[1:1 + 2 * couples:2], sizes[2:2 + 2 * couples:2]
    slack = jnp.minimum(giver - 1, bound - taker)
    moved = jax.random.randint(jax.random.fold_in(stream_key, 1), (couples,), 0, 1 << 20) % (slack + 1)
    sizes = sizes.at[1:1 + 2 * couples:2].set(giver - moved).at[2:2 + 2 * couples:2].set(taker + moved)
    return sizes[jax.random.permutation(jax.random.fold_in(stream_key, 2), count)]


def bell_draw(stream_key, shape, deviation, limit, pieces=(), kind=jnp.bfloat16):
    values = jax.random.normal(stream_key, shape, jnp.float32) * deviation
    if len(pieces) > 0:
        values = level_of(stream_key, shape, pieces, -0.22, 0.18) * values
    return jnp.clip(values, min=-limit, max=limit).astype(kind)


def setup_inputs(seed: int = 0) -> dict:
    seeds = jax.random.split(jax.random.key(seed), 12)
    tokens = bell_draw(seeds[0], (TOKENS, D), 1.0, 6.0, ((0, 32),))
    segments = jax.vmap(lambda own: jnp.searchsorted(jnp.cumsum(uneven(own, SEQS, GROUP_TOK, SEQ_MAX, 1)), jnp.arange(GROUP_TOK), side="right"))(jax.random.split(seeds[1], N_SHARD)).reshape((N_SHARD, GROUP_TOK)).astype(jnp.int32)
    w_qkv = bell_draw(seeds[2], (D, 3 * D), D ** -0.5, 0.1875, ((0, 2),))
    w_out = bell_draw(seeds[3], (D, D), (D // 64) ** -0.5, 1.5, ((0, 2),))
    ln1_gain = jnp.clip(1.0 + 0.1 * jax.random.normal(seeds[4], (D,), jnp.float32), 0.5, 1.5).astype(jnp.bfloat16)
    ln1_bias = bell_draw(seeds[5], (D,), 0.5, 3.0, ((0, 2),))
    ln2_gain = jnp.clip(1.0 + 0.1 * jax.random.normal(seeds[6], (D,), jnp.float32), 0.5, 1.5).astype(jnp.bfloat16)
    ln2_bias = bell_draw(seeds[7], (D,), 0.5, 3.0, ((0, 2),))
    w_up = bell_draw(seeds[8], (D, FF), D ** -0.5, 0.1875, ((0, 2), (1, 4)))
    w_down = bell_draw(seeds[9], (FF, D), FF ** -0.5, 0.09375, ((0, 4), (1, 2)))
    out_grad = bell_draw(seeds[10], (TOKENS, D), 1.0, 6.0, ((0, 32),))
    return dict(tokens=tokens, segments=segments, w_qkv=w_qkv, w_out=w_out, ln1_gain=ln1_gain, ln1_bias=ln1_bias, ln2_gain=ln2_gain, ln2_bias=ln2_bias, w_up=w_up, w_down=w_down, out_grad=out_grad)


@jax.custom_vjp
def low(v):
    return lax.optimization_barrier(v.astype(jnp.bfloat16)).astype(jnp.float32)

@jax.custom_vjp
def low_back(v):
    return v

def low_keep(v):
    return (low(v), None)

def low_pass(kept, grad):
    return (grad,)

def back_keep(v):
    return (v, None)

def back_low(kept, grad):
    return (low(grad),)
low.defvjp(low_keep, low_pass)
low_back.defvjp(back_keep, back_low)
HIGHEST = lax.Precision.HIGHEST
EPSILON = 1e-05

def layer_norm(values, gain, shift):
    average = lax.optimization_barrier(jnp.mean(values, axis=-1, keepdims=True))
    centred = values - average
    variance = lax.optimization_barrier(jnp.mean(centred * centred, axis=-1, keepdims=True))
    return centred * lax.rsqrt(variance + EPSILON) * gain + shift

def product(left, right):
    return jnp.dot(left, right, precision=HIGHEST, preferred_element_type=jnp.float32)

def attend_block(start, queries, keys, values, seq_ids):
    count = queries.shape[0]
    scale = 1.0 / math.sqrt(HEAD_DIM)
    query_seq = lax.dynamic_slice_in_dim(seq_ids, start, count)
    query_pos = start + jnp.arange(count, dtype=jnp.int32)
    key_pos = jnp.arange(keys.shape[0], dtype=jnp.int32)
    allowed = (key_pos[None, :] <= query_pos[:, None]) & (seq_ids[None, :] == query_seq[:, None])
    q_heads = queries.reshape(count, HEADS, HEAD_DIM).transpose(1, 0, 2)
    k_heads = keys.reshape(-1, HEADS, HEAD_DIM).transpose(1, 0, 2)
    v_heads = values.reshape(-1, HEADS, HEAD_DIM).transpose(1, 0, 2)
    scores = low_back(jnp.einsum('hqd,hkd->hqk', q_heads, k_heads, precision=HIGHEST) * scale)
    scores = jnp.where(allowed[None], scores, -1e+30)
    highest = lax.optimization_barrier(jnp.max(scores, axis=-1, keepdims=True))
    log_total = highest + jnp.log(lax.optimization_barrier(jnp.sum(jnp.exp(scores - highest), axis=-1, keepdims=True)))
    shares = low(jnp.exp(scores - log_total))
    joined = jnp.einsum('hqk,hkd->hqd', shares, v_heads, precision=HIGHEST)
    return joined.transpose(1, 0, 2).reshape(count, HEADS * HEAD_DIM)

def forward(inputs, seq_ids, w_qkv, w_out, gain_one, bias_one, gain_two, bias_two, w_up, w_down):
    width = inputs.shape[1]
    normed_one = low(layer_norm(inputs, gain_one, bias_one))
    projected = low(low_back(product(normed_one, w_qkv)))
    queries = projected[:, :width]
    keys = projected[:, width:2 * width]
    values = projected[:, 2 * width:]
    blocks = 8
    block_rows = inputs.shape[0] // blocks
    starts = jnp.arange(blocks, dtype=jnp.int32) * block_rows
    stacked = queries.reshape(blocks, block_rows, width)
    step_fn = jax.checkpoint(attend_block)
    attended = lax.map(lambda item: step_fn(item[0], item[1], keys, values, seq_ids), (starts, stacked))
    attended = low(low_back(attended.reshape(-1, width)))
    resid = inputs + low_back(product(attended, w_out))
    normed_two = low(layer_norm(resid, gain_two, bias_two))
    pre = low_back(product(normed_two, w_up))
    hidden = low(jax.nn.gelu(pre, approximate=True))
    return resid + product(hidden, w_down)

def reference(tokens, segments, w_qkv, w_out, ln1_gain, ln1_bias, ln2_gain, ln2_bias, w_up, w_down, out_grad):
    params = (w_qkv.astype(jnp.float32), w_out.astype(jnp.float32), ln1_gain.astype(jnp.float32), ln1_bias.astype(jnp.float32), ln2_gain.astype(jnp.float32), ln2_bias.astype(jnp.float32), w_up.astype(jnp.float32), w_down.astype(jnp.float32))
    width = tokens.shape[1]
    inputs = tokens.astype(jnp.float32).reshape(N_SHARD, -1, width)
    cotangents = out_grad.astype(jnp.float32).reshape(N_SHARD, -1, width)

    def one_group(totals, item):
        group_in, group_seq, group_ct = item

        def run(values, *weights):
            return forward(values, group_seq, *weights)
        output, pull = jax.vjp(run, group_in, *params)
        pulled = pull(group_ct)
        totals = tuple((before + added for before, added in zip(totals, pulled[1:])))
        return (totals, (output, pulled[0]))
    zeros = tuple((jnp.zeros_like(weight) for weight in params))
    totals, (outputs, in_grads) = lax.scan(one_group, zeros, (inputs, segments, cotangents))
    return (outputs.reshape(-1, width).astype(jnp.bfloat16), in_grads.reshape(-1, width).astype(jnp.bfloat16), totals[0], totals[1], totals[2], totals[3], totals[4], totals[5], totals[6], totals[7])
```

```python
import functools
import math

import jax
import jax.numpy as jnp
from jax import lax
from jax.experimental import pallas as pl
from jax.experimental.pallas import tpu as pltpu
from jax.sharding import PartitionSpec as P

HEADS = 17
HEAD_DIM = 64
SEQS = 6
EPSILON = 1e-05
NEG = -1e30
GROUP = ("context", "tensor")
TILE = 256
BF = jnp.bfloat16
F32 = jnp.float32


def contract(left, right, left_dim, right_dim):
    return lax.dot_general(
        left, right, (((left_dim,), (right_dim,)), ((), ())), preferred_element_type=F32
    )


def norm_stats(values):
    average = jnp.mean(values, axis=-1, keepdims=True)
    centred = values - average
    variance = jnp.mean(centred * centred, axis=-1, keepdims=True)
    inverse = lax.rsqrt(variance + EPSILON)
    return centred * inverse, inverse


def norm_back(grad, unit, inverse, gain):
    scaled = grad * gain
    first = jnp.mean(scaled, axis=-1, keepdims=True)
    second = jnp.mean(scaled * unit, axis=-1, keepdims=True)
    return inverse * (scaled - first - unit * second)


def swap_shard(part):
    return lax.ppermute(part, "shard", [(0, 1), (1, 0)])


def in_order(mine, other, axis):
    index = lax.axis_index("shard")
    return jnp.where(
        index == 0,
        jnp.concatenate([mine, other], axis=axis),
        jnp.concatenate([other, mine], axis=axis),
    )


def gather_small(part, count, axis):
    if count != 2:
        return lax.all_gather(part, "shard", axis=axis, tiled=True)
    return in_order(part, swap_shard(part), axis)


def gather_large(part, count, axis):
    if count != 2:
        return lax.all_gather(part, "shard", axis=axis, tiled=True)
    ways = lax.axis_size("context")
    core = lax.rem(lax.axis_index("context"), 2)
    half = part.shape[axis] // 2
    mine = lax.dynamic_slice_in_dim(part, core * half, half, axis)
    fetched = swap_shard(mine)
    partner = lax.ppermute(fetched, "context", [(i, i ^ 1) for i in range(ways)])
    other = jnp.where(
        core == 0,
        jnp.concatenate([fetched, partner], axis=axis),
        jnp.concatenate([partner, fetched], axis=axis),
    )
    return in_order(part, other, axis)


def sum_shard_rows(partial, count):
    if count != 2:
        return lax.psum_scatter(
            partial.astype(BF), "shard", scatter_dimension=0, tiled=True
        ).astype(F32)
    rows = partial.shape[0] // 2
    index = lax.axis_index("shard")
    away = lax.dynamic_slice_in_dim(partial, (1 - index) * rows, rows, 0).astype(BF)
    kept = lax.dynamic_slice_in_dim(partial, index * rows, rows, 0)
    return kept + swap_shard(away).astype(F32)


def pick_half(pair, high, scale=1.0):
    first = lax.broadcasted_iota(jnp.int32, pair.shape, 1) < HEAD_DIM
    values = pair.astype(F32) * scale
    return (jnp.where(first, 0.0, values) if high else jnp.where(first, values, 0.0)).astype(BF)


def lane_ids(count):
    return lax.broadcasted_iota(jnp.int32, (1, count), 1)


def band(shape, low, high, first_key):
    key = first_key + lax.broadcasted_iota(jnp.int32, shape, 0)
    return (key >= low) & (key <= high)


def forward_kernel(
    own, seq_own, nat, tr, packed, out_nat, lse, out_last, lse_last, start, start_own, end_own, meta,
    q_pad,
):
    rows = nat.shape[0]
    blocks = rows // TILE
    width = out_last.shape[0]
    scale = 1.0 / math.sqrt(HEAD_DIM)

    seq = tr[256:272, :].astype(F32)[0:1, :]
    mine = seq_own[...]
    begin = jnp.zeros_like(seq)
    begin_own = jnp.zeros_like(mine)
    finish_own = jnp.full_like(mine, float(rows))
    for number in range(1, SEQS):
        before = jnp.sum((seq < number).astype(F32), axis=1, keepdims=True)
        begin = jnp.where(seq >= number, before, begin)
        begin_own = jnp.where(mine >= number, before, begin_own)
        finish_own = jnp.where(mine == number - 1, before, finish_own)
    start[...] = begin.astype(jnp.int32)
    start_own[...] = begin_own.astype(jnp.int32)
    end_own[...] = finish_own.astype(jnp.int32)
    base = pl.multiple_of(own[0], 16)
    meta[2 * blocks] = jnp.min(begin_own).astype(jnp.int32) // TILE
    meta[2 * blocks + 1] = (base + width - 1) // TILE + 1
    meta[2 * blocks + 2] = base // width
    meta[2 * blocks + 3] = (jnp.max(finish_own).astype(jnp.int32) + width - 1) // width

    def scores_of(queries, kb):
        at = pl.multiple_of(kb * TILE, TILE)
        return contract(nat[pl.ds(at, TILE), 128:256], queries, 1, 1), at

    def weigh(shares, v_row, at):
        return contract(tr[v_row : v_row + HEAD_DIM, pl.ds(at, TILE)], shares.astype(BF), 1, 0)

    def step(queries, limits, v_row, kb, carry):
        top, total, acc = carry
        scores, at = scores_of(queries, kb)
        if limits is not None:
            scores = jnp.where(band(scores.shape, *limits, at), scores, NEG)
        now = jnp.maximum(top, jnp.max(scores, axis=0, keepdims=True))
        fade = jnp.exp(top - now)
        shares = jnp.exp(scores - now)
        total = total * fade + jnp.sum(shares, axis=0, keepdims=True)
        return now, total, acc * fade + weigh(shares, v_row, at)

    def one_block(qb, unused):
        at = pl.multiple_of(qb * TILE, TILE)
        queries = pick_half(nat[pl.ds(at, TILE), 0:128], False, scale)
        low = start[:, pl.ds(at, TILE)]
        near = low.astype(F32)
        first = jnp.min(near).astype(jnp.int32) // TILE
        full = jnp.minimum((jnp.max(near).astype(jnp.int32) + TILE - 1) // TILE, qb)
        meta[qb] = first
        meta[blocks + qb] = full
        limits = (low, at + lane_ids(TILE))
        scores, at_key = scores_of(queries, qb)
        scores = jnp.where(band(scores.shape, *limits, at_key), scores, NEG)
        top = jnp.max(scores, axis=0, keepdims=True)
        shares = jnp.exp(scores - top)
        carry = (top, jnp.sum(shares, axis=0, keepdims=True), weigh(shares, 128, at_key))
        carry = lax.fori_loop(first, full, functools.partial(step, queries, limits, 128), carry)
        carry = lax.fori_loop(full, qb, functools.partial(step, queries, None, 128), carry)
        top, total, acc = carry
        lse[:, pl.ds(at, TILE)] = top + jnp.log(total)
        out_nat[pl.ds(at, TILE), :] = (acc / total).T
        return unused

    lax.fori_loop(0, blocks, one_block, 0)

    q_pad[...] = jnp.zeros_like(q_pad)
    q_pad[0:width, :] = pick_half(nat[pl.ds(base, width), 0:128], True, scale)
    limits = (start_own[...], base + lane_ids(TILE))
    carry = (
        jnp.full((1, TILE), NEG, F32),
        jnp.zeros((1, TILE), F32),
        jnp.zeros((HEAD_DIM, TILE), F32),
    )
    top, total, acc = lax.fori_loop(
        meta[2 * blocks],
        meta[2 * blocks + 1],
        functools.partial(step, q_pad[...], limits, 192),
        carry,
    )
    lse_last[...] = top + jnp.log(total)
    out_last[...] = (acc / total).T[0:width, :]

    half = width // 2
    for dest in range(rows // width):
        first = out_nat[dest * width : dest * width + half, :]
        second = out_nat[dest * width + half : (dest + 1) * width, :]
        packed[dest] = jnp.concatenate([first, second], axis=1).astype(BF)


def backward_last_kernel(
    own, meta, start_own, end_own, nat, tr, came, lse_own, delta_own, last_qk, last_v,
    q_rows, o_rows, pad_q, pad_o,
):
    rows = nat.shape[0]
    blocks = rows // TILE
    width = last_qk.shape[0]
    scale = 1.0 / math.sqrt(HEAD_DIM)
    base = pl.multiple_of(own[0], 16)

    q_rows[0:rows, :] = (nat[:, 0:128].astype(F32) * scale).astype(BF)
    q_rows[rows:, :] = jnp.zeros((q_rows.shape[0] - rows, 2 * HEAD_DIM), BF)
    for source in range(rows // width):
        o_rows[source * width : (source + 1) * width, :] = came[source, 0:width, :]
    o_rows[rows:, :] = jnp.zeros((o_rows.shape[0] - rows, 2 * HEAD_DIM), BF)

    pad_q[...] = jnp.zeros_like(pad_q)
    pad_o[...] = jnp.zeros_like(pad_o)
    pad_q[0:width, :] = pick_half(nat[pl.ds(base, width), 0:128], True, scale)
    pad_o[0:width, :] = pick_half(o_rows[pl.ds(base, width), :], True)
    limits = (start_own[...], base + lane_ids(TILE))

    def query_step(kb, d_query):
        at = pl.multiple_of(kb * TILE, TILE)
        scores = contract(nat[pl.ds(at, TILE), 128:256], pad_q[...], 1, 1)
        scores = jnp.where(band(scores.shape, *limits, at), scores, NEG)
        shares = jnp.exp(scores - lse_own[...])
        d_shares = contract(nat[pl.ds(at, TILE), 256:384], pad_o[...], 1, 1)
        d_scores = (shares * (d_shares - delta_own[...])).astype(BF)
        return d_query + contract(tr[HEAD_DIM : 2 * HEAD_DIM, pl.ds(at, TILE)], d_scores, 1, 0)

    d_query = lax.fori_loop(
        meta[2 * blocks], meta[2 * blocks + 1], query_step, jnp.zeros((HEAD_DIM, TILE), F32)
    )
    last_qk[:, 0:HEAD_DIM] = (d_query.T[0:width, :] * scale).astype(BF)

    keys = pick_half(nat[pl.ds(base, width), 128:256], True)
    values = pick_half(nat[pl.ds(base, width), 256:384], True)
    key = base + lax.broadcasted_iota(jnp.int32, (width, TILE), 0)
    finish = jnp.broadcast_to(end_own[...].astype(F32), (128, TILE)).T[0:width, 0:1]
    finish = finish.astype(jnp.int32)
    lane = lane_ids(TILE)

    def key_step(source, carry):
        d_key, d_value = carry
        at = pl.multiple_of(source * width, 16)
        queries = q_rows[pl.ds(at, TILE), :]
        grads = o_rows[pl.ds(at, TILE), :]
        facts = came[source, width : width + 16, :].astype(F32)
        log_total = jnp.concatenate([facts[0:1] + facts[2:3], facts[1:2] + facts[3:4]], axis=1)
        delta = jnp.concatenate([facts[4:5] + facts[6:7], facts[5:6] + facts[7:8]], axis=1)
        query = at + lane
        keep = (key <= query) & (query < finish) & (lane < width)
        scores = jnp.where(keep, contract(keys, queries, 1, 1), NEG)
        shares = jnp.exp(scores - log_total)
        d_shares = contract(values, grads, 1, 1)
        d_scores = (shares * (d_shares - delta)).astype(BF)
        return (
            d_key + contract(d_scores, queries, 1, 0),
            d_value + contract(shares.astype(BF), grads, 1, 0),
        )

    zero = jnp.zeros((width, 2 * HEAD_DIM), F32)
    d_key, d_value = lax.fori_loop(
        meta[2 * blocks + 2], meta[2 * blocks + 3], key_step, (zero, zero)
    )
    last_qk[:, HEAD_DIM:] = d_key[:, HEAD_DIM:].astype(BF)
    last_v[...] = d_value[:, HEAD_DIM:].astype(BF)


def backward_kernel(
    meta, start, nat, tr, came, out_nat, lse, packed, d_qk, d_v, o_rows, q_rows, acc_k, acc_v
):
    rows = nat.shape[0]
    blocks = rows // TILE
    width = rows // packed.shape[0]
    scale = 1.0 / math.sqrt(HEAD_DIM)

    q_rows[...] = (nat[:, 0:128].astype(F32) * scale).astype(BF)
    for source in range(rows // width):
        o_rows[source * width : (source + 1) * width, :] = came[source, 0:width, :]
    acc_k[...] = jnp.zeros_like(acc_k)
    acc_v[...] = jnp.zeros_like(acc_v)

    def one_block(qb, unused):
        at_q = pl.multiple_of(qb * TILE, TILE)
        pair = q_rows[pl.ds(at_q, TILE), :]
        queries = pick_half(pair, False)
        grads = o_rows[pl.ds(at_q, TILE), :]
        product = grads[:, 0:HEAD_DIM].astype(F32) * out_nat[pl.ds(at_q, TILE), :]
        delta = jnp.sum(product.T, axis=0, keepdims=True)
        grads_low = pick_half(grads, False)
        log_total = lse[:, pl.ds(at_q, TILE)]
        limits = (start[:, pl.ds(at_q, TILE)], at_q + lane_ids(TILE))

        def step(masked, kb, d_query):
            at = pl.multiple_of(kb * TILE, TILE)
            scores = contract(nat[pl.ds(at, TILE), 128:256], queries, 1, 1)
            if masked:
                scores = jnp.where(band(scores.shape, *limits, at), scores, NEG)
            shares = jnp.exp(scores - log_total)
            d_shares = contract(nat[pl.ds(at, TILE), 256:384], grads_low, 1, 1)
            d_scores = (shares * (d_shares - delta)).astype(BF)
            acc_v[pl.ds(at, TILE), :] += contract(shares.astype(BF), grads, 1, 0)
            acc_k[pl.ds(at, TILE), :] += contract(d_scores, pair, 1, 0)
            return d_query + contract(tr[0:HEAD_DIM, pl.ds(at, TILE)], d_scores, 1, 0)

        d_query = step(True, qb, jnp.zeros((HEAD_DIM, TILE), F32))
        full = meta[blocks + qb]
        d_query = lax.fori_loop(meta[qb], full, functools.partial(step, True), d_query)
        d_query = lax.fori_loop(full, qb, functools.partial(step, False), d_query)
        d_qk[pl.ds(at_q, TILE), 0:HEAD_DIM] = (d_query.T * scale).astype(BF)
        return unused

    lax.fori_loop(0, blocks, one_block, 0)
    d_qk[:, HEAD_DIM:] = acc_k[:, 0:HEAD_DIM].astype(BF)
    d_v[...] = acc_v[:, 0:HEAD_DIM].astype(BF)
    half = width // 2
    for dest in range(rows // width):
        low_rows = slice(dest * width, dest * width + half)
        high_rows = slice(dest * width + half, (dest + 1) * width)
        packed[dest, 0:width, :] = d_qk[dest * width : (dest + 1) * width, :]
        packed[dest, width:, :] = jnp.concatenate([d_v[low_rows, :], d_v[high_rows, :]], axis=1)


def kernel_call(kernel, scalars, operands, outs, scratch, work, smem_out=None):
    vmem = pl.BlockSpec(memory_space=pltpu.VMEM)
    smem = pl.BlockSpec(memory_space=pltpu.SMEM)
    out_shape = [jax.ShapeDtypeStruct(shape, kind) for shape, kind in outs]
    out_specs = [vmem] * len(outs)
    if smem_out is not None:
        out_shape.append(jax.ShapeDtypeStruct((smem_out,), jnp.int32))
        out_specs.append(smem)
    return pl.pallas_call(
        kernel,
        out_shape=tuple(out_shape),
        in_specs=[smem] * len(scalars) + [vmem] * len(operands),
        out_specs=tuple(out_specs),
        scratch_shapes=[pltpu.VMEM(shape, kind) for shape, kind in scratch],
        cost_estimate=pl.CostEstimate(flops=work, bytes_accessed=8 << 20, transcendentals=0),
    )(*scalars, *operands)


def attend_forward(own, seq_own, nat, tr, width):
    rows = nat.shape[0]
    pair = 2 * HEAD_DIM
    return kernel_call(
        forward_kernel,
        (own,),
        (seq_own, nat, tr),
        [
            ((rows // width, width // 2, pair), BF),
            ((rows, HEAD_DIM), F32),
            ((1, rows), F32),
            ((width, HEAD_DIM), F32),
            ((1, TILE), F32),
            ((1, rows), jnp.int32),
            ((1, TILE), jnp.int32),
            ((1, TILE), jnp.int32),
        ],
        [((TILE, pair), BF)],
        16 * rows * rows * HEAD_DIM,
        2 * (rows // TILE) + 4,
    )


def attend_backward_last(own, meta, start_own, end_own, nat, tr, came, lse_own, delta_own, width):
    rows = nat.shape[0]
    pair = 2 * HEAD_DIM
    return kernel_call(
        backward_last_kernel,
        (own, meta),
        (start_own, end_own, nat, tr, came, lse_own, delta_own),
        [((width, pair), BF), ((width, HEAD_DIM), BF)],
        [((rows + TILE - width, pair), BF)] * 2 + [((TILE, pair), BF)] * 2,
        4 * rows * rows * HEAD_DIM,
    )


def attend_backward(meta, start, nat, tr, came, out_nat, lse, width):
    rows = nat.shape[0]
    pair = 2 * HEAD_DIM
    return kernel_call(
        backward_kernel,
        (meta,),
        (start, nat, tr, came, out_nat, lse),
        [
            ((rows // width, width + width // 2, pair), BF),
            ((rows, pair), BF),
            ((rows, HEAD_DIM), BF),
        ],
        [((rows, pair), BF)] * 2 + [((rows, pair), F32)] * 2,
        40 * rows * rows * HEAD_DIM,
    )


def join_kernel(pieces, shared, weights, joined, dots):
    heads = pieces.shape[0]
    total = jnp.zeros((joined.shape[0], 2 * HEAD_DIM), F32)
    rest = 0.0
    units = 3 * (heads + 1)

    def unit(index):
        part, head = divmod(index, heads + 1)
        columns = slice(part * HEAD_DIM, (part + 1) * HEAD_DIM)
        return shared[:, columns] if head == heads else pieces[head, :, columns]

    for block in range((units + 1) // 2):
        paired = 2 * block + 1 < units
        if paired:
            values = jnp.concatenate([unit(2 * block), unit(2 * block + 1)], axis=1)
        else:
            values = unit(2 * block)
        at = slice(2 * block * HEAD_DIM, 2 * block * HEAD_DIM + values.shape[1])
        values = values.astype(F32)
        joined[:, at] = values
        values = values * weights[:, at].astype(F32)
        if paired:
            total = total + values
        else:
            rest = jnp.sum(values, axis=1, keepdims=True)
    dots[...] = jnp.sum(total, axis=1, keepdims=True) + rest


def join_heads(pieces, shared, weights):
    heads, _, columns = pieces.shape
    rows = weights.shape[0]
    step = 272 if rows % 272 == 0 else rows
    return pl.pallas_call(
        join_kernel,
        grid=(rows // step,),
        out_shape=(
            jax.ShapeDtypeStruct(weights.shape, F32),
            jax.ShapeDtypeStruct((rows, 1), F32),
        ),
        in_specs=[
            pl.BlockSpec((heads, step, columns), lambda i: (0, i, 0)),
            pl.BlockSpec((step, shared.shape[1]), lambda i: (i, 0)),
            pl.BlockSpec((step, weights.shape[1]), lambda i: (i, 0)),
        ],
        out_specs=(
            pl.BlockSpec((step, weights.shape[1]), lambda i: (i, 0)),
            pl.BlockSpec((step, 1), lambda i: (i, 0)),
        ),
        cost_estimate=pl.CostEstimate(flops=1 << 20, bytes_accessed=14 << 20, transcendentals=0),
        name="join_heads",
    )(pieces, shared, weights)


def split_two(values):
    high = values.astype(BF)
    low = (values - high.astype(F32)).astype(BF)
    return [high, low]


def round_up(value, step):
    return (value + step - 1) // step * step


def to_tensor(part, ways):
    spread = jnp.broadcast_to(part[None], (ways,) + part.shape)
    got = lax.all_to_all(spread, "tensor", 0, 0, tiled=True)
    return got.reshape(ways * part.shape[0], part.shape[1])


def sum_tensor(partial, ways):
    rows = partial.shape[0] // ways
    got = lax.all_to_all(
        partial.astype(BF).reshape(ways, rows, partial.shape[1]), "tensor", 0, 0, tiled=True
    )
    return jnp.sum(got.astype(F32), axis=0)


def head_columns(matrix, head, width):
    return [
        lax.dynamic_slice_in_dim(matrix, part * width + head * HEAD_DIM, HEAD_DIM, 1)
        for part in range(3)
    ]


def gelu_pair(pre):
    factor = math.sqrt(2.0 / math.pi)
    square = pre * pre
    bend = jnp.tanh(factor * (pre + 0.044715 * pre * square))
    value = 0.5 * pre * (1.0 + bend)
    slope = 0.5 * (1.0 + bend) + 0.5 * pre * (1.0 - bend * bend) * factor * (
        1.0 + 3.0 * 0.044715 * square
    )
    return value, slope


def after(value, *others):
    return lax.optimization_barrier((value,) + others)[0]


def shards(
    tokens, segments, w_qkv, w_out, ln1_gain, ln1_bias, ln2_gain, ln2_bias, w_up, w_down, out_grad
):
    rows, width = tokens.shape
    count = lax.axis_size("shard")
    ways_c = lax.axis_size("context")
    ways_t = lax.axis_size("tensor")
    ways = ways_c * ways_t
    part_rows = w_qkv.shape[0]
    device = lax.axis_index(GROUP)
    shared = HEADS - 1
    padded = round_up(width, 128)
    columns = 3 * HEAD_DIM

    vectors = gather_small(
        jnp.stack([ln1_gain, ln1_bias, ln2_gain, ln2_bias]), count, 1
    ).astype(F32)
    gain_one, bias_one, gain_two, bias_two = [vectors[i : i + 1] for i in range(4)]

    inputs = tokens.astype(F32)
    unit_one, inverse_one = norm_stats(inputs)
    low_one = (unit_one * gain_one + bias_one).astype(BF)
    seq_row = segments[0]
    wide_one = jnp.concatenate(
        [low_one, seq_row[:, None].astype(BF), jnp.zeros((rows, padded - width - 1), BF)], axis=1
    )
    rows_one = lax.all_gather(wide_one, GROUP, axis=0, tiled=True)

    mine = head_columns(w_qkv, device, width)
    last = [
        w_qkv[:, part * width + shared * HEAD_DIM : part * width + (shared + 1) * HEAD_DIM]
        for part in range(3)
    ]
    head_w = gather_small(
        jnp.concatenate([mine[0], last[0], mine[1], last[1], mine[2], last[2]], axis=1),
        count,
        0,
    )
    head_w = jnp.pad(head_w, ((0, padded - width), (0, 0)))
    mark = (jnp.arange(padded)[:, None] == width) & (jnp.arange(16)[None] == 0)
    turn_w = jnp.concatenate([head_w[:, 2 * HEAD_DIM :], mark.astype(BF)], axis=1)
    out_full = gather_large(w_out, count, 0)
    up_full = gather_large(w_up, count, 0)
    down_full = gather_large(w_down, count, 1)
    qkv_full = gather_large(w_qkv, count, 0)
    grads_all = lax.all_gather(out_grad, "tensor", axis=0, tiled=True)
    split = ways * HEAD_DIM
    out_wide = jnp.concatenate(
        [
            out_full[:split].reshape(ways, HEAD_DIM, width),
            jnp.broadcast_to(out_full[None, split:], (ways, HEAD_DIM, width)),
        ],
        axis=1,
    ).reshape(2 * split, width)

    own = (device * rows).reshape(1).astype(jnp.int32)
    seq_own = jnp.concatenate(
        [seq_row, jnp.broadcast_to(seq_row[-1:], (TILE - rows,))]
    ).astype(F32)[None]
    nat = jnp.dot(rows_one, head_w, preferred_element_type=F32).astype(BF)
    tr = contract(turn_w, rows_one, 0, 1).astype(BF)
    packed, out_nat, lse, last_out, last_lse, start, start_own, end_own, meta = attend_forward(
        own, seq_own, nat, tr, rows
    )
    got = lax.all_to_all(packed, GROUP, 0, 0, tiled=True)
    half = rows // 2
    got = got.reshape(ways, half, 2, HEAD_DIM).transpose(2, 1, 0, 3).reshape(rows, split)
    attended = jnp.concatenate([got, last_out.astype(BF)], axis=1)

    resid = inputs + jnp.dot(attended, out_full, preferred_element_type=F32)
    unit_two, inverse_two = norm_stats(resid)
    low_two = (unit_two * gain_two + bias_two).astype(BF)

    d_hidden = contract(grads_all, down_full, 1, 1)
    rows_two = to_tensor(low_two, ways_t)
    hidden, slope = gelu_pair(jnp.dot(rows_two, up_full, preferred_element_type=F32))
    hidden = hidden.astype(BF)
    d_pre = (d_hidden * slope).astype(BF)
    d_normed_two = sum_tensor(contract(d_pre, up_full, 1, 1), ways_t)

    grad_up = contract(rows_two, d_pre, 0, 0).astype(BF)
    grad_down = contract(grads_all, hidden, 0, 0).astype(BF)
    pair = lax.psum_scatter(
        jnp.concatenate([grad_up, grad_down], axis=1),
        ("shard", "context"),
        scatter_dimension=0,
        tiled=True,
    )
    mixed = jnp.dot(hidden, down_full, preferred_element_type=F32).astype(BF)
    mixed = sum_tensor(after(mixed, d_normed_two), ways_t)
    result = (resid + mixed).astype(BF)

    grad_in = out_grad.astype(F32)
    d_resid = grad_in + norm_back(d_normed_two, unit_two, inverse_two, gain_two)
    d_branch = d_resid.astype(BF)

    d_wide = contract(d_branch, out_wide, 1, 1).astype(BF)
    last_grad = d_wide[:, HEAD_DIM : 2 * HEAD_DIM]
    last_delta = jnp.sum(last_grad.astype(F32) * last_out, axis=1)
    pieces = split_two(last_lse[0, :rows]) + split_two(last_delta)
    extra = jnp.pad(jnp.stack(pieces), ((0, 0), (0, TILE - rows))).reshape(8, 128)
    extra = jnp.pad(extra, ((0, 8), (0, 0)))
    payload = jnp.concatenate(
        [
            d_wide.reshape(rows, ways, 2 * HEAD_DIM).transpose(1, 0, 2),
            jnp.broadcast_to(extra[None], (ways,) + extra.shape),
        ],
        axis=1,
    )
    came = lax.all_to_all(payload, GROUP, 0, 0, tiled=True)
    delta_own = jnp.pad(last_delta, (0, TILE - rows))[None]

    grad_out_w = jnp.concatenate(
        [
            contract(attended, d_branch, 0, 0).astype(BF),
            jnp.sum(d_normed_two * unit_two, axis=0)[:, None].astype(BF),
            jnp.sum(d_normed_two, axis=0)[:, None].astype(BF),
            jnp.zeros((width, padded - width - 2), BF),
        ],
        axis=1,
    )
    grad_out_w = lax.psum_scatter(grad_out_w, ("shard", "context"), scatter_dimension=0, tiled=True)

    last_qk, last_v = attend_backward_last(
        own, meta, start_own, end_own, nat, tr, came, last_lse, delta_own, rows
    )
    last_all = jnp.concatenate([last_qk, last_v], axis=1)
    grad_last = sum_shard_rows(contract(low_one, last_all, 0, 0), count)
    chunk = round_up(-(-part_rows // ways), 16)
    grad_last = jnp.pad(grad_last.astype(BF), ((0, chunk * ways - part_rows), (0, 0)))
    grad_last = lax.all_to_all(
        grad_last.reshape(ways, chunk, columns), GROUP, 0, 0, tiled=True
    )
    grad_last = jnp.sum(grad_last.astype(F32), axis=0).astype(BF)

    packed, d_qk, d_v = attend_backward(meta, start, nat, tr, came, out_nat, lse, rows)
    came = lax.all_to_all(packed, GROUP, 0, 0, tiled=True)

    d_head = jnp.concatenate([d_qk, d_v], axis=1)
    grad_mine = contract(rows_one, d_head, 0, 0)[:width]
    sums = jnp.sum(d_head.astype(F32), axis=0).reshape(columns // 2, 2)
    sums_last = jnp.sum(last_all.astype(F32), axis=0).reshape(columns // 2, 2)
    sums = jnp.pad(
        jnp.concatenate([sums, sums_last], axis=1), ((0, part_rows - columns // 2), (0, 0))
    )
    away = jnp.concatenate([jnp.concatenate([grad_mine[i * part_rows : (i + 1) * part_rows], sums], axis=1) for i in range(count)], axis=0)
    both = sum_shard_rows(away, count)
    payload = jnp.concatenate(
        [both.astype(BF), jnp.pad(grad_last, ((0, 0), (0, 4)))], axis=0
    )
    pieces = lax.all_gather(payload, GROUP, axis=0, tiled=False)
    pieces = pieces.reshape(ways, part_rows + chunk, columns + 4)
    shared_w = pieces[:, part_rows:, :columns].reshape(ways * chunk, columns)[:part_rows]
    grad_qkv, dots = join_heads(pieces, shared_w, w_qkv)
    facts = pieces[:, : columns // 2, columns:].astype(F32)
    sums = facts[:, :, :2].reshape(ways, 3, HEAD_DIM)
    sums_last = jnp.sum(facts[:, :, 2:], axis=0).reshape(1, 3, HEAD_DIM)
    sums = jnp.concatenate([sums, sums_last], axis=0).transpose(1, 0, 2).reshape(1, 3 * width)
    grad_bias_one = jnp.sum(w_qkv.astype(F32) * sums, axis=1)
    grad_gain_one = (dots[:, 0] - ln1_bias.astype(F32) * grad_bias_one) / ln1_gain.astype(F32)

    pair = lax.all_gather(pair, "context", axis=0, tiled=True).astype(F32)
    grad_up = pair[:, : up_full.shape[1]]
    grad_down = pair[:, up_full.shape[1] :].T

    piece = part_rows // ways_c
    chunk = round_up(-(-piece // ways_t), 16)
    grad_out_w = jnp.pad(grad_out_w, ((0, chunk * ways_t - piece), (0, 0)))
    grad_out_w = lax.all_to_all(
        grad_out_w.reshape(ways_t, chunk, padded), "tensor", 0, 0, tiled=True
    )
    grad_out_w = jnp.sum(grad_out_w.astype(F32), axis=0).astype(BF)
    grad_out_w = lax.all_gather(grad_out_w, GROUP, axis=0, tiled=False)
    grad_out_w = grad_out_w.reshape(ways_c, chunk * ways_t, padded)[:, :piece]
    grad_out_w = grad_out_w.reshape(part_rows, padded).astype(F32)

    came_qk = came[:, :rows].reshape(ways, rows, 2, HEAD_DIM).transpose(1, 2, 0, 3)
    came_qk = came_qk.reshape(rows, 2, split)
    came_v = came[:, rows:].reshape(ways, half, 2, HEAD_DIM).transpose(2, 1, 0, 3)
    came_v = came_v.reshape(rows, 1, split)
    came = jnp.concatenate([came_qk, came_v], axis=1)
    d_projected = jnp.concatenate(
        [came, last_all.reshape(rows, 3, HEAD_DIM)], axis=2
    ).reshape(rows, 3 * width)
    d_normed_one = contract(d_projected, qkv_full, 1, 1)
    input_grad = (d_resid + norm_back(d_normed_one, unit_one, inverse_one, gain_one)).astype(BF)
    return (
        result,
        input_grad,
        grad_qkv,
        grad_out_w[:, :width],
        grad_gain_one,
        grad_bias_one,
        grad_out_w[:, width],
        grad_out_w[:, width + 1],
        grad_up,
        grad_down,
    )


def solution(mesh):
    in_specs = (
        P(("shard", "context", "tensor"), None),
        P("shard", ("context", "tensor")),
        P("shard", None),
        P("shard", None),
        P("shard"),
        P("shard"),
        P("shard"),
        P("shard"),
        P("shard", "tensor"),
        P("tensor", "shard"),
        P(("shard", "context", "tensor"), None),
    )
    out_specs = (
        P(("shard", "context", "tensor"), None),
        P(("shard", "context", "tensor"), None),
        P("shard", None),
        P("shard", None),
        P("shard"),
        P("shard"),
        P("shard"),
        P("shard"),
        P("shard", "tensor"),
        P("tensor", "shard"),
    )
    return jax.shard_map(shards, mesh=mesh, in_specs=in_specs, out_specs=out_specs, check_vma=False)
```

```python
import functools
import math

import jax
import jax.numpy as jnp
from jax import lax
from jax.experimental import pallas as pl
from jax.experimental.pallas import tpu as pltpu
from jax.sharding import PartitionSpec as P


HEADS = 17
HEAD_DIM = 64
SEQS = 6
EPSILON = 1e-05
NEG = -1e30
GROUP = ("context", "tensor")
TILE = 256
BF = jnp.bfloat16
F32 = jnp.float32


def contract(left, right, left_dim, right_dim):
    return lax.dot_general(
        left, right, (((left_dim,), (right_dim,)), ((), ())), preferred_element_type=F32
    )


def norm_stats(values):
    average = jnp.mean(values, axis=-1, keepdims=True)
    centred = values - average
    variance = jnp.mean(centred * centred, axis=-1, keepdims=True)
    inverse = lax.rsqrt(variance + EPSILON)
    return centred * inverse, inverse


def norm_back(grad, unit, inverse, gain):
    scaled = grad * gain
    first = jnp.mean(scaled, axis=-1, keepdims=True)
    second = jnp.mean(scaled * unit, axis=-1, keepdims=True)
    return inverse * (scaled - first - unit * second)


def swap_shard(part):
    return lax.ppermute(part, "shard", [(0, 1), (1, 0)])


def in_order(mine, other, axis):
    index = lax.axis_index("shard")
    return jnp.where(
        index == 0,
        jnp.concatenate([mine, other], axis=axis),
        jnp.concatenate([other, mine], axis=axis),
    )


def gather_small(part, count, axis):
    if count != 2:
        return lax.all_gather(part, "shard", axis=axis, tiled=True)
    return in_order(part, swap_shard(part), axis)


def gather_large(part, count, axis):
    if count != 2:
        return lax.all_gather(part, "shard", axis=axis, tiled=True)
    ways = lax.axis_size("context")
    core = lax.rem(lax.axis_index("context"), 2)
    half = part.shape[axis] // 2
    mine = lax.dynamic_slice_in_dim(part, core * half, half, axis)
    fetched = swap_shard(mine)
    partner = lax.ppermute(fetched, "context", [(i, i ^ 1) for i in range(ways)])
    other = jnp.where(
        core == 0,
        jnp.concatenate([fetched, partner], axis=axis),
        jnp.concatenate([partner, fetched], axis=axis),
    )
    return in_order(part, other, axis)


def swap_half(blocks, bit, axis, axis_name, pairs):
    kept = lax.dynamic_index_in_dim(blocks, bit, axis, keepdims=False)
    away = lax.dynamic_index_in_dim(blocks, 1 - bit, axis, keepdims=False).astype(BF)
    came = lax.ppermute(away, axis_name, pairs)
    return kept, came


def add(kept, came):
    return kept.astype(F32) + came.astype(F32)


def sum_shard_rows(partial, count):
    if count != 2:
        return lax.psum_scatter(
            partial.astype(BF), "shard", scatter_dimension=0, tiled=True
        ).astype(F32)
    index = lax.axis_index("shard")
    blocks = partial.reshape((2, -1) + partial.shape[1:])
    return add(*swap_half(blocks, index, 0, "shard", [(0, 1), (1, 0)]))


def reduce_rows(partial, count, ways_c, gates):
    if count != 2 or ways_c != 4:
        return lax.psum_scatter(partial, ("shard", "context"), scatter_dimension=0, tiled=True)
    context = lax.axis_index("context")
    core, chip = lax.rem(context, 2), lax.div(context, 2)
    rows, columns = partial.shape
    blocks = partial.reshape(2, 2, 2, rows // 8, columns)
    kept, came = swap_half(blocks, core, 2, "context", [(i, i ^ 1) for i in range(4)])
    blocks = add(kept, after(came, gates[0])).astype(BF)
    kept, came = swap_half(blocks, chip, 1, "context", [(i, i ^ 2) for i in range(4)])
    blocks = add(kept, after(came, gates[1])).astype(BF)
    kept, came = swap_half(blocks, lax.axis_index("shard"), 0, "shard", [(0, 1), (1, 0)])
    return add(kept, after(came, gates[2])).astype(BF)


def send_rows(part, ways_c):
    if ways_c != 4:
        return None
    return lax.ppermute(part, "context", [(i, i ^ 2) for i in range(4)])


def gather_rows(part, sent, ways_c):
    if ways_c != 4:
        return lax.all_gather(part, "context", axis=0, tiled=True)
    context = lax.axis_index("context")
    core, chip = lax.rem(context, 2), lax.div(context, 2)
    both = jnp.where(chip == 0, jnp.stack([part, sent]), jnp.stack([sent, part]))
    came = lax.ppermute(both, "context", [(i, i ^ 1) for i in range(4)])
    all_rows = jnp.where(
        core == 0, jnp.stack([both, came], axis=1), jnp.stack([came, both], axis=1)
    )
    return all_rows.reshape((4 * part.shape[0],) + part.shape[1:])


def rotate(blocks, ways, gate):
    index = lax.axis_index("tensor")
    shares = [lax.dynamic_index_in_dim(blocks, index, 0, keepdims=False)]
    for turn in range(1, ways):
        target = lax.rem(index + turn, ways)
        away = lax.dynamic_index_in_dim(blocks, target, 0, keepdims=False)
        away = after(away, gate)
        shares.append(lax.ppermute(away, "tensor", [(i, (i + turn) % ways) for i in range(ways)]))
    return shares


def total(shares):
    return sum(share.astype(F32) for share in shares)


def after(value, *others):
    return lax.optimization_barrier((value,) + others)[0]


def pick_half(pair, high, scale=1.0):
    first = lax.broadcasted_iota(jnp.int32, pair.shape, 1) < HEAD_DIM
    values = pair.astype(F32) * scale
    return (jnp.where(first, 0.0, values) if high else jnp.where(first, values, 0.0)).astype(BF)


def lane_ids(count):
    return lax.broadcasted_iota(jnp.int32, (1, count), 1)


def band(shape, low, high, first_key):
    key = first_key + lax.broadcasted_iota(jnp.int32, shape, 0)
    return (key >= low) & (key <= high)


def forward_kernel(
    own, seq_own, nat, tr, packed, out_nat, lse, out_last, lse_last, start, start_own, end_own, meta,
    q_pad,
):
    rows = nat.shape[0]
    blocks = rows // TILE
    width = out_last.shape[0]
    scale = 1.0 / math.sqrt(HEAD_DIM)

    seq = tr[256:272, :].astype(F32)[0:1, :]
    mine = seq_own[...]
    begin = jnp.zeros_like(seq)
    begin_own = jnp.zeros_like(mine)
    finish_own = jnp.full_like(mine, float(rows))
    for number in range(1, SEQS):
        before = jnp.sum((seq < number).astype(F32), axis=1, keepdims=True)
        begin = jnp.where(seq >= number, before, begin)
        begin_own = jnp.where(mine >= number, before, begin_own)
        finish_own = jnp.where(mine == number - 1, before, finish_own)
    start[...] = begin.astype(jnp.int32)
    start_own[...] = begin_own.astype(jnp.int32)
    end_own[...] = finish_own.astype(jnp.int32)
    base = pl.multiple_of(own[0], 16)
    meta[2 * blocks] = jnp.min(begin_own).astype(jnp.int32) // TILE
    meta[2 * blocks + 1] = (base + width - 1) // TILE + 1
    meta[2 * blocks + 2] = base // width
    meta[2 * blocks + 3] = (jnp.max(finish_own).astype(jnp.int32) + width - 1) // width

    def scores_of(queries, kb):
        at = pl.multiple_of(kb * TILE, TILE)
        return contract(nat[pl.ds(at, TILE), 128:256], queries, 1, 1), at

    def weigh(shares, v_row, at):
        return contract(tr[v_row : v_row + HEAD_DIM, pl.ds(at, TILE)], shares.astype(BF), 1, 0)

    def step(queries, limits, v_row, kb, carry):
        top, total, acc = carry
        scores, at = scores_of(queries, kb)
        if limits is not None:
            scores = jnp.where(band(scores.shape, *limits, at), scores, NEG)
        now = jnp.maximum(top, jnp.max(scores, axis=0, keepdims=True))
        fade = jnp.exp(top - now)
        shares = jnp.exp(scores - now)
        total = total * fade + jnp.sum(shares, axis=0, keepdims=True)
        return now, total, acc * fade + weigh(shares, v_row, at)

    def one_block(qb, unused):
        at = pl.multiple_of(qb * TILE, TILE)
        queries = pick_half(nat[pl.ds(at, TILE), 0:128], False, scale)
        low = start[:, pl.ds(at, TILE)]
        near = low.astype(F32)
        first = jnp.min(near).astype(jnp.int32) // TILE
        full = jnp.minimum((jnp.max(near).astype(jnp.int32) + TILE - 1) // TILE, qb)
        meta[qb] = first
        meta[blocks + qb] = full
        limits = (low, at + lane_ids(TILE))
        scores, at_key = scores_of(queries, qb)
        scores = jnp.where(band(scores.shape, *limits, at_key), scores, NEG)
        top = jnp.max(scores, axis=0, keepdims=True)
        shares = jnp.exp(scores - top)
        carry = (top, jnp.sum(shares, axis=0, keepdims=True), weigh(shares, 128, at_key))
        carry = lax.fori_loop(first, full, functools.partial(step, queries, limits, 128), carry)
        carry = lax.fori_loop(full, qb, functools.partial(step, queries, None, 128), carry)
        top, total, acc = carry
        lse[:, pl.ds(at, TILE)] = top + jnp.log(total)
        out_nat[pl.ds(at, TILE), :] = (acc / total).T
        return unused

    lax.fori_loop(0, blocks, one_block, 0)

    q_pad[...] = jnp.zeros_like(q_pad)
    q_pad[0:width, :] = pick_half(nat[pl.ds(base, width), 0:128], True, scale)
    limits = (start_own[...], base + lane_ids(TILE))
    carry = (
        jnp.full((1, TILE), NEG, F32),
        jnp.zeros((1, TILE), F32),
        jnp.zeros((HEAD_DIM, TILE), F32),
    )
    top, total, acc = lax.fori_loop(
        meta[2 * blocks],
        meta[2 * blocks + 1],
        functools.partial(step, q_pad[...], limits, 192),
        carry,
    )
    lse_last[...] = top + jnp.log(total)
    out_last[...] = (acc / total).T[0:width, :]

    half = width // 2
    for dest in range(rows // width):
        first = out_nat[dest * width : dest * width + half, :]
        second = out_nat[dest * width + half : (dest + 1) * width, :]
        packed[dest] = jnp.concatenate([first, second], axis=1).astype(BF)


def backward_last_kernel(
    own, meta, start_own, end_own, nat, tr, came, lse_own, delta_own, last_qk, last_v,
    q_rows, o_rows, pad_q, pad_o,
):
    rows = nat.shape[0]
    blocks = rows // TILE
    width = last_qk.shape[0]
    scale = 1.0 / math.sqrt(HEAD_DIM)
    base = pl.multiple_of(own[0], 16)

    q_rows[0:rows, :] = (nat[:, 0:128].astype(F32) * scale).astype(BF)
    q_rows[rows:, :] = jnp.zeros((q_rows.shape[0] - rows, 2 * HEAD_DIM), BF)
    for source in range(rows // width):
        o_rows[source * width : (source + 1) * width, :] = came[source, 0:width, :]
    o_rows[rows:, :] = jnp.zeros((o_rows.shape[0] - rows, 2 * HEAD_DIM), BF)

    pad_q[...] = jnp.zeros_like(pad_q)
    pad_o[...] = jnp.zeros_like(pad_o)
    pad_q[0:width, :] = pick_half(nat[pl.ds(base, width), 0:128], True, scale)
    pad_o[0:width, :] = pick_half(o_rows[pl.ds(base, width), :], True)
    limits = (start_own[...], base + lane_ids(TILE))

    def query_step(kb, d_query):
        at = pl.multiple_of(kb * TILE, TILE)
        scores = contract(nat[pl.ds(at, TILE), 128:256], pad_q[...], 1, 1)
        scores = jnp.where(band(scores.shape, *limits, at), scores, NEG)
        shares = jnp.exp(scores - lse_own[...])
        d_shares = contract(nat[pl.ds(at, TILE), 256:384], pad_o[...], 1, 1)
        d_scores = (shares * (d_shares - delta_own[...])).astype(BF)
        return d_query + contract(tr[HEAD_DIM : 2 * HEAD_DIM, pl.ds(at, TILE)], d_scores, 1, 0)

    d_query = lax.fori_loop(
        meta[2 * blocks], meta[2 * blocks + 1], query_step, jnp.zeros((HEAD_DIM, TILE), F32)
    )
    last_qk[:, 0:HEAD_DIM] = (d_query.T[0:width, :] * scale).astype(BF)

    keys = pick_half(nat[pl.ds(base, width), 128:256], True)
    values = pick_half(nat[pl.ds(base, width), 256:384], True)
    key = base + lax.broadcasted_iota(jnp.int32, (width, TILE), 0)
    finish = jnp.broadcast_to(end_own[...].astype(F32), (128, TILE)).T[0:width, 0:1]
    finish = finish.astype(jnp.int32)
    lane = lane_ids(TILE)

    def key_step(source, carry):
        d_key, d_value = carry
        at = pl.multiple_of(source * width, 16)
        queries = q_rows[pl.ds(at, TILE), :]
        grads = o_rows[pl.ds(at, TILE), :]
        facts = came[source, width : width + 16, :].astype(F32)
        log_total = jnp.concatenate([facts[0:1] + facts[2:3], facts[1:2] + facts[3:4]], axis=1)
        delta = jnp.concatenate([facts[4:5] + facts[6:7], facts[5:6] + facts[7:8]], axis=1)
        query = at + lane
        keep = (key <= query) & (query < finish) & (lane < width)
        scores = jnp.where(keep, contract(keys, queries, 1, 1), NEG)
        shares = jnp.exp(scores - log_total)
        d_shares = contract(values, grads, 1, 1)
        d_scores = (shares * (d_shares - delta)).astype(BF)
        return (
            d_key + contract(d_scores, queries, 1, 0),
            d_value + contract(shares.astype(BF), grads, 1, 0),
        )

    zero = jnp.zeros((width, 2 * HEAD_DIM), F32)
    d_key, d_value = lax.fori_loop(
        meta[2 * blocks + 2], meta[2 * blocks + 3], key_step, (zero, zero)
    )
    last_qk[:, HEAD_DIM:] = d_key[:, HEAD_DIM:].astype(BF)
    last_v[...] = d_value[:, HEAD_DIM:].astype(BF)


def backward_kernel(
    meta, start, nat, tr, came, out_nat, lse, packed, d_qk, d_v, o_rows, q_rows, acc_k, acc_v
):
    rows = nat.shape[0]
    blocks = rows // TILE
    width = rows // packed.shape[0]
    scale = 1.0 / math.sqrt(HEAD_DIM)

    q_rows[...] = (nat[:, 0:128].astype(F32) * scale).astype(BF)
    for source in range(rows // width):
        o_rows[source * width : (source + 1) * width, :] = came[source, 0:width, :]
    acc_k[...] = jnp.zeros_like(acc_k)
    acc_v[...] = jnp.zeros_like(acc_v)

    def one_block(qb, unused):
        at_q = pl.multiple_of(qb * TILE, TILE)
        pair = q_rows[pl.ds(at_q, TILE), :]
        queries = pick_half(pair, False)
        grads = o_rows[pl.ds(at_q, TILE), :]
        product = grads[:, 0:HEAD_DIM].astype(F32) * out_nat[pl.ds(at_q, TILE), :]
        delta = jnp.sum(product.T, axis=0, keepdims=True)
        grads_low = pick_half(grads, False)
        log_total = lse[:, pl.ds(at_q, TILE)]
        limits = (start[:, pl.ds(at_q, TILE)], at_q + lane_ids(TILE))

        def step(masked, kb, d_query):
            at = pl.multiple_of(kb * TILE, TILE)
            scores = contract(nat[pl.ds(at, TILE), 128:256], queries, 1, 1)
            if masked:
                scores = jnp.where(band(scores.shape, *limits, at), scores, NEG)
            shares = jnp.exp(scores - log_total)
            d_shares = contract(nat[pl.ds(at, TILE), 256:384], grads_low, 1, 1)
            d_scores = (shares * (d_shares - delta)).astype(BF)
            acc_v[pl.ds(at, TILE), :] += contract(shares.astype(BF), grads, 1, 0)
            acc_k[pl.ds(at, TILE), :] += contract(d_scores, pair, 1, 0)
            return d_query + contract(tr[0:HEAD_DIM, pl.ds(at, TILE)], d_scores, 1, 0)

        d_query = step(True, qb, jnp.zeros((HEAD_DIM, TILE), F32))
        full = meta[blocks + qb]
        d_query = lax.fori_loop(meta[qb], full, functools.partial(step, True), d_query)
        d_query = lax.fori_loop(full, qb, functools.partial(step, False), d_query)
        d_qk[pl.ds(at_q, TILE), 0:HEAD_DIM] = (d_query.T * scale).astype(BF)
        return unused

    lax.fori_loop(0, blocks, one_block, 0)
    d_qk[:, HEAD_DIM:] = acc_k[:, 0:HEAD_DIM].astype(BF)
    d_v[...] = acc_v[:, 0:HEAD_DIM].astype(BF)
    half = width // 2
    for dest in range(rows // width):
        low_rows = slice(dest * width, dest * width + half)
        high_rows = slice(dest * width + half, (dest + 1) * width)
        packed[dest, 0:width, :] = d_qk[dest * width : (dest + 1) * width, :]
        packed[dest, width:, :] = jnp.concatenate([d_v[low_rows, :], d_v[high_rows, :]], axis=1)


def kernel_call(kernel, scalars, operands, outs, scratch, work, smem_out=None):
    vmem = pl.BlockSpec(memory_space=pltpu.VMEM)
    smem = pl.BlockSpec(memory_space=pltpu.SMEM)
    out_shape = [jax.ShapeDtypeStruct(shape, kind) for shape, kind in outs]
    out_specs = [vmem] * len(outs)
    if smem_out is not None:
        out_shape.append(jax.ShapeDtypeStruct((smem_out,), jnp.int32))
        out_specs.append(smem)
    return pl.pallas_call(
        kernel,
        out_shape=tuple(out_shape),
        in_specs=[smem] * len(scalars) + [vmem] * len(operands),
        out_specs=tuple(out_specs),
        scratch_shapes=[pltpu.VMEM(shape, kind) for shape, kind in scratch],
        cost_estimate=pl.CostEstimate(flops=work, bytes_accessed=8 << 20, transcendentals=0),
    )(*scalars, *operands)


def attend_forward(own, seq_own, nat, tr, width):
    rows = nat.shape[0]
    pair = 2 * HEAD_DIM
    return kernel_call(
        forward_kernel,
        (own,),
        (seq_own, nat, tr),
        [
            ((rows // width, width // 2, pair), BF),
            ((rows, HEAD_DIM), F32),
            ((1, rows), F32),
            ((width, HEAD_DIM), F32),
            ((1, TILE), F32),
            ((1, rows), jnp.int32),
            ((1, TILE), jnp.int32),
            ((1, TILE), jnp.int32),
        ],
        [((TILE, pair), BF)],
        16 * rows * rows * HEAD_DIM,
        2 * (rows // TILE) + 4,
    )


def attend_backward_last(own, meta, start_own, end_own, nat, tr, came, lse_own, delta_own, width):
    rows = nat.shape[0]
    pair = 2 * HEAD_DIM
    return kernel_call(
        backward_last_kernel,
        (own, meta),
        (start_own, end_own, nat, tr, came, lse_own, delta_own),
        [((width, pair), BF), ((width, HEAD_DIM), BF)],
        [((rows + TILE - width, pair), BF)] * 2 + [((TILE, pair), BF)] * 2,
        4 * rows * rows * HEAD_DIM,
    )


def attend_backward(meta, start, nat, tr, came, out_nat, lse, width):
    rows = nat.shape[0]
    pair = 2 * HEAD_DIM
    return kernel_call(
        backward_kernel,
        (meta,),
        (start, nat, tr, came, out_nat, lse),
        [
            ((rows // width, width + width // 2, pair), BF),
            ((rows, pair), BF),
            ((rows, HEAD_DIM), BF),
        ],
        [((rows, pair), BF)] * 2 + [((rows, pair), F32)] * 2,
        40 * rows * rows * HEAD_DIM,
    )


def join_kernel(pieces, shared, weights, sums, joined, dots, dots_bias):
    heads = pieces.shape[0]
    running = [jnp.zeros((joined.shape[0], 2 * HEAD_DIM), F32)] * 2
    rest = [0.0, 0.0]
    units = 3 * (heads + 1)

    def unit(index):
        part, head = divmod(index, heads + 1)
        columns = slice(part * HEAD_DIM, (part + 1) * HEAD_DIM)
        return shared[:, columns] if head == heads else pieces[head, :, columns]

    for block in range((units + 1) // 2):
        paired = 2 * block + 1 < units
        if paired:
            values = jnp.concatenate([unit(2 * block), unit(2 * block + 1)], axis=1)
        else:
            values = unit(2 * block)
        at = slice(2 * block * HEAD_DIM, 2 * block * HEAD_DIM + values.shape[1])
        values = values.astype(F32)
        joined[:, at] = values
        weight = weights[:, at].astype(F32)
        products = [values * weight, weight * sums[:, at]]
        if paired:
            running = [so_far + product for so_far, product in zip(running, products)]
        else:
            rest = [jnp.sum(product, axis=1, keepdims=True) for product in products]
    dots[...] = jnp.sum(running[0], axis=1, keepdims=True) + rest[0]
    dots_bias[...] = jnp.sum(running[1], axis=1, keepdims=True) + rest[1]


def join_heads(pieces, shared, weights, sums):
    heads, _, columns = pieces.shape
    rows = weights.shape[0]
    step = 272 if rows % 272 == 0 else rows
    return pl.pallas_call(
        join_kernel,
        grid=(rows // step,),
        out_shape=(
            jax.ShapeDtypeStruct(weights.shape, F32),
            jax.ShapeDtypeStruct((rows, 1), F32),
            jax.ShapeDtypeStruct((rows, 1), F32),
        ),
        in_specs=[
            pl.BlockSpec((heads, step, columns), lambda i: (0, i, 0)),
            pl.BlockSpec((step, shared.shape[1]), lambda i: (i, 0)),
            pl.BlockSpec((step, weights.shape[1]), lambda i: (i, 0)),
            pl.BlockSpec((1, weights.shape[1]), lambda i: (0, 0)),
        ],
        out_specs=(
            pl.BlockSpec((step, weights.shape[1]), lambda i: (i, 0)),
            pl.BlockSpec((step, 1), lambda i: (i, 0)),
            pl.BlockSpec((step, 1), lambda i: (i, 0)),
        ),
        cost_estimate=pl.CostEstimate(flops=1 << 20, bytes_accessed=14 << 20, transcendentals=0),
        name="join_heads",
    )(pieces, shared, weights, sums)


def split_two(values):
    high = values.astype(BF)
    low = (values - high.astype(F32)).astype(BF)
    return [high, low]


def round_up(value, step):
    return (value + step - 1) // step * step


def to_tensor(part, ways):
    spread = jnp.broadcast_to(part[None], (ways,) + part.shape)
    got = lax.all_to_all(spread, "tensor", 0, 0, tiled=True)
    return got.reshape(ways * part.shape[0], part.shape[1])


def sum_tensor(partial, ways):
    rows = partial.shape[0] // ways
    got = lax.all_to_all(
        partial.astype(BF).reshape(ways, rows, partial.shape[1]), "tensor", 0, 0, tiled=True
    )
    return jnp.sum(got.astype(F32), axis=0)


def head_columns(matrix, head, width):
    return [
        lax.dynamic_slice_in_dim(matrix, part * width + head * HEAD_DIM, HEAD_DIM, 1)
        for part in range(3)
    ]


def gelu_pair(pre):
    factor = math.sqrt(2.0 / math.pi)
    square = pre * pre
    bend = jnp.tanh(factor * (pre + 0.044715 * pre * square))
    value = 0.5 * pre * (1.0 + bend)
    slope = 0.5 * (1.0 + bend) + 0.5 * pre * (1.0 - bend * bend) * factor * (
        1.0 + 3.0 * 0.044715 * square
    )
    return value, slope


def shards(
    tokens, segments, w_qkv, w_out, ln1_gain, ln1_bias, ln2_gain, ln2_bias, w_up, w_down, out_grad
):
    rows, width = tokens.shape
    count = lax.axis_size("shard")
    ways_c = lax.axis_size("context")
    ways_t = lax.axis_size("tensor")
    ways = ways_c * ways_t
    part_rows = w_qkv.shape[0]
    device = lax.axis_index(GROUP)
    shared = HEADS - 1
    padded = round_up(width, 128)
    columns = 3 * HEAD_DIM

    vectors = gather_small(
        jnp.stack([ln1_gain, ln1_bias, ln2_gain, ln2_bias]), count, 1
    ).astype(F32)
    gain_one, bias_one, gain_two, bias_two = [vectors[i : i + 1] for i in range(4)]

    inputs = tokens.astype(F32)
    unit_one, inverse_one = norm_stats(inputs)
    low_one = (unit_one * gain_one + bias_one).astype(BF)
    seq_row = segments[0]
    wide_one = jnp.concatenate(
        [low_one, seq_row[:, None].astype(BF), jnp.zeros((rows, padded - width - 1), BF)], axis=1
    )
    rows_one = lax.all_gather(wide_one, GROUP, axis=0, tiled=True)

    mine = head_columns(w_qkv, device, width)
    last = [
        w_qkv[:, part * width + shared * HEAD_DIM : part * width + (shared + 1) * HEAD_DIM]
        for part in range(3)
    ]
    head_w = gather_small(
        jnp.concatenate([mine[0], last[0], mine[1], last[1], mine[2], last[2]], axis=1),
        count,
        0,
    )
    head_w = jnp.pad(head_w, ((0, padded - width), (0, 0)))
    mark = (jnp.arange(padded)[:, None] == width) & (jnp.arange(16)[None] == 0)
    turn_w = jnp.concatenate([head_w[:, 2 * HEAD_DIM :], mark.astype(BF)], axis=1)
    out_full = gather_large(w_out, count, 0)
    up_full = gather_large(w_up, count, 0)
    down_turned = gather_large(w_down.T, count, 0)
    up_turned = after(up_full.T, up_full)
    down_full = after(down_turned.T, down_turned)
    qkv_full = gather_large(w_qkv, count, 0)
    grads_all = lax.all_gather(out_grad, "tensor", axis=0, tiled=True)
    split = ways * HEAD_DIM
    out_wide = jnp.concatenate(
        [
            out_full[:split].reshape(ways, HEAD_DIM, width),
            jnp.broadcast_to(out_full[None, split:], (ways, HEAD_DIM, width)),
        ],
        axis=1,
    ).reshape(2 * split, width)

    own = (device * rows).reshape(1).astype(jnp.int32)
    seq_own = jnp.concatenate(
        [seq_row, jnp.broadcast_to(seq_row[-1:], (TILE - rows,))]
    ).astype(F32)[None]
    nat = jnp.dot(rows_one, head_w, preferred_element_type=F32).astype(BF)
    tr = contract(turn_w, rows_one, 0, 1).astype(BF)
    packed, out_nat, lse, last_out, last_lse, start, start_own, end_own, meta = attend_forward(
        own, seq_own, nat, tr, rows
    )
    got = lax.all_to_all(packed, GROUP, 0, 0, tiled=True)
    half = rows // 2
    got = got.reshape(ways, half, 2, HEAD_DIM).transpose(2, 1, 0, 3).reshape(rows, split)
    attended = jnp.concatenate([got, last_out.astype(BF)], axis=1)

    resid = inputs + jnp.dot(attended, out_full, preferred_element_type=F32)
    unit_two, inverse_two = norm_stats(resid)
    low_two = (unit_two * gain_two + bias_two).astype(BF)

    d_hidden = jnp.dot(grads_all, down_turned, preferred_element_type=F32)
    rows_two = to_tensor(low_two, ways_t)
    rows_two, d_hidden = lax.optimization_barrier((rows_two, d_hidden))
    hidden, slope = gelu_pair(jnp.dot(rows_two, up_full, preferred_element_type=F32))
    hidden = hidden.astype(BF)
    d_pre = (d_hidden * slope).astype(BF)
    d_normed_two = sum_tensor(jnp.dot(d_pre, up_turned, preferred_element_type=F32), ways_t)

    grad_up = contract(rows_two, d_pre, 0, 0).astype(BF)
    grad_down = contract(grads_all, hidden, 0, 0).astype(BF)
    mixed = jnp.dot(hidden, down_full, preferred_element_type=F32).astype(BF)

    grad_in = out_grad.astype(F32)
    d_resid = grad_in + norm_back(d_normed_two, unit_two, inverse_two, gain_two)
    d_branch = d_resid.astype(BF)

    d_wide = contract(d_branch, out_wide, 1, 1).astype(BF)
    last_grad = d_wide[:, HEAD_DIM : 2 * HEAD_DIM]
    last_delta = jnp.sum(last_grad.astype(F32) * last_out, axis=1)
    pieces = split_two(last_lse[0, :rows]) + split_two(last_delta)
    extra = jnp.pad(jnp.stack(pieces), ((0, 0), (0, TILE - rows))).reshape(8, 128)
    extra = jnp.pad(extra, ((0, 8), (0, 0)))
    payload = jnp.concatenate(
        [
            d_wide.reshape(rows, ways, 2 * HEAD_DIM).transpose(1, 0, 2),
            jnp.broadcast_to(extra[None], (ways,) + extra.shape),
        ],
        axis=1,
    )
    came = lax.all_to_all(payload, GROUP, 0, 0, tiled=True)
    mixed = rotate(mixed.reshape(ways_t, rows, width), ways_t, came)
    came_heads = came
    delta_own = jnp.pad(last_delta, (0, TILE - rows))[None]

    late_branch = after(d_branch, payload)

    grad_out_w = jnp.concatenate(
        [
            contract(attended, late_branch, 0, 0).astype(BF),
            jnp.sum(d_normed_two * unit_two, axis=0)[:, None].astype(BF),
            jnp.sum(d_normed_two, axis=0)[:, None].astype(BF),
            jnp.zeros((width, padded - width - 2), BF),
        ],
        axis=1,
    )
    last_qk, last_v = attend_backward_last(
        own, meta, start_own, end_own, nat, tr, came, last_lse, delta_own, rows
    )
    last_all = jnp.concatenate([last_qk, last_v], axis=1)
    chunk = padded // ways
    grad_last = contract(wide_one, last_all, 0, 0).astype(BF)
    grad_last = lax.all_to_all(
        grad_last.reshape(ways, chunk, columns), GROUP, 0, 0, tiled=True
    )

    packed, d_qk, d_v = attend_backward(meta, start, nat, tr, came, out_nat, lse, rows)
    came = lax.all_to_all(packed, GROUP, 0, 0, tiled=True)
    grad_last = jnp.sum(grad_last.astype(F32), axis=0)

    pair = reduce_rows(
        jnp.concatenate([grad_up, grad_down], axis=1), count, ways_c, (grad_up, payload, came_heads)
    )
    grad_out_w = reduce_rows(grad_out_w, count, ways_c, (grad_out_w, came_heads, last_qk))
    piece = part_rows // ways_c
    deep = round_up(-(-piece // ways_t), 8)
    grad_out_w = jnp.pad(grad_out_w, ((0, deep * ways_t - piece), (0, 0)))
    grad_out_w = rotate(grad_out_w.reshape(ways_t, deep, padded), ways_t, last_qk)
    sent = send_rows(pair, ways_c)
    grad_out_w = total(grad_out_w).astype(BF)
    grad_out_w = lax.all_gather(grad_out_w, GROUP, axis=0, tiled=True)

    d_head = jnp.concatenate([d_qk, d_v], axis=1)
    grad_mine = contract(rows_one, d_head, 0, 0)[:width]
    sums = jnp.sum(d_head.astype(F32), axis=0).reshape(columns // 2, 2)
    sums_last = jnp.sum(last_all.astype(F32), axis=0).reshape(columns // 2, 2)
    sums = jnp.pad(
        jnp.concatenate([sums, sums_last], axis=1), ((0, part_rows - columns // 2), (0, 0))
    )
    wide = 256
    sums = jnp.pad(sums, ((0, 0), (0, wide - columns - 4)))
    both = jnp.concatenate(
        [
            grad_mine.reshape(count, part_rows, columns),
            jnp.broadcast_to(sums[None], (count,) + sums.shape),
        ],
        axis=2,
    )
    both = jnp.concatenate(
        [
            both,
            jnp.broadcast_to(
                jnp.pad(grad_last, ((0, 0), (0, wide - columns)))[None], (count, chunk, wide)
            ),
        ],
        axis=1,
    )
    both = sum_shard_rows(both.reshape(count * (part_rows + chunk), wide), count)
    payload = both.astype(BF)
    pieces = lax.all_gather(payload, GROUP, axis=0, tiled=True)
    pieces = pieces.reshape((ways,) + payload.shape)
    shared_w = pieces[:, part_rows : part_rows + chunk, :columns].reshape(ways * chunk, columns)
    facts = pieces[:, : columns // 2, columns : columns + 4].astype(F32)
    sums = facts[:, :, :2].reshape(ways, 3, HEAD_DIM)
    sums_last = jnp.sum(facts[:, :, 2:], axis=0).reshape(1, 3, HEAD_DIM)
    sums = jnp.concatenate([sums, sums_last], axis=0).transpose(1, 0, 2).reshape(1, 3 * width)
    shared_w = lax.dynamic_slice_in_dim(
        shared_w, lax.axis_index("shard") * part_rows, part_rows, 0
    )
    grad_qkv, dots, dots_bias = join_heads(pieces, shared_w, w_qkv, sums)
    grad_bias_one = dots_bias[:, 0]
    grad_gain_one = (dots[:, 0] - ln1_bias.astype(F32) * grad_bias_one) / ln1_gain.astype(F32)
    grad_out_w = grad_out_w.reshape(ways_c, deep * ways_t, padded)[:, :piece]
    grad_out_w = grad_out_w.reshape(part_rows, padded).astype(F32)

    result = (resid + total([mixed[0]] + [after(share, payload) for share in mixed[1:]])).astype(BF)
    sent = None if sent is None else after(sent, payload)
    pair = gather_rows(pair, sent, ways_c).astype(F32)
    grad_up = pair[:, : up_full.shape[1]]
    grad_down = pair[:, up_full.shape[1] :].T

    came_qk = came[:, :rows].reshape(ways, rows, 2, HEAD_DIM).transpose(1, 2, 0, 3)
    came_qk = came_qk.reshape(rows, 2, split)
    came_v = came[:, rows:].reshape(ways, half, 2, HEAD_DIM).transpose(2, 1, 0, 3)
    came_v = came_v.reshape(rows, 1, split)
    came = jnp.concatenate([came_qk, came_v], axis=1)
    d_projected = jnp.concatenate(
        [came, last_all.reshape(rows, 3, HEAD_DIM)], axis=2
    ).reshape(rows, 3 * width)
    d_normed_one = contract(d_projected, qkv_full, 1, 1)
    input_grad = (d_resid + norm_back(d_normed_one, unit_one, inverse_one, gain_one)).astype(BF)
    return (
        result,
        input_grad,
        grad_qkv,
        grad_out_w[:, :width],
        grad_gain_one,
        grad_bias_one,
        grad_out_w[:, width],
        grad_out_w[:, width + 1],
        grad_up,
        grad_down,
    )


def solution(mesh):
    in_specs = (
        P(("shard", "context", "tensor"), None),
        P("shard", ("context", "tensor")),
        P("shard", None),
        P("shard", None),
        P("shard"),
        P("shard"),
        P("shard"),
        P("shard"),
        P("shard", "tensor"),
        P("tensor", "shard"),
        P(("shard", "context", "tensor"), None),
    )
    out_specs = (
        P(("shard", "context", "tensor"), None),
        P(("shard", "context", "tensor"), None),
        P("shard", None),
        P("shard", None),
        P("shard"),
        P("shard"),
        P("shard"),
        P("shard"),
        P("shard", "tensor"),
        P("tensor", "shard"),
    )
    return jax.shard_map(shards, mesh=mesh, in_specs=in_specs, out_specs=out_specs, check_vma=False)
```

```python
import functools
import math

import jax
import jax.numpy as jnp
from jax import lax
from jax.experimental import pallas as pl
from jax.experimental.pallas import tpu as pltpu
from jax.sharding import PartitionSpec as P


HEADS = 17
HEAD_DIM = 64
SEQS = 6
EPSILON = 1e-05
NEG = -1e30
GROUP = ("context", "tensor")
TILE = 256
BF = jnp.bfloat16
F32 = jnp.float32


def contract(left, right, left_dim, right_dim):
    return lax.dot_general(
        left, right, (((left_dim,), (right_dim,)), ((), ())), preferred_element_type=F32
    )


def norm_stats(values):
    average = jnp.mean(values, axis=-1, keepdims=True)
    centred = values - average
    variance = jnp.mean(centred * centred, axis=-1, keepdims=True)
    inverse = lax.rsqrt(variance + EPSILON)
    return centred * inverse, inverse


def norm_back(grad, unit, inverse, gain):
    scaled = grad * gain
    first = jnp.mean(scaled, axis=-1, keepdims=True)
    second = jnp.mean(scaled * unit, axis=-1, keepdims=True)
    return inverse * (scaled - first - unit * second)


def swap_shard(part):
    return lax.ppermute(part, "shard", [(0, 1), (1, 0)])


def in_order(mine, other, axis):
    index = lax.axis_index("shard")
    return jnp.where(
        index == 0,
        jnp.concatenate([mine, other], axis=axis),
        jnp.concatenate([other, mine], axis=axis),
    )


def gather_small(part, count, axis):
    if count != 2:
        return lax.all_gather(part, "shard", axis=axis, tiled=True)
    return in_order(part, swap_shard(part), axis)


def gather_large(part, count, axis):
    if count != 2:
        return lax.all_gather(part, "shard", axis=axis, tiled=True)
    ways = lax.axis_size("context")
    core = lax.rem(lax.axis_index("context"), 2)
    half = part.shape[axis] // 2
    mine = lax.dynamic_slice_in_dim(part, core * half, half, axis)
    fetched = swap_shard(mine)
    partner = lax.ppermute(fetched, "context", [(i, i ^ 1) for i in range(ways)])
    other = jnp.where(
        core == 0,
        jnp.concatenate([fetched, partner], axis=axis),
        jnp.concatenate([partner, fetched], axis=axis),
    )
    return in_order(part, other, axis)


def swap_half(blocks, bit, axis, axis_name, pairs):
    kept = lax.dynamic_index_in_dim(blocks, bit, axis, keepdims=False)
    away = lax.dynamic_index_in_dim(blocks, 1 - bit, axis, keepdims=False).astype(BF)
    came = lax.ppermute(away, axis_name, pairs)
    return kept, came


def add(kept, came):
    return kept.astype(F32) + came.astype(F32)


def sum_shard_rows(partial, count):
    if count != 2:
        return lax.psum_scatter(
            partial.astype(BF), "shard", scatter_dimension=0, tiled=True
        ).astype(F32)
    index = lax.axis_index("shard")
    blocks = partial.reshape((2, -1) + partial.shape[1:])
    return add(*swap_half(blocks, index, 0, "shard", [(0, 1), (1, 0)]))


def reduce_rows(partial, count, ways_c, gates):
    if count != 2 or ways_c != 4:
        return lax.psum_scatter(partial, ("shard", "context"), scatter_dimension=0, tiled=True)
    context = lax.axis_index("context")
    core, chip = lax.rem(context, 2), lax.div(context, 2)
    rows, columns = partial.shape
    blocks = partial.reshape(2, 2, 2, rows // 8, columns)
    kept, came = swap_half(blocks, core, 2, "context", [(i, i ^ 1) for i in range(4)])
    blocks = add(kept, after(came, gates[0])).astype(BF)
    kept, came = swap_half(blocks, chip, 1, "context", [(i, i ^ 2) for i in range(4)])
    blocks = add(kept, after(came, gates[1])).astype(BF)
    kept, came = swap_half(blocks, lax.axis_index("shard"), 0, "shard", [(0, 1), (1, 0)])
    return add(kept, after(came, gates[2])).astype(BF)


def send_rows(part, ways_c):
    if ways_c != 4:
        return None
    return lax.ppermute(part, "context", [(i, i ^ 2) for i in range(4)])


def gather_rows(part, sent, ways_c):
    if ways_c != 4:
        return lax.all_gather(part, "context", axis=0, tiled=True)
    context = lax.axis_index("context")
    core, chip = lax.rem(context, 2), lax.div(context, 2)
    both = jnp.where(chip == 0, jnp.stack([part, sent]), jnp.stack([sent, part]))
    came = lax.ppermute(both, "context", [(i, i ^ 1) for i in range(4)])
    all_rows = jnp.where(
        core == 0, jnp.stack([both, came], axis=1), jnp.stack([came, both], axis=1)
    )
    return all_rows.reshape((4 * part.shape[0],) + part.shape[1:])


def rotate(blocks, ways, gate):
    index = lax.axis_index("tensor")
    shares = [lax.dynamic_index_in_dim(blocks, index, 0, keepdims=False)]
    for turn in range(1, ways):
        target = lax.rem(index + turn, ways)
        away = lax.dynamic_index_in_dim(blocks, target, 0, keepdims=False)
        away = after(away, gate)
        shares.append(lax.ppermute(away, "tensor", [(i, (i + turn) % ways) for i in range(ways)]))
    return shares


def gather_tensor(part, ways):
    index = lax.axis_index("tensor")
    parts = [part] + [
        lax.ppermute(part, "tensor", [(i, (i + turn) % ways) for i in range(ways)])
        for turn in range(1, ways)
    ]
    parts = jnp.stack(parts)
    return jnp.concatenate(
        [
            lax.dynamic_index_in_dim(parts, lax.rem(index + ways - i, ways), 0, keepdims=False)
            for i in range(ways)
        ]
    )


def total(shares):
    return sum(share.astype(F32) for share in shares)


def after(value, *others):
    return lax.optimization_barrier((value,) + others)[0]


def pick_half(pair, high, scale=1.0):
    first = lax.broadcasted_iota(jnp.int32, pair.shape, 1) < HEAD_DIM
    values = pair.astype(F32) * scale
    return (jnp.where(first, 0.0, values) if high else jnp.where(first, values, 0.0)).astype(BF)


def lane_ids(count):
    return lax.broadcasted_iota(jnp.int32, (1, count), 1)


def band(shape, low, high, first_key):
    key = first_key + lax.broadcasted_iota(jnp.int32, shape, 0)
    return (key >= low) & (key <= high)


def forward_kernel(
    own, seq_own, nat, tr, packed, out_nat, lse, out_last, lse_last, start, start_own, end_own, meta,
    q_pad,
):
    rows = nat.shape[0]
    blocks = rows // TILE
    width = out_last.shape[0]
    scale = 1.0 / math.sqrt(HEAD_DIM)

    seq = tr[256:272, :].astype(F32)[0:1, :]
    mine = seq_own[...]
    begin = jnp.zeros_like(seq)
    begin_own = jnp.zeros_like(mine)
    finish_own = jnp.full_like(mine, float(rows))
    for number in range(1, SEQS):
        before = jnp.sum((seq < number).astype(F32), axis=1, keepdims=True)
        begin = jnp.where(seq >= number, before, begin)
        begin_own = jnp.where(mine >= number, before, begin_own)
        finish_own = jnp.where(mine == number - 1, before, finish_own)
    start[...] = begin.astype(jnp.int32)
    start_own[...] = begin_own.astype(jnp.int32)
    end_own[...] = finish_own.astype(jnp.int32)
    base = pl.multiple_of(own[0], 16)
    meta[2 * blocks] = jnp.min(begin_own).astype(jnp.int32) // TILE
    meta[2 * blocks + 1] = (base + width - 1) // TILE + 1
    meta[2 * blocks + 2] = base // width
    meta[2 * blocks + 3] = (jnp.max(finish_own).astype(jnp.int32) + width - 1) // width

    def scores_of(queries, kb):
        at = pl.multiple_of(kb * TILE, TILE)
        return contract(nat[pl.ds(at, TILE), 128:256], queries, 1, 1), at

    def weigh(shares, v_row, at):
        return contract(tr[v_row : v_row + HEAD_DIM, pl.ds(at, TILE)], shares.astype(BF), 1, 0)

    def step(queries, limits, v_row, kb, carry):
        top, total, acc = carry
        scores, at = scores_of(queries, kb)
        if limits is not None:
            scores = jnp.where(band(scores.shape, *limits, at), scores, NEG)
        now = jnp.maximum(top, jnp.max(scores, axis=0, keepdims=True))
        fade = jnp.exp(top - now)
        shares = jnp.exp(scores - now)
        total = total * fade + jnp.sum(shares, axis=0, keepdims=True)
        return now, total, acc * fade + weigh(shares, v_row, at)

    def one_block(qb, unused):
        at = pl.multiple_of(qb * TILE, TILE)
        queries = pick_half(nat[pl.ds(at, TILE), 0:128], False, scale)
        low = start[:, pl.ds(at, TILE)]
        near = low.astype(F32)
        first = jnp.min(near).astype(jnp.int32) // TILE
        full = jnp.minimum((jnp.max(near).astype(jnp.int32) + TILE - 1) // TILE, qb)
        meta[qb] = first
        meta[blocks + qb] = full
        limits = (low, at + lane_ids(TILE))
        scores, at_key = scores_of(queries, qb)
        scores = jnp.where(band(scores.shape, *limits, at_key), scores, NEG)
        top = jnp.max(scores, axis=0, keepdims=True)
        shares = jnp.exp(scores - top)
        carry = (top, jnp.sum(shares, axis=0, keepdims=True), weigh(shares, 128, at_key))
        carry = lax.fori_loop(first, full, functools.partial(step, queries, limits, 128), carry)
        carry = lax.fori_loop(full, qb, functools.partial(step, queries, None, 128), carry)
        top, total, acc = carry
        lse[:, pl.ds(at, TILE)] = top + jnp.log(total)
        out_nat[pl.ds(at, TILE), :] = (acc / total).T
        return unused

    lax.fori_loop(0, blocks, one_block, 0)

    q_pad[...] = jnp.zeros_like(q_pad)
    q_pad[0:width, :] = pick_half(nat[pl.ds(base, width), 0:128], True, scale)
    limits = (start_own[...], base + lane_ids(TILE))
    carry = (
        jnp.full((1, TILE), NEG, F32),
        jnp.zeros((1, TILE), F32),
        jnp.zeros((HEAD_DIM, TILE), F32),
    )
    top, total, acc = lax.fori_loop(
        meta[2 * blocks],
        meta[2 * blocks + 1],
        functools.partial(step, q_pad[...], limits, 192),
        carry,
    )
    lse_last[...] = top + jnp.log(total)
    out_last[...] = (acc / total).T[0:width, :]

    half = width // 2
    for dest in range(rows // width):
        first = out_nat[dest * width : dest * width + half, :]
        second = out_nat[dest * width + half : (dest + 1) * width, :]
        packed[dest] = jnp.concatenate([first, second], axis=1).astype(BF)


def backward_last_kernel(
    own, meta, start_own, end_own, nat, tr, came, lse_own, delta_own, last_qk, last_v,
    q_rows, o_rows, pad_q, pad_o,
):
    rows = nat.shape[0]
    blocks = rows // TILE
    width = last_qk.shape[0]
    scale = 1.0 / math.sqrt(HEAD_DIM)
    base = pl.multiple_of(own[0], 16)

    q_rows[0:rows, :] = (nat[:, 0:128].astype(F32) * scale).astype(BF)
    q_rows[rows:, :] = jnp.zeros((q_rows.shape[0] - rows, 2 * HEAD_DIM), BF)
    for source in range(rows // width):
        o_rows[source * width : (source + 1) * width, :] = came[source, 0:width, :]
    o_rows[rows:, :] = jnp.zeros((o_rows.shape[0] - rows, 2 * HEAD_DIM), BF)

    pad_q[...] = jnp.zeros_like(pad_q)
    pad_o[...] = jnp.zeros_like(pad_o)
    pad_q[0:width, :] = pick_half(nat[pl.ds(base, width), 0:128], True, scale)
    pad_o[0:width, :] = pick_half(o_rows[pl.ds(base, width), :], True)
    limits = (start_own[...], base + lane_ids(TILE))

    def query_step(kb, d_query):
        at = pl.multiple_of(kb * TILE, TILE)
        scores = contract(nat[pl.ds(at, TILE), 128:256], pad_q[...], 1, 1)
        scores = jnp.where(band(scores.shape, *limits, at), scores, NEG)
        shares = jnp.exp(scores - lse_own[...])
        d_shares = contract(nat[pl.ds(at, TILE), 256:384], pad_o[...], 1, 1)
        d_scores = (shares * (d_shares - delta_own[...])).astype(BF)
        return d_query + contract(tr[HEAD_DIM : 2 * HEAD_DIM, pl.ds(at, TILE)], d_scores, 1, 0)

    d_query = lax.fori_loop(
        meta[2 * blocks], meta[2 * blocks + 1], query_step, jnp.zeros((HEAD_DIM, TILE), F32)
    )
    last_qk[:, 0:HEAD_DIM] = (d_query.T[0:width, :] * scale).astype(BF)

    keys = pick_half(nat[pl.ds(base, width), 128:256], True)
    values = pick_half(nat[pl.ds(base, width), 256:384], True)
    key = base + lax.broadcasted_iota(jnp.int32, (width, TILE), 0)
    finish = jnp.broadcast_to(end_own[...].astype(F32), (128, TILE)).T[0:width, 0:1]
    finish = finish.astype(jnp.int32)
    lane = lane_ids(TILE)

    def key_step(source, carry):
        d_key, d_value = carry
        at = pl.multiple_of(source * width, 16)
        queries = q_rows[pl.ds(at, TILE), :]
        grads = o_rows[pl.ds(at, TILE), :]
        facts = came[source, width : width + 16, :].astype(F32)
        log_total = jnp.concatenate([facts[0:1] + facts[2:3], facts[1:2] + facts[3:4]], axis=1)
        delta = jnp.concatenate([facts[4:5] + facts[6:7], facts[5:6] + facts[7:8]], axis=1)
        query = at + lane
        keep = (key <= query) & (query < finish) & (lane < width)
        scores = jnp.where(keep, contract(keys, queries, 1, 1), NEG)
        shares = jnp.exp(scores - log_total)
        d_shares = contract(values, grads, 1, 1)
        d_scores = (shares * (d_shares - delta)).astype(BF)
        return (
            d_key + contract(d_scores, queries, 1, 0),
            d_value + contract(shares.astype(BF), grads, 1, 0),
        )

    zero = jnp.zeros((width, 2 * HEAD_DIM), F32)
    d_key, d_value = lax.fori_loop(
        meta[2 * blocks + 2], meta[2 * blocks + 3], key_step, (zero, zero)
    )
    last_qk[:, HEAD_DIM:] = d_key[:, HEAD_DIM:].astype(BF)
    last_v[...] = d_value[:, HEAD_DIM:].astype(BF)


def backward_kernel(
    meta, start, nat, tr, came, out_nat, lse, packed, d_qk, d_v, o_rows, q_rows, acc_k, acc_v
):
    rows = nat.shape[0]
    blocks = rows // TILE
    width = rows // packed.shape[0]
    scale = 1.0 / math.sqrt(HEAD_DIM)

    q_rows[...] = (nat[:, 0:128].astype(F32) * scale).astype(BF)
    for source in range(rows // width):
        o_rows[source * width : (source + 1) * width, :] = came[source, 0:width, :]
    acc_k[...] = jnp.zeros_like(acc_k)
    acc_v[...] = jnp.zeros_like(acc_v)

    def one_block(qb, unused):
        at_q = pl.multiple_of(qb * TILE, TILE)
        pair = q_rows[pl.ds(at_q, TILE), :]
        queries = pick_half(pair, False)
        grads = o_rows[pl.ds(at_q, TILE), :]
        product = grads[:, 0:HEAD_DIM].astype(F32) * out_nat[pl.ds(at_q, TILE), :]
        delta = jnp.sum(product.T, axis=0, keepdims=True)
        grads_low = pick_half(grads, False)
        log_total = lse[:, pl.ds(at_q, TILE)]
        limits = (start[:, pl.ds(at_q, TILE)], at_q + lane_ids(TILE))

        def step(masked, kb, d_query):
            at = pl.multiple_of(kb * TILE, TILE)
            scores = contract(nat[pl.ds(at, TILE), 128:256], queries, 1, 1)
            if masked:
                scores = jnp.where(band(scores.shape, *limits, at), scores, NEG)
            shares = jnp.exp(scores - log_total)
            d_shares = contract(nat[pl.ds(at, TILE), 256:384], grads_low, 1, 1)
            d_scores = (shares * (d_shares - delta)).astype(BF)
            acc_v[pl.ds(at, TILE), :] += contract(shares.astype(BF), grads, 1, 0)
            acc_k[pl.ds(at, TILE), :] += contract(d_scores, pair, 1, 0)
            return d_query + contract(tr[0:HEAD_DIM, pl.ds(at, TILE)], d_scores, 1, 0)

        d_query = step(True, qb, jnp.zeros((HEAD_DIM, TILE), F32))
        full = meta[blocks + qb]
        d_query = lax.fori_loop(meta[qb], full, functools.partial(step, True), d_query)
        d_query = lax.fori_loop(full, qb, functools.partial(step, False), d_query)
        d_qk[pl.ds(at_q, TILE), 0:HEAD_DIM] = (d_query.T * scale).astype(BF)
        return unused

    lax.fori_loop(0, blocks, one_block, 0)
    d_qk[:, HEAD_DIM:] = acc_k[:, 0:HEAD_DIM].astype(BF)
    d_v[...] = acc_v[:, 0:HEAD_DIM].astype(BF)
    half = width // 2
    for dest in range(rows // width):
        low_rows = slice(dest * width, dest * width + half)
        high_rows = slice(dest * width + half, (dest + 1) * width)
        packed[dest, 0:width, :] = d_qk[dest * width : (dest + 1) * width, :]
        packed[dest, width:, :] = jnp.concatenate([d_v[low_rows, :], d_v[high_rows, :]], axis=1)


def kernel_call(kernel, scalars, operands, outs, scratch, work, smem_out=None):
    vmem = pl.BlockSpec(memory_space=pltpu.VMEM)
    smem = pl.BlockSpec(memory_space=pltpu.SMEM)
    out_shape = [jax.ShapeDtypeStruct(shape, kind) for shape, kind in outs]
    out_specs = [vmem] * len(outs)
    if smem_out is not None:
        out_shape.append(jax.ShapeDtypeStruct((smem_out,), jnp.int32))
        out_specs.append(smem)
    return pl.pallas_call(
        kernel,
        out_shape=tuple(out_shape),
        in_specs=[smem] * len(scalars) + [vmem] * len(operands),
        out_specs=tuple(out_specs),
        scratch_shapes=[pltpu.VMEM(shape, kind) for shape, kind in scratch],
        cost_estimate=pl.CostEstimate(flops=work, bytes_accessed=8 << 20, transcendentals=0),
    )(*scalars, *operands)


def attend_forward(own, seq_own, nat, tr, width):
    rows = nat.shape[0]
    pair = 2 * HEAD_DIM
    return kernel_call(
        forward_kernel,
        (own,),
        (seq_own, nat, tr),
        [
            ((rows // width, width // 2, pair), BF),
            ((rows, HEAD_DIM), F32),
            ((1, rows), F32),
            ((width, HEAD_DIM), F32),
            ((1, TILE), F32),
            ((1, rows), jnp.int32),
            ((1, TILE), jnp.int32),
            ((1, TILE), jnp.int32),
        ],
        [((TILE, pair), BF)],
        16 * rows * rows * HEAD_DIM,
        2 * (rows // TILE) + 4,
    )


def attend_backward_last(own, meta, start_own, end_own, nat, tr, came, lse_own, delta_own, width):
    rows = nat.shape[0]
    pair = 2 * HEAD_DIM
    return kernel_call(
        backward_last_kernel,
        (own, meta),
        (start_own, end_own, nat, tr, came, lse_own, delta_own),
        [((width, pair), BF), ((width, HEAD_DIM), BF)],
        [((rows + TILE - width, pair), BF)] * 2 + [((TILE, pair), BF)] * 2,
        4 * rows * rows * HEAD_DIM,
    )


def attend_backward(meta, start, nat, tr, came, out_nat, lse, width):
    rows = nat.shape[0]
    pair = 2 * HEAD_DIM
    return kernel_call(
        backward_kernel,
        (meta,),
        (start, nat, tr, came, out_nat, lse),
        [
            ((rows // width, width + width // 2, pair), BF),
            ((rows, pair), BF),
            ((rows, HEAD_DIM), BF),
        ],
        [((rows, pair), BF)] * 2 + [((rows, pair), F32)] * 2,
        40 * rows * rows * HEAD_DIM,
    )


def join_kernel(pieces, shared, weights, facts, joined, dots, dots_bias):
    heads = pieces.shape[0]
    running = [jnp.zeros((joined.shape[0], 2 * HEAD_DIM), F32)] * 2
    rest = [0.0, 0.0]
    units = 3 * (heads + 1)

    def unit(index):
        part, head = divmod(index, heads + 1)
        columns = slice(part * HEAD_DIM, (part + 1) * HEAD_DIM)
        return shared[:, columns] if head == heads else pieces[head, :, columns]

    facts_of = [facts[head].astype(F32) for head in range(heads)]
    sums = [fact[0:1, :] for fact in facts_of] + [sum(fact[1:2, :] for fact in facts_of)]

    def unit_sum(index):
        part, head = divmod(index, heads + 1)
        return sums[head][:, part * HEAD_DIM : (part + 1) * HEAD_DIM]

    for block in range((units + 1) // 2):
        paired = 2 * block + 1 < units
        if paired:
            values = jnp.concatenate([unit(2 * block), unit(2 * block + 1)], axis=1)
        else:
            values = unit(2 * block)
        at = slice(2 * block * HEAD_DIM, 2 * block * HEAD_DIM + values.shape[1])
        values = values.astype(F32)
        joined[:, at] = values
        weight = weights[:, at].astype(F32)
        row = [unit_sum(2 * block + i) for i in range(1 + paired)]
        products = [values * weight, weight * jnp.concatenate(row, axis=1)]
        if paired:
            running = [so_far + product for so_far, product in zip(running, products)]
        else:
            rest = [jnp.sum(product, axis=1, keepdims=True) for product in products]
    dots[...] = jnp.sum(running[0], axis=1, keepdims=True) + rest[0]
    dots_bias[...] = jnp.sum(running[1], axis=1, keepdims=True) + rest[1]


def join_heads(pieces, shared, weights):
    heads, _, columns = pieces.shape
    rows = weights.shape[0]
    step = 272 if rows % 272 == 0 else rows
    return pl.pallas_call(
        join_kernel,
        grid=(rows // step,),
        out_shape=(
            jax.ShapeDtypeStruct(weights.shape, F32),
            jax.ShapeDtypeStruct((rows, 1), F32),
            jax.ShapeDtypeStruct((rows, 1), F32),
        ),
        in_specs=[
            pl.BlockSpec((heads, step, columns), lambda i: (0, i, 0)),
            pl.BlockSpec((step, shared.shape[1]), lambda i: (i, 0)),
            pl.BlockSpec((step, weights.shape[1]), lambda i: (i, 0)),
            pl.BlockSpec((heads, 8, columns), lambda i: (0, pieces.shape[1] // 8 - 1, 0)),
        ],
        out_specs=(
            pl.BlockSpec((step, weights.shape[1]), lambda i: (i, 0)),
            pl.BlockSpec((step, 1), lambda i: (i, 0)),
            pl.BlockSpec((step, 1), lambda i: (i, 0)),
        ),
        cost_estimate=pl.CostEstimate(flops=1 << 20, bytes_accessed=14 << 20, transcendentals=0),
        name="join_heads",
    )(pieces, shared, weights, pieces)


def split_two(values):
    high = values.astype(BF)
    low = (values - high.astype(F32)).astype(BF)
    return [high, low]


def round_up(value, step):
    return (value + step - 1) // step * step


def to_tensor(part, ways):
    spread = jnp.broadcast_to(part[None], (ways,) + part.shape)
    got = lax.all_to_all(spread, "tensor", 0, 0, tiled=True)
    return got.reshape(ways * part.shape[0], part.shape[1])


def sum_tensor(partial, ways):
    rows = partial.shape[0] // ways
    got = lax.all_to_all(
        partial.astype(BF).reshape(ways, rows, partial.shape[1]), "tensor", 0, 0, tiled=True
    )
    return jnp.sum(got.astype(F32), axis=0)


def head_columns(matrix, head, width):
    return [
        lax.dynamic_slice_in_dim(matrix, part * width + head * HEAD_DIM, HEAD_DIM, 1)
        for part in range(3)
    ]


def gelu_pair(pre):
    factor = math.sqrt(2.0 / math.pi)
    square = pre * pre
    bend = jnp.tanh(factor * (pre + 0.044715 * pre * square))
    value = 0.5 * pre * (1.0 + bend)
    slope = 0.5 * (1.0 + bend) + 0.5 * pre * (1.0 - bend * bend) * factor * (
        1.0 + 3.0 * 0.044715 * square
    )
    return value, slope


def shards(
    tokens, segments, w_qkv, w_out, ln1_gain, ln1_bias, ln2_gain, ln2_bias, w_up, w_down, out_grad
):
    rows, width = tokens.shape
    count = lax.axis_size("shard")
    ways_c = lax.axis_size("context")
    ways_t = lax.axis_size("tensor")
    ways = ways_c * ways_t
    part_rows = w_qkv.shape[0]
    device = lax.axis_index(GROUP)
    shared = HEADS - 1
    padded = round_up(width, 128)
    columns = 3 * HEAD_DIM

    vectors = gather_small(
        jnp.stack([ln1_gain, ln1_bias, ln2_gain, ln2_bias]), count, 1
    ).astype(F32)
    gain_one, bias_one, gain_two, bias_two = [vectors[i : i + 1] for i in range(4)]

    inputs = tokens.astype(F32)
    unit_one, inverse_one = norm_stats(inputs)
    low_one = (unit_one * gain_one + bias_one).astype(BF)
    seq_row = segments[0]
    wide_one = jnp.concatenate(
        [low_one, seq_row[:, None].astype(BF), jnp.zeros((rows, padded - width - 1), BF)], axis=1
    )
    rows_one = lax.all_gather(wide_one, GROUP, axis=0, tiled=True)

    mine = head_columns(w_qkv, device, width)
    last = [
        w_qkv[:, part * width + shared * HEAD_DIM : part * width + (shared + 1) * HEAD_DIM]
        for part in range(3)
    ]
    head_w = gather_small(
        jnp.concatenate([mine[0], last[0], mine[1], last[1], mine[2], last[2]], axis=1),
        count,
        0,
    )
    head_w = jnp.pad(head_w, ((0, padded - width), (0, 0)))
    mark = (jnp.arange(padded)[:, None] == width) & (jnp.arange(16)[None] == 0)
    turn_w = jnp.concatenate([head_w[:, 2 * HEAD_DIM :], mark.astype(BF)], axis=1)
    out_full = gather_large(w_out, count, 0)
    up_full = gather_large(w_up, count, 0)
    down_turned = gather_large(w_down.T, count, 0)
    up_turned = after(up_full.T, up_full)
    down_full = after(down_turned.T, down_turned)
    qkv_full = gather_large(w_qkv, count, 0)
    grads_all = lax.all_gather(out_grad, "tensor", axis=0, tiled=True)
    split = ways * HEAD_DIM
    out_wide = jnp.concatenate(
        [
            out_full[:split].reshape(ways, HEAD_DIM, width),
            jnp.broadcast_to(out_full[None, split:], (ways, HEAD_DIM, width)),
        ],
        axis=1,
    ).reshape(2 * split, width)

    own = (device * rows).reshape(1).astype(jnp.int32)
    seq_own = jnp.concatenate(
        [seq_row, jnp.broadcast_to(seq_row[-1:], (TILE - rows,))]
    ).astype(F32)[None]
    nat = jnp.dot(rows_one, head_w, preferred_element_type=F32).astype(BF)
    tr = contract(turn_w, rows_one, 0, 1).astype(BF)
    packed, out_nat, lse, last_out, last_lse, start, start_own, end_own, meta = attend_forward(
        own, seq_own, nat, tr, rows
    )
    got = lax.all_to_all(packed, GROUP, 0, 0, tiled=True)
    half = rows // 2
    got = got.reshape(ways, half, 2, HEAD_DIM).transpose(2, 1, 0, 3).reshape(rows, split)
    attended = jnp.concatenate([got, last_out.astype(BF)], axis=1)

    resid = inputs + jnp.dot(attended, out_full, preferred_element_type=F32)
    unit_two, inverse_two = norm_stats(resid)
    low_two = (unit_two * gain_two + bias_two).astype(BF)

    d_hidden = jnp.dot(grads_all, down_turned, preferred_element_type=F32)
    rows_two = to_tensor(low_two, ways_t)
    rows_two, d_hidden = lax.optimization_barrier((rows_two, d_hidden))
    hidden, slope = gelu_pair(jnp.dot(rows_two, up_full, preferred_element_type=F32))
    hidden = hidden.astype(BF)
    d_pre = (d_hidden * slope).astype(BF)
    d_normed_two = sum_tensor(jnp.dot(d_pre, up_turned, preferred_element_type=F32), ways_t)

    grad_up = contract(rows_two, d_pre, 0, 0).astype(BF)
    grad_down = contract(grads_all, hidden, 0, 0).astype(BF)
    mixed = jnp.dot(hidden, down_full, preferred_element_type=F32).astype(BF)

    grad_in = out_grad.astype(F32)
    d_resid = grad_in + norm_back(d_normed_two, unit_two, inverse_two, gain_two)
    d_branch = d_resid.astype(BF)

    d_wide = contract(d_branch, out_wide, 1, 1).astype(BF)
    last_grad = d_wide[:, HEAD_DIM : 2 * HEAD_DIM]
    last_delta = jnp.sum(last_grad.astype(F32) * last_out, axis=1)
    pieces = split_two(last_lse[0, :rows]) + split_two(last_delta)
    extra = jnp.pad(jnp.stack(pieces), ((0, 0), (0, TILE - rows))).reshape(8, 128)
    extra = jnp.pad(extra, ((0, 8), (0, 0)))
    payload = jnp.concatenate(
        [
            d_wide.reshape(rows, ways, 2 * HEAD_DIM).transpose(1, 0, 2),
            jnp.broadcast_to(extra[None], (ways,) + extra.shape),
        ],
        axis=1,
    )
    came = lax.all_to_all(payload, GROUP, 0, 0, tiled=True)
    mixed = rotate(mixed.reshape(ways_t, rows, width), ways_t, came)
    came_heads = came
    delta_own = jnp.pad(last_delta, (0, TILE - rows))[None]

    late_branch = after(d_branch, payload)

    grad_out_w = jnp.concatenate(
        [
            contract(attended, late_branch, 0, 0).astype(BF),
            jnp.sum(d_normed_two * unit_two, axis=0)[:, None].astype(BF),
            jnp.sum(d_normed_two, axis=0)[:, None].astype(BF),
            jnp.zeros((width, padded - width - 2), BF),
        ],
        axis=1,
    )
    last_qk, last_v = attend_backward_last(
        own, meta, start_own, end_own, nat, tr, came, last_lse, delta_own, rows
    )
    last_all = jnp.concatenate([last_qk, last_v], axis=1)
    chunk = padded // ways
    grad_last = contract(wide_one, last_all, 0, 0).astype(BF)
    grad_last = lax.all_to_all(
        grad_last.reshape(ways, chunk, columns), GROUP, 0, 0, tiled=True
    )

    packed, d_qk, d_v = attend_backward(meta, start, nat, tr, came, out_nat, lse, rows)
    came = lax.all_to_all(packed, GROUP, 0, 0, tiled=True)
    grad_last = jnp.sum(grad_last.astype(F32), axis=0)

    d_head = jnp.concatenate([d_qk, d_v], axis=1)
    grad_mine = contract(rows_one, d_head, 0, 0)[:width]
    wide = 256
    sums = jnp.stack(
        [jnp.sum(d_head.astype(F32), axis=0), jnp.sum(last_all.astype(F32), axis=0)]
    )
    extra = jnp.concatenate([grad_last, jnp.pad(sums, ((0, 6), (0, 0)))], axis=0)
    both = jnp.concatenate(
        [
            grad_mine.reshape(count, part_rows, columns),
            jnp.broadcast_to(extra[None], (count,) + extra.shape),
        ],
        axis=1,
    )
    both = jnp.pad(both, ((0, 0), (0, 0), (0, wide - columns)))
    both = sum_shard_rows(both.reshape(count * (part_rows + chunk + 8), wide), count)
    payload = both.astype(BF)

    pair = reduce_rows(
        jnp.concatenate([grad_up, grad_down], axis=1), count, ways_c, (grad_up, d_qk, both)
    )
    grad_out_w = reduce_rows(grad_out_w, count, ways_c, (grad_out_w, came_heads, d_qk))
    piece = part_rows // ways_c
    deep = round_up(-(-piece // ways_t), 8)
    grad_out_w = jnp.pad(grad_out_w, ((0, deep * ways_t - piece), (0, 0)))
    grad_out_w = rotate(grad_out_w.reshape(ways_t, deep, padded), ways_t, last_qk)
    sent = send_rows(pair, ways_c)
    grad_out_w = total(grad_out_w).astype(BF)
    grad_out_w = gather_tensor(grad_out_w, ways_t)[:piece]
    grad_out_w = gather_rows(grad_out_w, send_rows(grad_out_w, ways_c), ways_c)

    pieces = lax.all_gather(payload, GROUP, axis=0, tiled=True)
    pieces = pieces.reshape((ways,) + payload.shape)
    shared_w = pieces[:, part_rows : part_rows + chunk, :columns].reshape(ways * chunk, columns)
    shared_w = lax.dynamic_slice_in_dim(
        shared_w, lax.axis_index("shard") * part_rows, part_rows, 0
    )
    grad_qkv, dots, dots_bias = join_heads(pieces, shared_w, w_qkv)
    grad_bias_one = dots_bias[:, 0]
    grad_gain_one = (dots[:, 0] - ln1_bias.astype(F32) * grad_bias_one) / ln1_gain.astype(F32)
    grad_out_w = grad_out_w.astype(F32)

    result = (resid + total([mixed[0]] + [after(share, payload) for share in mixed[1:]])).astype(BF)
    sent = None if sent is None else after(sent, payload)
    pair = gather_rows(pair, sent, ways_c).astype(F32)
    grad_up = pair[:, : up_full.shape[1]]
    grad_down = pair[:, up_full.shape[1] :].T

    came_qk = came[:, :rows].reshape(ways, rows, 2, HEAD_DIM).transpose(1, 2, 0, 3)
    came_qk = came_qk.reshape(rows, 2, split)
    came_v = came[:, rows:].reshape(ways, half, 2, HEAD_DIM).transpose(2, 1, 0, 3)
    came_v = came_v.reshape(rows, 1, split)
    came = jnp.concatenate([came_qk, came_v], axis=1)
    d_projected = jnp.concatenate(
        [came, last_all.reshape(rows, 3, HEAD_DIM)], axis=2
    ).reshape(rows, 3 * width)
    d_normed_one = contract(d_projected, qkv_full, 1, 1)
    input_grad = (d_resid + norm_back(d_normed_one, unit_one, inverse_one, gain_one)).astype(BF)
    return (
        result,
        input_grad,
        grad_qkv,
        grad_out_w[:, :width],
        grad_gain_one,
        grad_bias_one,
        grad_out_w[:, width],
        grad_out_w[:, width + 1],
        grad_up,
        grad_down,
    )


def solution(mesh):
    in_specs = (
        P(("shard", "context", "tensor"), None),
        P("shard", ("context", "tensor")),
        P("shard", None),
        P("shard", None),
        P("shard"),
        P("shard"),
        P("shard"),
        P("shard"),
        P("shard", "tensor"),
        P("tensor", "shard"),
        P(("shard", "context", "tensor"), None),
    )
    out_specs = (
        P(("shard", "context", "tensor"), None),
        P(("shard", "context", "tensor"), None),
        P("shard", None),
        P("shard", None),
        P("shard"),
        P("shard"),
        P("shard"),
        P("shard"),
        P("shard", "tensor"),
        P("tensor", "shard"),
    )
    return jax.shard_map(shards, mesh=mesh, in_specs=in_specs, out_specs=out_specs, check_vma=False)
```

```python
import math

import jax
import jax.numpy as jnp
from jax import lax
from jax.experimental import pallas as pl
from jax.experimental.pallas import tpu as pltpu
from jax.sharding import PartitionSpec as P


HEADS = 17
HEAD_DIM = 64
SEQS = 6
EPSILON = 1e-05
NEG = -1e30
GROUP = ("context", "tensor")
TILE = 256
BF = jnp.bfloat16
F32 = jnp.float32


def contract(left, right, left_dim, right_dim):
    return lax.dot_general(
        left, right, (((left_dim,), (right_dim,)), ((), ())), preferred_element_type=F32
    )


def norm_stats(values):
    average = jnp.mean(values, axis=-1, keepdims=True)
    centred = values - average
    variance = jnp.mean(centred * centred, axis=-1, keepdims=True)
    inverse = lax.rsqrt(variance + EPSILON)
    return centred * inverse, inverse


def norm_back(grad, unit, inverse, gain):
    scaled = grad * gain
    first = jnp.mean(scaled, axis=-1, keepdims=True)
    second = jnp.mean(scaled * unit, axis=-1, keepdims=True)
    return inverse * (scaled - first - unit * second)


def swap_shard(part):
    return lax.ppermute(part, "shard", [(0, 1), (1, 0)])


def in_order(mine, other, axis):
    index = lax.axis_index("shard")
    return jnp.where(
        index == 0,
        jnp.concatenate([mine, other], axis=axis),
        jnp.concatenate([other, mine], axis=axis),
    )


def gather_small(part, count, axis):
    if count != 2:
        return lax.all_gather(part, "shard", axis=axis, tiled=True)
    return in_order(part, swap_shard(part), axis)


def gather_large(part, count, axis):
    if count != 2:
        return lax.all_gather(part, "shard", axis=axis, tiled=True)
    ways = lax.axis_size("context")
    core = lax.rem(lax.axis_index("context"), 2)
    half = part.shape[axis] // 2
    mine = lax.dynamic_slice_in_dim(part, core * half, half, axis)
    fetched = swap_shard(mine)
    partner = lax.ppermute(fetched, "context", [(i, i ^ 1) for i in range(ways)])
    other = jnp.where(
        core == 0,
        jnp.concatenate([fetched, partner], axis=axis),
        jnp.concatenate([partner, fetched], axis=axis),
    )
    return in_order(part, other, axis)


def swap_half(blocks, bit, axis, axis_name, pairs):
    kept = lax.dynamic_index_in_dim(blocks, bit, axis, keepdims=False)
    away = lax.dynamic_index_in_dim(blocks, 1 - bit, axis, keepdims=False).astype(BF)
    came = lax.ppermute(away, axis_name, pairs)
    return kept, came


def add(kept, came):
    return kept.astype(F32) + came.astype(F32)


def sum_shard_rows(partial, count):
    if count != 2:
        return lax.psum_scatter(
            partial.astype(BF), "shard", scatter_dimension=0, tiled=True
        ).astype(F32)
    index = lax.axis_index("shard")
    blocks = partial.reshape((2, -1) + partial.shape[1:])
    return add(*swap_half(blocks, index, 0, "shard", [(0, 1), (1, 0)]))


def reduce_rows(partial, count, ways_c, gates):
    if count != 2 or ways_c != 4:
        return lax.psum_scatter(partial, ("shard", "context"), scatter_dimension=0, tiled=True)
    context = lax.axis_index("context")
    core, chip = lax.rem(context, 2), lax.div(context, 2)
    rows, columns = partial.shape
    blocks = partial.reshape(2, 2, 2, rows // 8, columns)
    kept, came = swap_half(blocks, core, 2, "context", [(i, i ^ 1) for i in range(4)])
    blocks = add(kept, after(came, gates[0])).astype(BF)
    kept, came = swap_half(blocks, chip, 1, "context", [(i, i ^ 2) for i in range(4)])
    blocks = add(kept, after(came, gates[1])).astype(BF)
    kept, came = swap_half(blocks, lax.axis_index("shard"), 0, "shard", [(0, 1), (1, 0)])
    return add(kept, after(came, gates[2])).astype(BF)


def send_rows(part, ways_c):
    if ways_c != 4:
        return None
    return lax.ppermute(part, "context", [(i, i ^ 2) for i in range(4)])


def gather_rows(part, sent, ways_c):
    if ways_c != 4:
        return lax.all_gather(part, "context", axis=0, tiled=True)
    context = lax.axis_index("context")
    core, chip = lax.rem(context, 2), lax.div(context, 2)
    both = jnp.where(chip == 0, jnp.stack([part, sent]), jnp.stack([sent, part]))
    came = lax.ppermute(both, "context", [(i, i ^ 1) for i in range(4)])
    all_rows = jnp.where(
        core == 0, jnp.stack([both, came], axis=1), jnp.stack([came, both], axis=1)
    )
    return all_rows.reshape((4 * part.shape[0],) + part.shape[1:])


def rotate(blocks, ways, gate):
    index = lax.axis_index("tensor")
    shares = [lax.dynamic_index_in_dim(blocks, index, 0, keepdims=False)]
    for turn in range(1, ways):
        target = lax.rem(index + turn, ways)
        away = lax.dynamic_index_in_dim(blocks, target, 0, keepdims=False)
        away = after(away, gate)
        shares.append(lax.ppermute(away, "tensor", [(i, (i + turn) % ways) for i in range(ways)]))
    return shares


def gather_tensor(part, ways, gate):
    index = lax.axis_index("tensor")
    parts = [part] + [
        after(lax.ppermute(part, "tensor", [(i, (i + turn) % ways) for i in range(ways)]), gate)
        for turn in range(1, ways)
    ]
    parts = jnp.stack(parts)
    return jnp.concatenate(
        [
            lax.dynamic_index_in_dim(parts, lax.rem(index + ways - i, ways), 0, keepdims=False)
            for i in range(ways)
        ]
    )


def total(shares):
    return sum(share.astype(F32) for share in shares)


def after(value, *others):
    return lax.optimization_barrier((value,) + others)[0]


def pick_half(pair, high, scale=1.0):
    first = lax.broadcasted_iota(jnp.int32, pair.shape, 1) < HEAD_DIM
    values = pair.astype(F32) * scale
    return (jnp.where(first, 0.0, values) if high else jnp.where(first, values, 0.0)).astype(BF)


def lane_ids(count):
    return lax.broadcasted_iota(jnp.int32, (1, count), 1)


def band(shape, low, high, first_key):
    key = first_key + lax.broadcasted_iota(jnp.int32, shape, 0)
    return (key >= low) & (key <= high)


def forward_kernel(
    own, seq_own, nat, tr, packed, out_nat, lse, out_last, lse_last, start, start_own, end_own, meta,
    q_pad,
):
    rows = nat.shape[0]
    blocks = rows // TILE
    width = out_last.shape[0]
    scale = 1.0 / math.sqrt(HEAD_DIM)

    seq = tr[256:272, :].astype(F32)[0:1, :]
    mine = seq_own[...]
    begin = jnp.zeros_like(seq)
    begin_own = jnp.zeros_like(mine)
    finish_own = jnp.full_like(mine, float(rows))
    for number in range(1, SEQS):
        before = jnp.sum((seq < number).astype(F32), axis=1, keepdims=True)
        begin = jnp.where(seq >= number, before, begin)
        begin_own = jnp.where(mine >= number, before, begin_own)
        finish_own = jnp.where(mine == number - 1, before, finish_own)
    start[...] = begin.astype(jnp.int32)
    start_own[...] = begin_own.astype(jnp.int32)
    end_own[...] = finish_own.astype(jnp.int32)
    base = pl.multiple_of(own[0], 16)
    meta[2 * blocks] = jnp.min(begin_own).astype(jnp.int32) // TILE
    meta[2 * blocks + 1] = (base + width - 1) // TILE + 1
    meta[2 * blocks + 2] = base // width
    meta[2 * blocks + 3] = (jnp.max(finish_own).astype(jnp.int32) + width - 1) // width

    def step(queries, limits, v_row, low_tile, carry):
        top, total, acc = carry
        places, scores = [], []
        for tile in (low_tile, low_tile + 1):
            at = pl.multiple_of(jnp.clip(tile, 0, blocks - 1) * TILE, TILE)
            score = contract(nat[pl.ds(at, TILE), 128:256], queries, 1, 1)
            if limits is not None:
                score = jnp.where(band(score.shape, *limits, tile * TILE), score, NEG)
            places.append(at)
            scores.append(score)
        now = jnp.maximum(top, jnp.max(jnp.maximum(*scores), axis=0, keepdims=True))
        fade = jnp.exp(top - now)
        total, acc = total * fade, acc * fade
        for at, score in zip(places, scores):
            shares = jnp.exp(score - now)
            total = total + jnp.sum(shares, axis=0, keepdims=True)
            values = tr[v_row : v_row + HEAD_DIM, pl.ds(at, TILE)]
            acc = acc + contract(values, shares.astype(BF), 1, 0)
        return now, total, acc

    empty = (
        jnp.full((1, TILE), NEG, F32),
        jnp.zeros((1, TILE), F32),
        jnp.zeros((HEAD_DIM, TILE), F32),
    )

    def one_block(qb, unused):
        at = pl.multiple_of(qb * TILE, TILE)
        queries = pick_half(nat[pl.ds(at, TILE), 0:128], False, scale)
        low = start[:, pl.ds(at, TILE)]
        near = low.astype(F32)
        first = jnp.min(near).astype(jnp.int32) // TILE
        full = (jnp.max(near).astype(jnp.int32) + TILE - 1) // TILE
        plain = jnp.maximum(qb - 1 - full, 0) // 2
        every = (jnp.maximum(qb - 1 - first, 0) + 1) // 2
        meta[qb] = plain
        meta[blocks + qb] = every
        limits = (low, at + lane_ids(TILE))
        carry = step(queries, limits, 128, qb - 1, empty)
        carry = lax.fori_loop(
            0, plain, lambda j, c: step(queries, None, 128, qb - 3 - 2 * j, c), carry
        )
        carry = lax.fori_loop(
            plain, every, lambda j, c: step(queries, limits, 128, qb - 3 - 2 * j, c), carry
        )
        top, total, acc = carry
        lse[:, pl.ds(at, TILE)] = top + jnp.log(total)
        out_nat[pl.ds(at, TILE), :] = (acc / total).T
        return unused

    lax.fori_loop(0, blocks, one_block, 0)

    q_pad[...] = jnp.zeros_like(q_pad)
    q_pad[0:width, :] = pick_half(nat[pl.ds(base, width), 0:128], True, scale)
    limits = (start_own[...], base + lane_ids(TILE))
    begin_tile, end_tile = meta[2 * blocks], meta[2 * blocks + 1]
    top, total, acc = lax.fori_loop(
        0,
        (end_tile - begin_tile + 1) // 2,
        lambda j, c: step(q_pad[...], limits, 192, begin_tile + 2 * j, c),
        empty,
    )
    lse_last[...] = top + jnp.log(total)
    out_last[...] = (acc / total).T[0:width, :]

    half = width // 2
    for dest in range(rows // width):
        first = out_nat[dest * width : dest * width + half, :]
        second = out_nat[dest * width + half : (dest + 1) * width, :]
        packed[dest] = jnp.concatenate([first, second], axis=1).astype(BF)


def backward_last_kernel(
    own, meta, start_own, end_own, nat, tr, came, lse_own, delta_own, last_qk, last_v,
    q_rows, o_rows, pad_q, pad_o,
):
    rows = nat.shape[0]
    blocks = rows // TILE
    width = last_qk.shape[0]
    scale = 1.0 / math.sqrt(HEAD_DIM)
    base = pl.multiple_of(own[0], 16)

    q_rows[0:rows, :] = (nat[:, 0:128].astype(F32) * scale).astype(BF)
    q_rows[rows:, :] = jnp.zeros((q_rows.shape[0] - rows, 2 * HEAD_DIM), BF)
    for source in range(rows // width):
        o_rows[source * width : (source + 1) * width, :] = came[source, 0:width, :]
    o_rows[rows:, :] = jnp.zeros((o_rows.shape[0] - rows, 2 * HEAD_DIM), BF)

    pad_q[...] = jnp.zeros_like(pad_q)
    pad_o[...] = jnp.zeros_like(pad_o)
    pad_q[0:width, :] = pick_half(nat[pl.ds(base, width), 0:128], True, scale)
    pad_o[0:width, :] = pick_half(o_rows[pl.ds(base, width), :], True)
    limits = (start_own[...], base + lane_ids(TILE))

    begin_tile, end_tile = meta[2 * blocks], meta[2 * blocks + 1]

    def query_step(j, d_query):
        for tile in (begin_tile + 2 * j, begin_tile + 2 * j + 1):
            at = pl.multiple_of(jnp.minimum(tile, blocks - 1) * TILE, TILE)
            scores = contract(nat[pl.ds(at, TILE), 128:256], pad_q[...], 1, 1)
            scores = jnp.where(band(scores.shape, *limits, tile * TILE), scores, NEG)
            shares = jnp.exp(scores - lse_own[...])
            d_shares = contract(nat[pl.ds(at, TILE), 256:384], pad_o[...], 1, 1)
            d_scores = (shares * (d_shares - delta_own[...])).astype(BF)
            keys_t = tr[HEAD_DIM : 2 * HEAD_DIM, pl.ds(at, TILE)]
            d_query = d_query + contract(keys_t, d_scores, 1, 0)
        return d_query

    d_query = lax.fori_loop(
        0, (end_tile - begin_tile + 1) // 2, query_step, jnp.zeros((HEAD_DIM, TILE), F32)
    )
    last_qk[:, 0:HEAD_DIM] = (d_query.T[0:width, :] * scale).astype(BF)

    keys = pick_half(nat[pl.ds(base, width), 128:256], True)
    values = pick_half(nat[pl.ds(base, width), 256:384], True)
    key = base + lax.broadcasted_iota(jnp.int32, (width, TILE), 0)
    finish = jnp.broadcast_to(end_own[...].astype(F32), (128, TILE)).T[0:width, 0:1]
    finish = finish.astype(jnp.int32)
    lane = lane_ids(TILE)

    ways = rows // width

    def key_step(j, carry):
        d_key, d_value = carry
        for turn in range(2):
            query_source = begin_source + 2 * j + turn
            source = jnp.minimum(query_source, ways - 1)
            at = pl.multiple_of(source * width, 16)
            queries = q_rows[pl.ds(at, TILE), :]
            grads = o_rows[pl.ds(at, TILE), :]
            facts = came[source, width : width + 16, :].astype(F32)
            log_total = jnp.concatenate([facts[0:1] + facts[2:3], facts[1:2] + facts[3:4]], axis=1)
            delta = jnp.concatenate([facts[4:5] + facts[6:7], facts[5:6] + facts[7:8]], axis=1)
            query = query_source * width + lane
            keep = (key <= query) & (query < finish) & (lane < width)
            scores = jnp.where(keep, contract(keys, queries, 1, 1), NEG)
            shares = jnp.exp(scores - log_total)
            d_shares = contract(values, grads, 1, 1)
            d_scores = (shares * (d_shares - delta)).astype(BF)
            d_key = d_key + contract(d_scores, queries, 1, 0)
            d_value = d_value + contract(shares.astype(BF), grads, 1, 0)
        return d_key, d_value

    zero = jnp.zeros((width, 2 * HEAD_DIM), F32)
    begin_source, end_source = meta[2 * blocks + 2], meta[2 * blocks + 3]
    d_key, d_value = lax.fori_loop(
        0, (end_source - begin_source + 1) // 2, key_step, (zero, zero)
    )
    last_qk[:, HEAD_DIM:] = d_key[:, HEAD_DIM:].astype(BF)
    last_v[...] = d_value[:, HEAD_DIM:].astype(BF)


def backward_kernel(
    meta, start, nat, tr, came, out_nat, lse, packed, d_qk, d_v, o_rows, q_rows, acc_k, acc_v
):
    rows = nat.shape[0]
    blocks = rows // TILE
    width = rows // packed.shape[0]
    scale = 1.0 / math.sqrt(HEAD_DIM)

    q_rows[...] = (nat[:, 0:128].astype(F32) * scale).astype(BF)
    for source in range(rows // width):
        o_rows[source * width : (source + 1) * width, :] = came[source, 0:width, :]
    acc_k[...] = jnp.zeros_like(acc_k)
    acc_v[...] = jnp.zeros_like(acc_v)

    def one_block(qb, unused):
        at_q = pl.multiple_of(qb * TILE, TILE)
        pair = q_rows[pl.ds(at_q, TILE), :]
        queries = pick_half(pair, False)
        grads = o_rows[pl.ds(at_q, TILE), :]
        product = grads[:, 0:HEAD_DIM].astype(F32) * out_nat[pl.ds(at_q, TILE), :]
        delta = jnp.sum(product.T, axis=0, keepdims=True)
        grads_low = pick_half(grads, False)
        log_total = lse[:, pl.ds(at_q, TILE)]
        limits = (start[:, pl.ds(at_q, TILE)], at_q + lane_ids(TILE))

        def step(masked, low_tile, d_query):
            tiles = (low_tile, low_tile + 1)
            places = [pl.multiple_of(jnp.maximum(tile, 0) * TILE, TILE) for tile in tiles]
            scores = [contract(nat[pl.ds(at, TILE), 128:256], queries, 1, 1) for at in places]
            d_shares = [contract(nat[pl.ds(at, TILE), 256:384], grads_low, 1, 1) for at in places]
            if masked:
                scores = [
                    jnp.where(band(score.shape, *limits, tile * TILE), score, NEG)
                    for score, tile in zip(scores, tiles)
                ]
            shares = [jnp.exp(score - log_total) for score in scores]
            d_scores = [
                (share * (d_share - delta)).astype(BF) for share, d_share in zip(shares, d_shares)
            ]
            added_v = [contract(share.astype(BF), grads, 1, 0) for share in shares]
            added_k = [contract(d_score, pair, 1, 0) for d_score in d_scores]
            for at, d_score in zip(places, d_scores):
                d_query = d_query + contract(tr[0:HEAD_DIM, pl.ds(at, TILE)], d_score, 1, 0)
            for at, value, key in zip(places, added_v, added_k):
                acc_v[pl.ds(at, TILE), :] += value
                acc_k[pl.ds(at, TILE), :] += key
            return d_query

        plain, every = meta[qb], meta[blocks + qb]
        d_query = step(True, qb - 1, jnp.zeros((HEAD_DIM, TILE), F32))
        d_query = lax.fori_loop(0, plain, lambda j, c: step(False, qb - 3 - 2 * j, c), d_query)
        d_query = lax.fori_loop(plain, every, lambda j, c: step(True, qb - 3 - 2 * j, c), d_query)
        d_qk[pl.ds(at_q, TILE), 0:HEAD_DIM] = (d_query.T * scale).astype(BF)
        return unused

    lax.fori_loop(0, blocks, one_block, 0)
    d_qk[:, HEAD_DIM:] = acc_k[:, 0:HEAD_DIM].astype(BF)
    d_v[...] = acc_v[:, 0:HEAD_DIM].astype(BF)
    half = width // 2
    for dest in range(rows // width):
        low_rows = slice(dest * width, dest * width + half)
        high_rows = slice(dest * width + half, (dest + 1) * width)
        packed[dest, 0:width, :] = d_qk[dest * width : (dest + 1) * width, :]
        packed[dest, width:, :] = jnp.concatenate([d_v[low_rows, :], d_v[high_rows, :]], axis=1)


def kernel_call(kernel, scalars, operands, outs, scratch, work, smem_out=None):
    vmem = pl.BlockSpec(memory_space=pltpu.VMEM)
    smem = pl.BlockSpec(memory_space=pltpu.SMEM)
    out_shape = [jax.ShapeDtypeStruct(shape, kind) for shape, kind in outs]
    out_specs = [vmem] * len(outs)
    if smem_out is not None:
        out_shape.append(jax.ShapeDtypeStruct((smem_out,), jnp.int32))
        out_specs.append(smem)
    return pl.pallas_call(
        kernel,
        out_shape=tuple(out_shape),
        in_specs=[smem] * len(scalars) + [vmem] * len(operands),
        out_specs=tuple(out_specs),
        scratch_shapes=[pltpu.VMEM(shape, kind) for shape, kind in scratch],
        cost_estimate=pl.CostEstimate(flops=work, bytes_accessed=8 << 20, transcendentals=0),
    )(*scalars, *operands)


def attend_forward(own, seq_own, nat, tr, width):
    rows = nat.shape[0]
    pair = 2 * HEAD_DIM
    return kernel_call(
        forward_kernel,
        (own,),
        (seq_own, nat, tr),
        [
            ((rows // width, width // 2, pair), BF),
            ((rows, HEAD_DIM), F32),
            ((1, rows), F32),
            ((width, HEAD_DIM), F32),
            ((1, TILE), F32),
            ((1, rows), jnp.int32),
            ((1, TILE), jnp.int32),
            ((1, TILE), jnp.int32),
        ],
        [((TILE, pair), BF)],
        16 * rows * rows * HEAD_DIM,
        2 * (rows // TILE) + 4,
    )


def attend_backward_last(own, meta, start_own, end_own, nat, tr, came, lse_own, delta_own, width):
    rows = nat.shape[0]
    pair = 2 * HEAD_DIM
    return kernel_call(
        backward_last_kernel,
        (own, meta),
        (start_own, end_own, nat, tr, came, lse_own, delta_own),
        [((width, pair), BF), ((width, HEAD_DIM), BF)],
        [((rows + TILE - width, pair), BF)] * 2 + [((TILE, pair), BF)] * 2,
        4 * rows * rows * HEAD_DIM,
    )


def attend_backward(meta, start, nat, tr, came, out_nat, lse, width):
    rows = nat.shape[0]
    pair = 2 * HEAD_DIM
    return kernel_call(
        backward_kernel,
        (meta,),
        (start, nat, tr, came, out_nat, lse),
        [
            ((rows // width, width + width // 2, pair), BF),
            ((rows, pair), BF),
            ((rows, HEAD_DIM), BF),
        ],
        [((rows, pair), BF)] * 2 + [((rows, pair), F32)] * 2,
        40 * rows * rows * HEAD_DIM,
    )


def join_kernel(pieces, shared, weights, facts, joined, dots, dots_bias):
    heads = pieces.shape[0]
    running = [jnp.zeros((joined.shape[0], 2 * HEAD_DIM), F32)] * 2
    rest = [0.0, 0.0]
    units = 3 * (heads + 1)

    def unit(index):
        part, head = divmod(index, heads + 1)
        columns = slice(part * HEAD_DIM, (part + 1) * HEAD_DIM)
        return shared[:, columns] if head == heads else pieces[head, :, columns]

    facts_of = [facts[head].astype(F32) for head in range(heads)]
    sums = [fact[0:1, :] for fact in facts_of] + [sum(fact[1:2, :] for fact in facts_of)]

    def unit_sum(index):
        part, head = divmod(index, heads + 1)
        return sums[head][:, part * HEAD_DIM : (part + 1) * HEAD_DIM]

    for block in range((units + 1) // 2):
        paired = 2 * block + 1 < units
        if paired:
            values = jnp.concatenate([unit(2 * block), unit(2 * block + 1)], axis=1)
        else:
            values = unit(2 * block)
        at = slice(2 * block * HEAD_DIM, 2 * block * HEAD_DIM + values.shape[1])
        values = values.astype(F32)
        joined[:, at] = values
        weight = weights[:, at].astype(F32)
        row = [unit_sum(2 * block + i) for i in range(1 + paired)]
        products = [values * weight, weight * jnp.concatenate(row, axis=1)]
        if paired:
            running = [so_far + product for so_far, product in zip(running, products)]
        else:
            rest = [jnp.sum(product, axis=1, keepdims=True) for product in products]
    dots[...] = jnp.sum(running[0], axis=1, keepdims=True) + rest[0]
    dots_bias[...] = jnp.sum(running[1], axis=1, keepdims=True) + rest[1]


def join_heads(pieces, shared, weights):
    heads, _, columns = pieces.shape
    rows = weights.shape[0]
    step = 272 if rows % 272 == 0 else rows
    return pl.pallas_call(
        join_kernel,
        grid=(rows // step,),
        out_shape=(
            jax.ShapeDtypeStruct(weights.shape, F32),
            jax.ShapeDtypeStruct((rows, 1), F32),
            jax.ShapeDtypeStruct((rows, 1), F32),
        ),
        in_specs=[
            pl.BlockSpec((heads, step, columns), lambda i: (0, i, 0)),
            pl.BlockSpec((step, shared.shape[1]), lambda i: (i, 0)),
            pl.BlockSpec((step, weights.shape[1]), lambda i: (i, 0)),
            pl.BlockSpec((heads, 8, columns), lambda i: (0, pieces.shape[1] // 8 - 1, 0)),
        ],
        out_specs=(
            pl.BlockSpec((step, weights.shape[1]), lambda i: (i, 0)),
            pl.BlockSpec((step, 1), lambda i: (i, 0)),
            pl.BlockSpec((step, 1), lambda i: (i, 0)),
        ),
        cost_estimate=pl.CostEstimate(flops=1 << 20, bytes_accessed=14 << 20, transcendentals=0),
        name="join_heads",
    )(pieces, shared, weights, pieces)


def split_two(values):
    high = values.astype(BF)
    low = (values - high.astype(F32)).astype(BF)
    return [high, low]


def round_up(value, step):
    return (value + step - 1) // step * step


def to_tensor(part, ways):
    spread = jnp.broadcast_to(part[None], (ways,) + part.shape)
    got = lax.all_to_all(spread, "tensor", 0, 0, tiled=True)
    return got.reshape(ways * part.shape[0], part.shape[1])


def sum_tensor(partial, ways):
    rows = partial.shape[0] // ways
    got = lax.all_to_all(
        partial.astype(BF).reshape(ways, rows, partial.shape[1]), "tensor", 0, 0, tiled=True
    )
    return jnp.sum(got.astype(F32), axis=0)


def head_columns(matrix, head, width):
    return [
        lax.dynamic_slice_in_dim(matrix, part * width + head * HEAD_DIM, HEAD_DIM, 1)
        for part in range(3)
    ]


def gelu_pair(pre):
    factor = math.sqrt(2.0 / math.pi)
    square = pre * pre
    bend = jnp.tanh(factor * (pre + 0.044715 * pre * square))
    value = 0.5 * pre * (1.0 + bend)
    slope = 0.5 * (1.0 + bend) + 0.5 * pre * (1.0 - bend * bend) * factor * (
        1.0 + 3.0 * 0.044715 * square
    )
    return value, slope


def shards(
    tokens, segments, w_qkv, w_out, ln1_gain, ln1_bias, ln2_gain, ln2_bias, w_up, w_down, out_grad
):
    rows, width = tokens.shape
    count = lax.axis_size("shard")
    ways_c = lax.axis_size("context")
    ways_t = lax.axis_size("tensor")
    ways = ways_c * ways_t
    part_rows = w_qkv.shape[0]
    device = lax.axis_index(GROUP)
    shared = HEADS - 1
    padded = round_up(width, 128)
    columns = 3 * HEAD_DIM

    vectors = gather_small(
        jnp.stack([ln1_gain, ln1_bias, ln2_gain, ln2_bias]), count, 1
    ).astype(F32)
    gain_one, bias_one, gain_two, bias_two = [vectors[i : i + 1] for i in range(4)]

    inputs = tokens.astype(F32)
    unit_one, inverse_one = norm_stats(inputs)
    low_one = (unit_one * gain_one + bias_one).astype(BF)
    seq_row = segments[0]
    wide_one = jnp.concatenate(
        [low_one, seq_row[:, None].astype(BF), jnp.zeros((rows, padded - width - 1), BF)], axis=1
    )
    rows_one = lax.all_gather(wide_one, GROUP, axis=0, tiled=True)

    mine = head_columns(w_qkv, device, width)
    last = [
        w_qkv[:, part * width + shared * HEAD_DIM : part * width + (shared + 1) * HEAD_DIM]
        for part in range(3)
    ]
    head_w = gather_small(
        jnp.concatenate([mine[0], last[0], mine[1], last[1], mine[2], last[2]], axis=1),
        count,
        0,
    )
    head_w = jnp.pad(head_w, ((0, padded - width), (0, 0)))
    mark = (jnp.arange(padded)[:, None] == width) & (jnp.arange(16)[None] == 0)
    turn_w = jnp.concatenate([head_w[:, 2 * HEAD_DIM :], mark.astype(BF)], axis=1)
    out_full = gather_large(w_out, count, 0)
    up_full = gather_large(w_up, count, 0)
    down_turned = gather_large(w_down.T, count, 0)
    up_turned = after(up_full.T, up_full)
    down_full = after(down_turned.T, down_turned)
    qkv_full = gather_large(w_qkv, count, 0)
    grads_all = lax.all_gather(out_grad, "tensor", axis=0, tiled=True)
    split = ways * HEAD_DIM
    out_wide = jnp.concatenate(
        [
            out_full[:split].reshape(ways, HEAD_DIM, width),
            jnp.broadcast_to(out_full[None, split:], (ways, HEAD_DIM, width)),
        ],
        axis=1,
    ).reshape(2 * split, width)

    own = (device * rows).reshape(1).astype(jnp.int32)
    seq_own = jnp.concatenate(
        [seq_row, jnp.broadcast_to(seq_row[-1:], (TILE - rows,))]
    ).astype(F32)[None]
    nat = jnp.dot(rows_one, head_w, preferred_element_type=F32).astype(BF)
    tr = contract(turn_w, rows_one, 0, 1).astype(BF)
    packed, out_nat, lse, last_out, last_lse, start, start_own, end_own, meta = attend_forward(
        own, seq_own, nat, tr, rows
    )
    got = lax.all_to_all(packed, GROUP, 0, 0, tiled=True)
    half = rows // 2
    got = got.reshape(ways, half, 2, HEAD_DIM).transpose(2, 1, 0, 3).reshape(rows, split)
    attended = jnp.concatenate([got, last_out.astype(BF)], axis=1)

    resid = inputs + jnp.dot(attended, out_full, preferred_element_type=F32)
    unit_two, inverse_two = norm_stats(resid)
    low_two = (unit_two * gain_two + bias_two).astype(BF)

    d_hidden = jnp.dot(grads_all, down_turned, preferred_element_type=F32)
    rows_two = to_tensor(low_two, ways_t)
    rows_two, d_hidden = lax.optimization_barrier((rows_two, d_hidden))
    hidden, slope = gelu_pair(jnp.dot(rows_two, up_full, preferred_element_type=F32))
    hidden = hidden.astype(BF)
    d_pre = (d_hidden * slope).astype(BF)
    d_normed_two = sum_tensor(jnp.dot(d_pre, up_turned, preferred_element_type=F32), ways_t)

    grad_up = contract(rows_two, d_pre, 0, 0).astype(BF)
    grad_down = contract(grads_all, hidden, 0, 0).astype(BF)
    mixed = jnp.dot(hidden, down_full, preferred_element_type=F32).astype(BF)

    grad_in = out_grad.astype(F32)
    d_resid = grad_in + norm_back(d_normed_two, unit_two, inverse_two, gain_two)
    d_branch = d_resid.astype(BF)

    d_wide = contract(d_branch, out_wide, 1, 1).astype(BF)
    last_grad = d_wide[:, HEAD_DIM : 2 * HEAD_DIM]
    last_delta = jnp.sum(last_grad.astype(F32) * last_out, axis=1)
    pieces = split_two(last_lse[0, :rows]) + split_two(last_delta)
    extra = jnp.pad(jnp.stack(pieces), ((0, 0), (0, TILE - rows))).reshape(8, 128)
    extra = jnp.pad(extra, ((0, 8), (0, 0)))
    payload = jnp.concatenate(
        [
            d_wide.reshape(rows, ways, 2 * HEAD_DIM).transpose(1, 0, 2),
            jnp.broadcast_to(extra[None], (ways,) + extra.shape),
        ],
        axis=1,
    )
    came = lax.all_to_all(payload, GROUP, 0, 0, tiled=True)
    mixed = rotate(mixed.reshape(ways_t, rows, width), ways_t, came)
    came_heads = came
    delta_own = jnp.pad(last_delta, (0, TILE - rows))[None]

    late_branch = after(d_branch, payload)

    grad_out_w = jnp.concatenate(
        [
            contract(attended, late_branch, 0, 0).astype(BF),
            jnp.sum(d_normed_two * unit_two, axis=0)[:, None].astype(BF),
            jnp.sum(d_normed_two, axis=0)[:, None].astype(BF),
            jnp.zeros((width, padded - width - 2), BF),
        ],
        axis=1,
    )
    last_qk, last_v = attend_backward_last(
        own, meta, start_own, end_own, nat, tr, came, last_lse, delta_own, rows
    )
    last_all = jnp.concatenate([last_qk, last_v], axis=1)
    chunk = padded // ways
    grad_last = contract(wide_one, last_all, 0, 0).astype(BF)
    grad_last = lax.all_to_all(
        grad_last.reshape(ways, chunk, columns), GROUP, 0, 0, tiled=True
    )

    packed, d_qk, d_v = attend_backward(meta, start, nat, tr, came, out_nat, lse, rows)
    came = lax.all_to_all(packed, GROUP, 0, 0, tiled=True)
    came_rows = came
    grad_last = jnp.sum(grad_last.astype(F32), axis=0)

    d_head = jnp.concatenate([d_qk, d_v], axis=1)
    grad_mine = contract(rows_one, d_head, 0, 0)[:width]
    wide = 256
    sums = jnp.stack(
        [jnp.sum(d_head.astype(F32), axis=0), jnp.sum(last_all.astype(F32), axis=0)]
    )
    extra = jnp.concatenate([grad_last, jnp.pad(sums, ((0, 6), (0, 0)))], axis=0)
    both = jnp.concatenate(
        [
            grad_mine.reshape(count, part_rows, columns),
            jnp.broadcast_to(extra[None], (count,) + extra.shape),
        ],
        axis=1,
    )
    both = jnp.pad(both, ((0, 0), (0, 0), (0, wide - columns)))
    both = sum_shard_rows(both.reshape(count * (part_rows + chunk + 8), wide), count)
    payload = both.astype(BF)

    pair = reduce_rows(
        jnp.concatenate([grad_up, grad_down], axis=1), count, ways_c, (grad_up, d_qk, came_rows)
    )
    grad_out_w = reduce_rows(grad_out_w, count, ways_c, (grad_out_w, came_heads, d_qk))
    piece = part_rows // ways_c
    deep = round_up(-(-piece // ways_t), 8)
    grad_out_w = jnp.pad(grad_out_w, ((0, deep * ways_t - piece), (0, 0)))
    grad_out_w = rotate(grad_out_w.reshape(ways_t, deep, padded), ways_t, last_qk)
    sent_pair = send_rows(pair, ways_c)
    grad_out_w = total([grad_out_w[0]] + [after(share, came_rows) for share in grad_out_w[1:]])
    grad_out_w = grad_out_w.astype(BF)
    pieces = lax.all_gather(payload, GROUP, axis=0, tiled=True)
    pieces = pieces.reshape((ways,) + payload.shape)
    shared_w = pieces[:, part_rows : part_rows + chunk, :columns].reshape(ways * chunk, columns)
    shared_w = lax.dynamic_slice_in_dim(
        shared_w, lax.axis_index("shard") * part_rows, part_rows, 0
    )
    grad_qkv, dots, dots_bias = join_heads(pieces, shared_w, w_qkv)
    grad_bias_one = dots_bias[:, 0]
    grad_gain_one = (dots[:, 0] - ln1_bias.astype(F32) * grad_bias_one) / ln1_gain.astype(F32)
    result = (resid + total([mixed[0]] + [after(share, payload) for share in mixed[1:]])).astype(BF)

    came_qk = came[:, :rows].reshape(ways, rows, 2, HEAD_DIM).transpose(1, 2, 0, 3)
    came_qk = came_qk.reshape(rows, 2, split)
    came_v = came[:, rows:].reshape(ways, half, 2, HEAD_DIM).transpose(2, 1, 0, 3)
    came_v = came_v.reshape(rows, 1, split)
    came = jnp.concatenate([came_qk, came_v], axis=1)
    d_projected = jnp.concatenate(
        [came, last_all.reshape(rows, 3, HEAD_DIM)], axis=2
    ).reshape(rows, 3 * width)
    d_normed_one = contract(d_projected, qkv_full, 1, 1)

    grad_out_w = gather_tensor(grad_out_w, ways_t, d_normed_one)[:piece]
    sent = send_rows(grad_out_w, ways_c)
    sent_pair = None if sent_pair is None else after(sent_pair, d_normed_one)
    pair = gather_rows(pair, sent_pair, ways_c).astype(F32)
    grad_up = pair[:, : up_full.shape[1]]
    grad_down = pair[:, up_full.shape[1] :].T
    grad_out_w = gather_rows(grad_out_w, sent, ways_c).astype(F32)

    input_grad = (d_resid + norm_back(d_normed_one, unit_one, inverse_one, gain_one)).astype(BF)
    return (
        result,
        input_grad,
        grad_qkv,
        grad_out_w[:, :width],
        grad_gain_one,
        grad_bias_one,
        grad_out_w[:, width],
        grad_out_w[:, width + 1],
        grad_up,
        grad_down,
    )


def solution(mesh):
    in_specs = (
        P(("shard", "context", "tensor"), None),
        P("shard", ("context", "tensor")),
        P("shard", None),
        P("shard", None),
        P("shard"),
        P("shard"),
        P("shard"),
        P("shard"),
        P("shard", "tensor"),
        P("tensor", "shard"),
        P(("shard", "context", "tensor"), None),
    )
    out_specs = (
        P(("shard", "context", "tensor"), None),
        P(("shard", "context", "tensor"), None),
        P("shard", None),
        P("shard", None),
        P("shard"),
        P("shard"),
        P("shard"),
        P("shard"),
        P("shard", "tensor"),
        P("tensor", "shard"),
    )
    return jax.shard_map(shards, mesh=mesh, in_specs=in_specs, out_specs=out_specs, check_vma=False)
```

```python
import math

import jax
import jax.numpy as jnp
from jax import lax
from jax.experimental import pallas as pl
from jax.experimental.pallas import tpu as pltpu
from jax.sharding import PartitionSpec as P


HEADS = 17
HEAD_DIM = 64
SEQS = 6
EPSILON = 1e-05
NEG = -1e30
GROUP = ("context", "tensor")
TILE = 256
BF = jnp.bfloat16
F32 = jnp.float32


def contract(left, right, left_dim, right_dim):
    return lax.dot_general(
        left, right, (((left_dim,), (right_dim,)), ((), ())), preferred_element_type=F32
    )


def norm_stats(values):
    average = jnp.mean(values, axis=-1, keepdims=True)
    centred = values - average
    variance = jnp.mean(centred * centred, axis=-1, keepdims=True)
    inverse = lax.rsqrt(variance + EPSILON)
    return centred * inverse, inverse


def norm_back(grad, unit, inverse, gain):
    scaled = grad * gain
    first = jnp.mean(scaled, axis=-1, keepdims=True)
    second = jnp.mean(scaled * unit, axis=-1, keepdims=True)
    return inverse * (scaled - first - unit * second)


def swap_shard(part):
    return lax.ppermute(part, "shard", [(0, 1), (1, 0)])


def in_order(mine, other, axis):
    index = lax.axis_index("shard")
    return jnp.where(
        index == 0,
        jnp.concatenate([mine, other], axis=axis),
        jnp.concatenate([other, mine], axis=axis),
    )


def gather_small(part, count, axis):
    if count != 2:
        return lax.all_gather(part, "shard", axis=axis, tiled=True)
    return in_order(part, swap_shard(part), axis)


def gather_large(part, count, axis):
    if count != 2:
        return lax.all_gather(part, "shard", axis=axis, tiled=True)
    ways = lax.axis_size("context")
    core = lax.rem(lax.axis_index("context"), 2)
    half = part.shape[axis] // 2
    mine = lax.dynamic_slice_in_dim(part, core * half, half, axis)
    fetched = swap_shard(mine)
    partner = lax.ppermute(fetched, "context", [(i, i ^ 1) for i in range(ways)])
    other = jnp.where(
        core == 0,
        jnp.concatenate([fetched, partner], axis=axis),
        jnp.concatenate([partner, fetched], axis=axis),
    )
    return in_order(part, other, axis)


def swap_half(blocks, bit, axis, axis_name, pairs):
    kept = lax.dynamic_index_in_dim(blocks, bit, axis, keepdims=False)
    away = lax.dynamic_index_in_dim(blocks, 1 - bit, axis, keepdims=False).astype(BF)
    came = lax.ppermute(away, axis_name, pairs)
    return kept, came


def add(kept, came):
    return kept.astype(F32) + came.astype(F32)


def sum_shard_rows(partial, count):
    if count != 2:
        return lax.psum_scatter(
            partial.astype(BF), "shard", scatter_dimension=0, tiled=True
        ).astype(F32)
    index = lax.axis_index("shard")
    blocks = partial.reshape((2, -1) + partial.shape[1:])
    return add(*swap_half(blocks, index, 0, "shard", [(0, 1), (1, 0)]))


def reduce_rows(partial, count, ways_c, gates):
    if count != 2 or ways_c != 4:
        return lax.psum_scatter(partial, ("shard", "context"), scatter_dimension=0, tiled=True)
    context = lax.axis_index("context")
    core, chip = lax.rem(context, 2), lax.div(context, 2)
    rows, columns = partial.shape
    blocks = partial.reshape(2, 2, 2, rows // 8, columns)
    kept, came = swap_half(blocks, core, 2, "context", [(i, i ^ 1) for i in range(4)])
    blocks = add(kept, after(came, gates[0])).astype(BF)
    kept, came = swap_half(blocks, chip, 1, "context", [(i, i ^ 2) for i in range(4)])
    blocks = add(kept, after(came, gates[1])).astype(BF)
    kept, came = swap_half(blocks, lax.axis_index("shard"), 0, "shard", [(0, 1), (1, 0)])
    return add(kept, after(came, gates[2])).astype(BF)


def send_rows(part, ways_c):
    if ways_c != 4:
        return None
    return lax.ppermute(part, "context", [(i, i ^ 2) for i in range(4)])


def gather_rows(part, sent, ways_c):
    if ways_c != 4:
        return lax.all_gather(part, "context", axis=0, tiled=True)
    context = lax.axis_index("context")
    core, chip = lax.rem(context, 2), lax.div(context, 2)
    both = jnp.where(chip == 0, jnp.stack([part, sent]), jnp.stack([sent, part]))
    came = lax.ppermute(both, "context", [(i, i ^ 1) for i in range(4)])
    all_rows = jnp.where(
        core == 0, jnp.stack([both, came], axis=1), jnp.stack([came, both], axis=1)
    )
    return all_rows.reshape((4 * part.shape[0],) + part.shape[1:])


def rotate(blocks, ways, gate):
    index = lax.axis_index("tensor")
    shares = [lax.dynamic_index_in_dim(blocks, index, 0, keepdims=False)]
    for turn in range(1, ways):
        target = lax.rem(index + turn, ways)
        away = lax.dynamic_index_in_dim(blocks, target, 0, keepdims=False)
        away = after(away, gate)
        shares.append(lax.ppermute(away, "tensor", [(i, (i + turn) % ways) for i in range(ways)]))
    return shares


def gather_tensor(part, ways, gate):
    index = lax.axis_index("tensor")
    parts = [part] + [
        after(lax.ppermute(part, "tensor", [(i, (i + turn) % ways) for i in range(ways)]), gate)
        for turn in range(1, ways)
    ]
    parts = jnp.stack(parts)
    return jnp.concatenate(
        [
            lax.dynamic_index_in_dim(parts, lax.rem(index + ways - i, ways), 0, keepdims=False)
            for i in range(ways)
        ]
    )


def total(shares):
    return sum(share.astype(F32) for share in shares)


def after(value, *others):
    return lax.optimization_barrier((value,) + others)[0]


def pick_half(pair, high, scale=1.0):
    first = lax.broadcasted_iota(jnp.int32, pair.shape, 1) < HEAD_DIM
    values = pair.astype(F32) * scale
    return (jnp.where(first, 0.0, values) if high else jnp.where(first, values, 0.0)).astype(BF)


def lane_ids(count):
    return lax.broadcasted_iota(jnp.int32, (1, count), 1)


def band(shape, low, high, first_key):
    key = first_key + lax.broadcasted_iota(jnp.int32, shape, 0)
    return (key >= low) & (key <= high)


def forward_kernel(
    own, seq_own, nat, tr, packed, out_nat, lse, out_last, lse_last, start, start_own, end_own, meta,
    q_pad,
):
    rows = nat.shape[0]
    blocks = rows // TILE
    width = out_last.shape[0]
    scale = 1.0 / math.sqrt(HEAD_DIM)

    seq = tr[256:272, :].astype(F32)[0:1, :]
    mine = seq_own[...]
    begin = jnp.zeros_like(seq)
    begin_own = jnp.zeros_like(mine)
    finish_own = jnp.full_like(mine, float(rows))
    for number in range(1, SEQS):
        before = jnp.sum((seq < number).astype(F32), axis=1, keepdims=True)
        begin = jnp.where(seq >= number, before, begin)
        begin_own = jnp.where(mine >= number, before, begin_own)
        finish_own = jnp.where(mine == number - 1, before, finish_own)
    start[...] = begin.astype(jnp.int32)
    start_own[...] = begin_own.astype(jnp.int32)
    end_own[...] = finish_own.astype(jnp.int32)
    base = pl.multiple_of(own[0], 16)
    meta[2 * blocks] = jnp.min(begin_own).astype(jnp.int32) // TILE
    meta[2 * blocks + 1] = (base + width - 1) // TILE + 1
    meta[2 * blocks + 2] = base // width
    meta[2 * blocks + 3] = (jnp.max(finish_own).astype(jnp.int32) + width - 1) // width

    def step(queries, limits, v_row, low_tile, carry):
        top, total, acc = carry
        places, scores = [], []
        for tile in (low_tile, low_tile + 1):
            at = pl.multiple_of(jnp.clip(tile, 0, blocks - 1) * TILE, TILE)
            score = contract(nat[pl.ds(at, TILE), 128:256], queries, 1, 1)
            if limits is not None:
                score = jnp.where(band(score.shape, *limits, tile * TILE), score, NEG)
            places.append(at)
            scores.append(score)
        now = jnp.maximum(top, jnp.max(jnp.maximum(*scores), axis=0, keepdims=True))
        fade = jnp.exp(top - now)
        total, acc = total * fade, acc * fade
        for at, score in zip(places, scores):
            shares = jnp.exp(score - now)
            total = total + jnp.sum(shares, axis=0, keepdims=True)
            values = tr[v_row : v_row + HEAD_DIM, pl.ds(at, TILE)]
            acc = acc + contract(values, shares.astype(BF), 1, 0)
        return now, total, acc

    empty = (
        jnp.full((1, TILE), NEG, F32),
        jnp.zeros((1, TILE), F32),
        jnp.zeros((HEAD_DIM, TILE), F32),
    )

    def one_block(qb, unused):
        at = pl.multiple_of(qb * TILE, TILE)
        queries = pick_half(nat[pl.ds(at, TILE), 0:128], False, scale)
        low = start[:, pl.ds(at, TILE)]
        near = low.astype(F32)
        first = jnp.min(near).astype(jnp.int32) // TILE
        full = (jnp.max(near).astype(jnp.int32) + TILE - 1) // TILE
        plain = jnp.maximum(qb - 1 - full, 0) // 2
        every = (jnp.maximum(qb - 1 - first, 0) + 1) // 2
        meta[qb] = plain
        meta[blocks + qb] = every
        limits = (low, at + lane_ids(TILE))
        carry = step(queries, limits, 128, qb - 1, empty)
        carry = lax.fori_loop(
            0, plain, lambda j, c: step(queries, None, 128, qb - 3 - 2 * j, c), carry
        )
        carry = lax.fori_loop(
            plain, every, lambda j, c: step(queries, limits, 128, qb - 3 - 2 * j, c), carry
        )
        top, total, acc = carry
        lse[:, pl.ds(at, TILE)] = top + jnp.log(total)
        out_nat[pl.ds(at, TILE), :] = (acc / total).T
        return unused

    lax.fori_loop(0, blocks, one_block, 0)

    q_pad[...] = jnp.zeros_like(q_pad)
    q_pad[0:width, :] = pick_half(nat[pl.ds(base, width), 0:128], True, scale)
    limits = (start_own[...], base + lane_ids(TILE))
    begin_tile, end_tile = meta[2 * blocks], meta[2 * blocks + 1]
    top, total, acc = lax.fori_loop(
        0,
        (end_tile - begin_tile + 1) // 2,
        lambda j, c: step(q_pad[...], limits, 192, begin_tile + 2 * j, c),
        empty,
    )
    lse_last[...] = top + jnp.log(total)
    out_last[...] = (acc / total).T[0:width, :]

    half = width // 2
    for dest in range(rows // width):
        first = out_nat[dest * width : dest * width + half, :]
        second = out_nat[dest * width + half : (dest + 1) * width, :]
        packed[dest] = jnp.concatenate([first, second], axis=1).astype(BF)


def backward_last_kernel(
    own, meta, start_own, end_own, nat, tr, came, lse_own, delta_own, last_qk, last_v,
    q_rows, o_rows, pad_q, pad_o,
):
    rows = nat.shape[0]
    blocks = rows // TILE
    width = last_qk.shape[0]
    scale = 1.0 / math.sqrt(HEAD_DIM)
    base = pl.multiple_of(own[0], 16)

    q_rows[0:rows, :] = (nat[:, 0:128].astype(F32) * scale).astype(BF)
    q_rows[rows:, :] = jnp.zeros((q_rows.shape[0] - rows, 2 * HEAD_DIM), BF)
    for source in range(rows // width):
        o_rows[source * width : (source + 1) * width, :] = came[source, 0:width, :]
    o_rows[rows:, :] = jnp.zeros((o_rows.shape[0] - rows, 2 * HEAD_DIM), BF)

    pad_q[...] = jnp.zeros_like(pad_q)
    pad_o[...] = jnp.zeros_like(pad_o)
    pad_q[0:width, :] = pick_half(nat[pl.ds(base, width), 0:128], True, scale)
    pad_o[0:width, :] = pick_half(o_rows[pl.ds(base, width), :], True)
    limits = (start_own[...], base + lane_ids(TILE))

    begin_tile, end_tile = meta[2 * blocks], meta[2 * blocks + 1]

    def query_step(j, d_query):
        for tile in (begin_tile + 2 * j, begin_tile + 2 * j + 1):
            at = pl.multiple_of(jnp.minimum(tile, blocks - 1) * TILE, TILE)
            scores = contract(nat[pl.ds(at, TILE), 128:256], pad_q[...], 1, 1)
            scores = jnp.where(band(scores.shape, *limits, tile * TILE), scores, NEG)
            shares = jnp.exp(scores - lse_own[...])
            d_shares = contract(nat[pl.ds(at, TILE), 256:384], pad_o[...], 1, 1)
            d_scores = (shares * (d_shares - delta_own[...])).astype(BF)
            keys_t = tr[HEAD_DIM : 2 * HEAD_DIM, pl.ds(at, TILE)]
            d_query = d_query + contract(keys_t, d_scores, 1, 0)
        return d_query

    d_query = lax.fori_loop(
        0, (end_tile - begin_tile + 1) // 2, query_step, jnp.zeros((HEAD_DIM, TILE), F32)
    )
    last_qk[:, 0:HEAD_DIM] = (d_query.T[0:width, :] * scale).astype(BF)

    keys = pick_half(nat[pl.ds(base, width), 128:256], True)
    values = pick_half(nat[pl.ds(base, width), 256:384], True)
    key = base + lax.broadcasted_iota(jnp.int32, (width, TILE), 0)
    finish = jnp.broadcast_to(end_own[...].astype(F32), (128, TILE)).T[0:width, 0:1]
    finish = finish.astype(jnp.int32)
    lane = lane_ids(TILE)

    ways = rows // width

    def key_step(j, carry):
        d_key, d_value = carry
        for turn in range(2):
            query_source = begin_source + 2 * j + turn
            source = jnp.minimum(query_source, ways - 1)
            at = pl.multiple_of(source * width, 16)
            queries = q_rows[pl.ds(at, TILE), :]
            grads = o_rows[pl.ds(at, TILE), :]
            facts = came[source, width : width + 16, :].astype(F32)
            log_total = jnp.concatenate([facts[0:1] + facts[2:3], facts[1:2] + facts[3:4]], axis=1)
            delta = jnp.concatenate([facts[4:5] + facts[6:7], facts[5:6] + facts[7:8]], axis=1)
            query = query_source * width + lane
            keep = (key <= query) & (query < finish) & (lane < width)
            scores = jnp.where(keep, contract(keys, queries, 1, 1), NEG)
            shares = jnp.exp(scores - log_total)
            d_shares = contract(values, grads, 1, 1)
            d_scores = (shares * (d_shares - delta)).astype(BF)
            d_key = d_key + contract(d_scores, queries, 1, 0)
            d_value = d_value + contract(shares.astype(BF), grads, 1, 0)
        return d_key, d_value

    zero = jnp.zeros((width, 2 * HEAD_DIM), F32)
    begin_source, end_source = meta[2 * blocks + 2], meta[2 * blocks + 3]
    d_key, d_value = lax.fori_loop(
        0, (end_source - begin_source + 1) // 2, key_step, (zero, zero)
    )
    last_qk[:, HEAD_DIM:] = d_key[:, HEAD_DIM:].astype(BF)
    last_v[...] = d_value[:, HEAD_DIM:].astype(BF)


def backward_kernel(
    meta, start, nat, tr, came, out_nat, lse, packed, d_qk, d_v, o_rows, q_rows, acc_k, acc_v
):
    rows = nat.shape[0]
    blocks = rows // TILE
    width = rows // packed.shape[0]
    scale = 1.0 / math.sqrt(HEAD_DIM)

    q_rows[...] = (nat[:, 0:128].astype(F32) * scale).astype(BF)
    for source in range(rows // width):
        o_rows[source * width : (source + 1) * width, :] = came[source, 0:width, :]
    acc_k[...] = jnp.zeros_like(acc_k)
    acc_v[...] = jnp.zeros_like(acc_v)

    def one_block(qb, unused):
        at_q = pl.multiple_of(qb * TILE, TILE)
        pair = q_rows[pl.ds(at_q, TILE), :]
        queries = pick_half(pair, False)
        grads = o_rows[pl.ds(at_q, TILE), :]
        product = grads[:, 0:HEAD_DIM].astype(F32) * out_nat[pl.ds(at_q, TILE), :]
        delta = jnp.sum(product.T, axis=0, keepdims=True)
        grads_low = pick_half(grads, False)
        log_total = lse[:, pl.ds(at_q, TILE)]
        limits = (start[:, pl.ds(at_q, TILE)], at_q + lane_ids(TILE))

        def step(masked, low_tile, d_query):
            tiles = (low_tile, low_tile + 1)
            places = [pl.multiple_of(jnp.maximum(tile, 0) * TILE, TILE) for tile in tiles]
            scores = [contract(nat[pl.ds(at, TILE), 128:256], queries, 1, 1) for at in places]
            d_shares = [contract(nat[pl.ds(at, TILE), 256:384], grads_low, 1, 1) for at in places]
            if masked:
                scores = [
                    jnp.where(band(score.shape, *limits, tile * TILE), score, NEG)
                    for score, tile in zip(scores, tiles)
                ]
            shares = [jnp.exp(score - log_total) for score in scores]
            d_scores = [
                (share * (d_share - delta)).astype(BF) for share, d_share in zip(shares, d_shares)
            ]
            added_v = [contract(share.astype(BF), grads, 1, 0) for share in shares]
            added_k = [contract(d_score, pair, 1, 0) for d_score in d_scores]
            for at, d_score in zip(places, d_scores):
                d_query = d_query + contract(tr[0:HEAD_DIM, pl.ds(at, TILE)], d_score, 1, 0)
            for at, value, key in zip(places, added_v, added_k):
                acc_v[pl.ds(at, TILE), :] += value
                acc_k[pl.ds(at, TILE), :] += key
            return d_query

        plain, every = meta[qb], meta[blocks + qb]
        d_query = step(True, qb - 1, jnp.zeros((HEAD_DIM, TILE), F32))
        d_query = lax.fori_loop(0, plain, lambda j, c: step(False, qb - 3 - 2 * j, c), d_query)
        d_query = lax.fori_loop(plain, every, lambda j, c: step(True, qb - 3 - 2 * j, c), d_query)
        d_qk[pl.ds(at_q, TILE), 0:HEAD_DIM] = (d_query.T * scale).astype(BF)
        return unused

    lax.fori_loop(0, blocks, one_block, 0)
    d_qk[:, HEAD_DIM:] = acc_k[:, 0:HEAD_DIM].astype(BF)
    d_v[...] = acc_v[:, 0:HEAD_DIM].astype(BF)
    half = width // 2
    for dest in range(rows // width):
        low_rows = slice(dest * width, dest * width + half)
        high_rows = slice(dest * width + half, (dest + 1) * width)
        packed[dest, 0:width, :] = d_qk[dest * width : (dest + 1) * width, :]
        packed[dest, width:, :] = jnp.concatenate([d_v[low_rows, :], d_v[high_rows, :]], axis=1)


def kernel_call(kernel, scalars, operands, outs, scratch, work, smem_out=None):
    vmem = pl.BlockSpec(memory_space=pltpu.VMEM)
    smem = pl.BlockSpec(memory_space=pltpu.SMEM)
    out_shape = [jax.ShapeDtypeStruct(shape, kind) for shape, kind in outs]
    out_specs = [vmem] * len(outs)
    if smem_out is not None:
        out_shape.append(jax.ShapeDtypeStruct((smem_out,), jnp.int32))
        out_specs.append(smem)
    return pl.pallas_call(
        kernel,
        out_shape=tuple(out_shape),
        in_specs=[smem] * len(scalars) + [vmem] * len(operands),
        out_specs=tuple(out_specs),
        scratch_shapes=[pltpu.VMEM(shape, kind) for shape, kind in scratch],
        cost_estimate=pl.CostEstimate(flops=work, bytes_accessed=8 << 20, transcendentals=0),
    )(*scalars, *operands)


def attend_forward(own, seq_own, nat, tr, width):
    rows = nat.shape[0]
    pair = 2 * HEAD_DIM
    return kernel_call(
        forward_kernel,
        (own,),
        (seq_own, nat, tr),
        [
            ((rows // width, width // 2, pair), BF),
            ((rows, HEAD_DIM), F32),
            ((1, rows), F32),
            ((width, HEAD_DIM), F32),
            ((1, TILE), F32),
            ((1, rows), jnp.int32),
            ((1, TILE), jnp.int32),
            ((1, TILE), jnp.int32),
        ],
        [((TILE, pair), BF)],
        16 * rows * rows * HEAD_DIM,
        2 * (rows // TILE) + 4,
    )


def attend_backward_last(own, meta, start_own, end_own, nat, tr, came, lse_own, delta_own, width):
    rows = nat.shape[0]
    pair = 2 * HEAD_DIM
    return kernel_call(
        backward_last_kernel,
        (own, meta),
        (start_own, end_own, nat, tr, came, lse_own, delta_own),
        [((width, pair), BF), ((width, HEAD_DIM), BF)],
        [((rows + TILE - width, pair), BF)] * 2 + [((TILE, pair), BF)] * 2,
        4 * rows * rows * HEAD_DIM,
    )


def attend_backward(meta, start, nat, tr, came, out_nat, lse, width):
    rows = nat.shape[0]
    pair = 2 * HEAD_DIM
    return kernel_call(
        backward_kernel,
        (meta,),
        (start, nat, tr, came, out_nat, lse),
        [
            ((rows // width, width + width // 2, pair), BF),
            ((rows, pair), BF),
            ((rows, HEAD_DIM), BF),
        ],
        [((rows, pair), BF)] * 2 + [((rows, pair), F32)] * 2,
        40 * rows * rows * HEAD_DIM,
    )


def join_kernel(pieces, shared, weights, facts, joined, dots, dots_bias):
    heads = pieces.shape[0]
    running = [jnp.zeros((joined.shape[0], 2 * HEAD_DIM), F32)] * 2
    rest = [0.0, 0.0]
    units = 3 * (heads + 1)

    def unit(index):
        part, head = divmod(index, heads + 1)
        columns = slice(part * HEAD_DIM, (part + 1) * HEAD_DIM)
        return shared[:, columns] if head == heads else pieces[head, :, columns]

    facts_of = [facts[head].astype(F32) for head in range(heads)]
    sums = [fact[0:1, :] for fact in facts_of] + [sum(fact[1:2, :] for fact in facts_of)]

    def unit_sum(index):
        part, head = divmod(index, heads + 1)
        return sums[head][:, part * HEAD_DIM : (part + 1) * HEAD_DIM]

    for block in range((units + 1) // 2):
        paired = 2 * block + 1 < units
        if paired:
            values = jnp.concatenate([unit(2 * block), unit(2 * block + 1)], axis=1)
        else:
            values = unit(2 * block)
        at = slice(2 * block * HEAD_DIM, 2 * block * HEAD_DIM + values.shape[1])
        values = values.astype(F32)
        joined[:, at] = values
        weight = weights[:, at].astype(F32)
        row = [unit_sum(2 * block + i) for i in range(1 + paired)]
        products = [values * weight, weight * jnp.concatenate(row, axis=1)]
        if paired:
            running = [so_far + product for so_far, product in zip(running, products)]
        else:
            rest = [jnp.sum(product, axis=1, keepdims=True) for product in products]
    dots[...] = jnp.sum(running[0], axis=1, keepdims=True) + rest[0]
    dots_bias[...] = jnp.sum(running[1], axis=1, keepdims=True) + rest[1]


def join_heads(pieces, shared, weights):
    heads, _, columns = pieces.shape
    rows = weights.shape[0]
    step = 272 if rows % 272 == 0 else rows
    return pl.pallas_call(
        join_kernel,
        grid=(rows // step,),
        out_shape=(
            jax.ShapeDtypeStruct(weights.shape, F32),
            jax.ShapeDtypeStruct((rows, 1), F32),
            jax.ShapeDtypeStruct((rows, 1), F32),
        ),
        in_specs=[
            pl.BlockSpec((heads, step, columns), lambda i: (0, i, 0)),
            pl.BlockSpec((step, shared.shape[1]), lambda i: (i, 0)),
            pl.BlockSpec((step, weights.shape[1]), lambda i: (i, 0)),
            pl.BlockSpec((heads, 8, columns), lambda i: (0, pieces.shape[1] // 8 - 1, 0)),
        ],
        out_specs=(
            pl.BlockSpec((step, weights.shape[1]), lambda i: (i, 0)),
            pl.BlockSpec((step, 1), lambda i: (i, 0)),
            pl.BlockSpec((step, 1), lambda i: (i, 0)),
        ),
        cost_estimate=pl.CostEstimate(flops=1 << 20, bytes_accessed=14 << 20, transcendentals=0),
        name="join_heads",
    )(pieces, shared, weights, pieces)


def gelu_pair(pre):
    factor = math.sqrt(2.0 / math.pi)
    square = pre * pre
    bend = jnp.tanh(factor * (pre + 0.044715 * pre * square))
    value = 0.5 * pre * (1.0 + bend)
    slope = 0.5 * (1.0 + bend) + 0.5 * pre * (1.0 - bend * bend) * factor * (
        1.0 + 3.0 * 0.044715 * square
    )
    return value, slope


def feed_kernel(rows, d_hidden, up, hidden, d_pre, partial):
    value, slope = gelu_pair(jnp.dot(rows[...], up[...], preferred_element_type=F32))
    hidden[...] = value.astype(BF)
    grads = (d_hidden[...] * slope).astype(BF)
    d_pre[...] = grads
    partial[...] = contract(grads, up[...], 1, 1).astype(BF)


def turned_kernel(left, right, out):
    out[...] = contract(left[...], right[...], 1, 1).astype(BF)


def row_blocks(kernel, by_rows, whole, outs):
    count = by_rows[0].shape[0]
    step = count // 2

    def block(columns):
        return pl.BlockSpec((step, columns), lambda i: (i, 0))

    return pl.pallas_call(
        kernel,
        grid=(count // step,),
        out_shape=tuple(jax.ShapeDtypeStruct((count, columns), BF) for columns in outs),
        in_specs=[block(part.shape[1]) for part in by_rows]
        + [pl.BlockSpec(whole.shape, lambda i: (0, 0), pipeline_mode=pl.Buffered(1))],
        out_specs=tuple(block(columns) for columns in outs),
        cost_estimate=pl.CostEstimate(
            flops=2 * count * whole.size, bytes_accessed=8 << 20, transcendentals=0
        ),
    )(*by_rows, whole)


def split_two(values):
    high = values.astype(BF)
    low = (values - high.astype(F32)).astype(BF)
    return [high, low]


def round_up(value, step):
    return (value + step - 1) // step * step


def sum_tensor(partial, ways):
    rows = partial.shape[0] // ways
    got = lax.all_to_all(
        partial.astype(BF).reshape(ways, rows, partial.shape[1]), "tensor", 0, 0, tiled=True
    )
    return jnp.sum(got.astype(F32), axis=0)


def head_columns(matrix, head, width):
    return [
        lax.dynamic_slice_in_dim(matrix, part * width + head * HEAD_DIM, HEAD_DIM, 1)
        for part in range(3)
    ]


def shards(
    tokens, segments, w_qkv, w_out, ln1_gain, ln1_bias, ln2_gain, ln2_bias, w_up, w_down, out_grad
):
    rows, width = tokens.shape
    count = lax.axis_size("shard")
    ways_c = lax.axis_size("context")
    ways_t = lax.axis_size("tensor")
    ways = ways_c * ways_t
    part_rows = w_qkv.shape[0]
    device = lax.axis_index(GROUP)
    shared = HEADS - 1
    padded = round_up(width, 128)
    columns = 3 * HEAD_DIM

    vectors = gather_small(
        jnp.stack([ln1_gain, ln1_bias, ln2_gain, ln2_bias]), count, 1
    ).astype(F32)
    gain_one, bias_one, gain_two, bias_two = [vectors[i : i + 1] for i in range(4)]

    inputs = tokens.astype(F32)
    unit_one, inverse_one = norm_stats(inputs)
    low_one = (unit_one * gain_one + bias_one).astype(BF)
    seq_row = segments[0]
    wide_one = jnp.concatenate(
        [low_one, seq_row[:, None].astype(BF), jnp.zeros((rows, padded - width - 1), BF)], axis=1
    )
    rows_one = lax.all_gather(wide_one, GROUP, axis=0, tiled=True)

    mine = head_columns(w_qkv, device, width)
    last = [
        w_qkv[:, part * width + shared * HEAD_DIM : part * width + (shared + 1) * HEAD_DIM]
        for part in range(3)
    ]
    head_w = gather_small(
        jnp.concatenate([mine[0], last[0], mine[1], last[1], mine[2], last[2]], axis=1),
        count,
        0,
    )
    head_w = jnp.pad(head_w, ((0, padded - width), (0, 0)))
    mark = (jnp.arange(padded)[:, None] == width) & (jnp.arange(16)[None] == 0)
    turn_w = jnp.concatenate([head_w[:, 2 * HEAD_DIM :], mark.astype(BF)], axis=1)
    out_full = gather_large(w_out, count, 0)
    up_full = gather_large(w_up, count, 0)
    down_turned = gather_large(w_down.T, count, 0)
    qkv_full = gather_large(w_qkv, count, 0)
    grads_all = lax.all_gather(out_grad, "tensor", axis=0, tiled=True)
    split = ways * HEAD_DIM
    out_wide = jnp.concatenate(
        [
            out_full[:split].reshape(ways, HEAD_DIM, width),
            jnp.broadcast_to(out_full[None, split:], (ways, HEAD_DIM, width)),
        ],
        axis=1,
    ).reshape(2 * split, width)

    own = (device * rows).reshape(1).astype(jnp.int32)
    seq_own = jnp.concatenate(
        [seq_row, jnp.broadcast_to(seq_row[-1:], (TILE - rows,))]
    ).astype(F32)[None]
    nat = jnp.dot(rows_one, head_w, preferred_element_type=F32).astype(BF)
    tr = contract(turn_w, rows_one, 0, 1).astype(BF)
    packed, out_nat, lse, last_out, last_lse, start, start_own, end_own, meta = attend_forward(
        own, seq_own, nat, tr, rows
    )
    got = lax.all_to_all(packed, GROUP, 0, 0, tiled=True)
    half = rows // 2
    got = got.reshape(ways, half, 2, HEAD_DIM).transpose(2, 1, 0, 3).reshape(rows, split)
    attended = jnp.concatenate([got, last_out.astype(BF)], axis=1)

    resid = inputs + jnp.dot(attended, out_full, preferred_element_type=F32)
    unit_two, inverse_two = norm_stats(resid)
    low_two = (unit_two * gain_two + bias_two).astype(BF)

    d_hidden = jnp.dot(grads_all, down_turned, preferred_element_type=F32)
    rows_two = lax.all_gather(low_two, "tensor", axis=0, tiled=True)
    rows_two, d_hidden = lax.optimization_barrier((rows_two, d_hidden))
    units = up_full.shape[1]
    hidden, d_pre, partial = row_blocks(
        feed_kernel, (rows_two, d_hidden), up_full, (units, units, width)
    )
    d_normed_two = sum_tensor(partial, ways_t)

    grad_up = contract(rows_two, d_pre, 0, 0).astype(BF)
    grad_down = contract(grads_all, hidden, 0, 0).astype(BF)
    (mixed,) = row_blocks(turned_kernel, (hidden,), down_turned, (width,))

    grad_in = out_grad.astype(F32)
    d_resid = grad_in + norm_back(d_normed_two, unit_two, inverse_two, gain_two)
    d_branch = d_resid.astype(BF)

    d_wide = contract(d_branch, out_wide, 1, 1).astype(BF)
    last_grad = d_wide[:, HEAD_DIM : 2 * HEAD_DIM]
    last_delta = jnp.sum(last_grad.astype(F32) * last_out, axis=1)
    pieces = split_two(last_lse[0, :rows]) + split_two(last_delta)
    extra = jnp.pad(jnp.stack(pieces), ((0, 0), (0, TILE - rows))).reshape(8, 128)
    extra = jnp.pad(extra, ((0, 8), (0, 0)))
    payload = jnp.concatenate(
        [
            d_wide.reshape(rows, ways, 2 * HEAD_DIM).transpose(1, 0, 2),
            jnp.broadcast_to(extra[None], (ways,) + extra.shape),
        ],
        axis=1,
    )
    came = lax.all_to_all(payload, GROUP, 0, 0, tiled=True)
    mixed = rotate(mixed.reshape(ways_t, rows, width), ways_t, came)
    came_heads = came
    delta_own = jnp.pad(last_delta, (0, TILE - rows))[None]

    late_branch = after(d_branch, payload)

    grad_out_w = jnp.concatenate(
        [
            contract(attended, late_branch, 0, 0).astype(BF),
            jnp.sum(d_normed_two * unit_two, axis=0)[:, None].astype(BF),
            jnp.sum(d_normed_two, axis=0)[:, None].astype(BF),
            jnp.zeros((width, padded - width - 2), BF),
        ],
        axis=1,
    )
    last_qk, last_v = attend_backward_last(
        own, meta, start_own, end_own, nat, tr, came, last_lse, delta_own, rows
    )
    last_all = jnp.concatenate([last_qk, last_v], axis=1)
    chunk = padded // ways
    grad_last = contract(wide_one, last_all, 0, 0).astype(BF)
    grad_last = lax.all_to_all(
        grad_last.reshape(ways, chunk, columns), GROUP, 0, 0, tiled=True
    )

    packed, d_qk, d_v = attend_backward(meta, start, nat, tr, came, out_nat, lse, rows)
    came = lax.all_to_all(packed, GROUP, 0, 0, tiled=True)
    came_rows = came
    grad_last = jnp.sum(grad_last.astype(F32), axis=0)

    d_head = jnp.concatenate([d_qk, d_v], axis=1)
    grad_mine = contract(rows_one, d_head, 0, 0)[:width]
    wide = 256
    sums = jnp.stack(
        [jnp.sum(d_head.astype(F32), axis=0), jnp.sum(last_all.astype(F32), axis=0)]
    )
    extra = jnp.concatenate([grad_last, jnp.pad(sums, ((0, 6), (0, 0)))], axis=0)
    both = jnp.concatenate(
        [
            grad_mine.reshape(count, part_rows, columns),
            jnp.broadcast_to(extra[None], (count,) + extra.shape),
        ],
        axis=1,
    )
    both = jnp.pad(both, ((0, 0), (0, 0), (0, wide - columns)))
    both = sum_shard_rows(both.reshape(count * (part_rows + chunk + 8), wide), count)
    payload = both.astype(BF)

    pair = reduce_rows(
        jnp.concatenate([grad_up, grad_down], axis=1), count, ways_c, (grad_up, d_qk, came_rows)
    )
    grad_out_w = reduce_rows(grad_out_w, count, ways_c, (grad_out_w, came_heads, d_qk))
    piece = part_rows // ways_c
    deep = round_up(-(-piece // ways_t), 8)
    grad_out_w = jnp.pad(grad_out_w, ((0, deep * ways_t - piece), (0, 0)))
    grad_out_w = rotate(grad_out_w.reshape(ways_t, deep, padded), ways_t, last_qk)
    sent_pair = send_rows(pair, ways_c)
    grad_out_w = total([grad_out_w[0]] + [after(share, came_rows) for share in grad_out_w[1:]])
    grad_out_w = grad_out_w.astype(BF)
    pieces = lax.all_gather(payload, GROUP, axis=0, tiled=True)
    pieces = pieces.reshape((ways,) + payload.shape)
    shared_w = pieces[:, part_rows : part_rows + chunk, :columns].reshape(ways * chunk, columns)
    shared_w = lax.dynamic_slice_in_dim(
        shared_w, lax.axis_index("shard") * part_rows, part_rows, 0
    )
    grad_qkv, dots, dots_bias = join_heads(pieces, shared_w, w_qkv)
    grad_bias_one = dots_bias[:, 0]
    grad_gain_one = (dots[:, 0] - ln1_bias.astype(F32) * grad_bias_one) / ln1_gain.astype(F32)
    result = (resid + total([mixed[0]] + [after(share, payload) for share in mixed[1:]])).astype(BF)

    came_qk = came[:, :rows].reshape(ways, rows, 2, HEAD_DIM).transpose(1, 2, 0, 3)
    came_qk = came_qk.reshape(rows, 2, split)
    came_v = came[:, rows:].reshape(ways, half, 2, HEAD_DIM).transpose(2, 1, 0, 3)
    came_v = came_v.reshape(rows, 1, split)
    came = jnp.concatenate([came_qk, came_v], axis=1)
    d_projected = jnp.concatenate(
        [came, last_all.reshape(rows, 3, HEAD_DIM)], axis=2
    ).reshape(rows, 3 * width)
    d_normed_one = contract(d_projected, qkv_full, 1, 1)

    grad_out_w = gather_tensor(grad_out_w, ways_t, d_normed_one)[:piece]
    sent = send_rows(grad_out_w, ways_c)
    sent_pair = None if sent_pair is None else after(sent_pair, d_normed_one)
    pair = gather_rows(pair, sent_pair, ways_c).astype(F32)
    grad_up = pair[:, : up_full.shape[1]]
    grad_down = pair[:, up_full.shape[1] :].T
    grad_out_w = gather_rows(grad_out_w, sent, ways_c).astype(F32)

    input_grad = (d_resid + norm_back(d_normed_one, unit_one, inverse_one, gain_one)).astype(BF)
    return (
        result,
        input_grad,
        grad_qkv,
        grad_out_w[:, :width],
        grad_gain_one,
        grad_bias_one,
        grad_out_w[:, width],
        grad_out_w[:, width + 1],
        grad_up,
        grad_down,
    )


def solution(mesh):
    in_specs = (
        P(("shard", "context", "tensor"), None),
        P("shard", ("context", "tensor")),
        P("shard", None),
        P("shard", None),
        P("shard"),
        P("shard"),
        P("shard"),
        P("shard"),
        P("shard", "tensor"),
        P("tensor", "shard"),
        P(("shard", "context", "tensor"), None),
    )
    out_specs = (
        P(("shard", "context", "tensor"), None),
        P(("shard", "context", "tensor"), None),
        P("shard", None),
        P("shard", None),
        P("shard"),
        P("shard"),
        P("shard"),
        P("shard"),
        P("shard", "tensor"),
        P("tensor", "shard"),
    )
    return jax.shard_map(shards, mesh=mesh, in_specs=in_specs, out_specs=out_specs, check_vma=False)
```

```python
import math

import jax
import jax.numpy as jnp
from jax import lax
from jax.experimental import pallas as pl
from jax.experimental.pallas import tpu as pltpu
from jax.sharding import PartitionSpec as P


HEADS = 17
HEAD_DIM = 64
SEQS = 6
EPSILON = 1e-05
NEG = -1e30
GROUP = ("context", "tensor")
TILE = 256
BF = jnp.bfloat16
F32 = jnp.float32


def contract(left, right, left_dim, right_dim):
    return lax.dot_general(
        left, right, (((left_dim,), (right_dim,)), ((), ())), preferred_element_type=F32
    )


def norm_stats(values):
    average = jnp.mean(values, axis=-1, keepdims=True)
    centred = values - average
    variance = jnp.mean(centred * centred, axis=-1, keepdims=True)
    inverse = lax.rsqrt(variance + EPSILON)
    return centred * inverse, inverse


def norm_back(grad, unit, inverse, gain):
    scaled = grad * gain
    first = jnp.mean(scaled, axis=-1, keepdims=True)
    second = jnp.mean(scaled * unit, axis=-1, keepdims=True)
    return inverse * (scaled - first - unit * second)


def swap_shard(part):
    return lax.ppermute(part, "shard", [(0, 1), (1, 0)])


def in_order(mine, other, axis):
    index = lax.axis_index("shard")
    return jnp.where(
        index == 0,
        jnp.concatenate([mine, other], axis=axis),
        jnp.concatenate([other, mine], axis=axis),
    )


def gather_small(part, count, axis):
    if count != 2:
        return lax.all_gather(part, "shard", axis=axis, tiled=True)
    return in_order(part, swap_shard(part), axis)


def gather_large(part, count, axis):
    if count != 2:
        return lax.all_gather(part, "shard", axis=axis, tiled=True)
    ways = lax.axis_size("context")
    core = lax.rem(lax.axis_index("context"), 2)
    half = part.shape[axis] // 2
    mine = lax.dynamic_slice_in_dim(part, core * half, half, axis)
    fetched = swap_shard(mine)
    partner = lax.ppermute(fetched, "context", [(i, i ^ 1) for i in range(ways)])
    other = jnp.where(
        core == 0,
        jnp.concatenate([fetched, partner], axis=axis),
        jnp.concatenate([partner, fetched], axis=axis),
    )
    return in_order(part, other, axis)


def swap_half(blocks, bit, axis, axis_name, pairs):
    kept = lax.dynamic_index_in_dim(blocks, bit, axis, keepdims=False)
    away = lax.dynamic_index_in_dim(blocks, 1 - bit, axis, keepdims=False).astype(BF)
    came = lax.ppermute(away, axis_name, pairs)
    return kept, came


def add(kept, came):
    return kept.astype(F32) + came.astype(F32)


def sum_shard_rows(partial, count):
    if count != 2:
        return lax.psum_scatter(
            partial.astype(BF), "shard", scatter_dimension=0, tiled=True
        ).astype(F32)
    index = lax.axis_index("shard")
    blocks = partial.reshape((2, -1) + partial.shape[1:])
    return add(*swap_half(blocks, index, 0, "shard", [(0, 1), (1, 0)]))


def reduce_rows(partial, count, ways_c, gates):
    if count != 2 or ways_c != 4:
        return lax.psum_scatter(partial, ("shard", "context"), scatter_dimension=0, tiled=True)
    context = lax.axis_index("context")
    core, chip = lax.rem(context, 2), lax.div(context, 2)
    rows, columns = partial.shape
    blocks = partial.reshape(2, 2, 2, rows // 8, columns)
    kept, came = swap_half(blocks, core, 2, "context", [(i, i ^ 1) for i in range(4)])
    blocks = add(kept, after(came, gates[0])).astype(BF)
    kept, came = swap_half(blocks, chip, 1, "context", [(i, i ^ 2) for i in range(4)])
    blocks = add(kept, after(came, gates[1])).astype(BF)
    kept, came = swap_half(blocks, lax.axis_index("shard"), 0, "shard", [(0, 1), (1, 0)])
    return add(kept, after(came, gates[2])).astype(BF)


def send_rows(part, ways_c):
    if ways_c != 4:
        return None
    return lax.ppermute(part, "context", [(i, i ^ 2) for i in range(4)])


def gather_rows(part, sent, ways_c):
    if ways_c != 4:
        return lax.all_gather(part, "context", axis=0, tiled=True)
    context = lax.axis_index("context")
    core, chip = lax.rem(context, 2), lax.div(context, 2)
    both = jnp.where(chip == 0, jnp.stack([part, sent]), jnp.stack([sent, part]))
    came = lax.ppermute(both, "context", [(i, i ^ 1) for i in range(4)])
    all_rows = jnp.where(
        core == 0, jnp.stack([both, came], axis=1), jnp.stack([came, both], axis=1)
    )
    return all_rows.reshape((4 * part.shape[0],) + part.shape[1:])


def rotate(blocks, ways, gate):
    index = lax.axis_index("tensor")
    shares = [lax.dynamic_index_in_dim(blocks, index, 0, keepdims=False)]
    for turn in range(1, ways):
        target = lax.rem(index + turn, ways)
        away = lax.dynamic_index_in_dim(blocks, target, 0, keepdims=False)
        away = after(away, gate)
        shares.append(lax.ppermute(away, "tensor", [(i, (i + turn) % ways) for i in range(ways)]))
    return shares


def gather_tensor(part, ways, gate):
    index = lax.axis_index("tensor")
    parts = [part] + [
        after(lax.ppermute(part, "tensor", [(i, (i + turn) % ways) for i in range(ways)]), gate)
        for turn in range(1, ways)
    ]
    parts = jnp.stack(parts)
    return jnp.concatenate(
        [
            lax.dynamic_index_in_dim(parts, lax.rem(index + ways - i, ways), 0, keepdims=False)
            for i in range(ways)
        ]
    )


def total(shares):
    return sum(share.astype(F32) for share in shares)


def after(value, *others):
    return lax.optimization_barrier((value,) + others)[0]


def pick_half(pair, high, scale=1.0):
    first = lax.broadcasted_iota(jnp.int32, pair.shape, 1) < HEAD_DIM
    values = pair.astype(F32) * scale
    return (jnp.where(first, 0.0, values) if high else jnp.where(first, values, 0.0)).astype(BF)


def lane_ids(count):
    return lax.broadcasted_iota(jnp.int32, (1, count), 1)


def band(shape, low, high, first_key):
    key = first_key + lax.broadcasted_iota(jnp.int32, shape, 0)
    return (key >= low) & (key <= high)


def forward_kernel(
    own, seq_own, nat, tr, packed, out_nat, lse, out_last, lse_last, start, start_own, end_own, meta,
    q_pad,
):
    rows = nat.shape[0]
    blocks = rows // TILE
    width = out_last.shape[0]
    scale = 1.0 / math.sqrt(HEAD_DIM)

    seq = tr[256:272, :].astype(F32)[0:1, :]
    mine = seq_own[...]
    begin = jnp.zeros_like(seq)
    begin_own = jnp.zeros_like(mine)
    finish_own = jnp.full_like(mine, float(rows))
    for number in range(1, SEQS):
        before = jnp.sum((seq < number).astype(F32), axis=1, keepdims=True)
        begin = jnp.where(seq >= number, before, begin)
        begin_own = jnp.where(mine >= number, before, begin_own)
        finish_own = jnp.where(mine == number - 1, before, finish_own)
    start[...] = begin.astype(jnp.int32)
    start_own[...] = begin_own.astype(jnp.int32)
    end_own[...] = finish_own.astype(jnp.int32)
    base = pl.multiple_of(own[0], 16)
    meta[2 * blocks] = jnp.min(begin_own).astype(jnp.int32) // TILE
    meta[2 * blocks + 1] = (base + width - 1) // TILE + 1
    meta[2 * blocks + 2] = base // width
    meta[2 * blocks + 3] = (jnp.max(finish_own).astype(jnp.int32) + width - 1) // width

    def step(queries, limits, v_row, low_tile, carry):
        top, total, acc = carry
        places, scores = [], []
        for tile in (low_tile, low_tile + 1):
            at = pl.multiple_of(jnp.clip(tile, 0, blocks - 1) * TILE, TILE)
            score = contract(nat[pl.ds(at, TILE), 128:256], queries, 1, 1)
            if limits is not None:
                score = jnp.where(band(score.shape, *limits, tile * TILE), score, NEG)
            places.append(at)
            scores.append(score)
        now = jnp.maximum(top, jnp.max(jnp.maximum(*scores), axis=0, keepdims=True))
        fade = jnp.exp(top - now)
        total, acc = total * fade, acc * fade
        for at, score in zip(places, scores):
            shares = jnp.exp(score - now)
            total = total + jnp.sum(shares, axis=0, keepdims=True)
            values = tr[v_row : v_row + HEAD_DIM, pl.ds(at, TILE)]
            acc = acc + contract(values, shares.astype(BF), 1, 0)
        return now, total, acc

    empty = (
        jnp.full((1, TILE), NEG, F32),
        jnp.zeros((1, TILE), F32),
        jnp.zeros((HEAD_DIM, TILE), F32),
    )

    def one_block(qb, unused):
        at = pl.multiple_of(qb * TILE, TILE)
        queries = pick_half(nat[pl.ds(at, TILE), 0:128], False, scale)
        low = start[:, pl.ds(at, TILE)]
        near = low.astype(F32)
        first = jnp.min(near).astype(jnp.int32) // TILE
        full = (jnp.max(near).astype(jnp.int32) + TILE - 1) // TILE
        plain = jnp.maximum(qb - 1 - full, 0) // 2
        every = (jnp.maximum(qb - 1 - first, 0) + 1) // 2
        meta[qb] = plain
        meta[blocks + qb] = every
        limits = (low, at + lane_ids(TILE))
        carry = step(queries, limits, 128, qb - 1, empty)
        carry = lax.fori_loop(
            0, plain, lambda j, c: step(queries, None, 128, qb - 3 - 2 * j, c), carry
        )
        carry = lax.fori_loop(
            plain, every, lambda j, c: step(queries, limits, 128, qb - 3 - 2 * j, c), carry
        )
        top, total, acc = carry
        lse[:, pl.ds(at, TILE)] = top + jnp.log(total)
        out_nat[pl.ds(at, TILE), :] = (acc / total).T
        return unused

    lax.fori_loop(0, blocks, one_block, 0)

    q_pad[...] = jnp.zeros_like(q_pad)
    q_pad[0:width, :] = pick_half(nat[pl.ds(base, width), 0:128], True, scale)
    limits = (start_own[...], base + lane_ids(TILE))
    begin_tile, end_tile = meta[2 * blocks], meta[2 * blocks + 1]
    top, total, acc = lax.fori_loop(
        0,
        (end_tile - begin_tile + 1) // 2,
        lambda j, c: step(q_pad[...], limits, 192, begin_tile + 2 * j, c),
        empty,
    )
    lse_last[...] = top + jnp.log(total)
    out_last[...] = (acc / total).T[0:width, :]

    half = width // 2
    for dest in range(rows // width):
        first = out_nat[dest * width : dest * width + half, :]
        second = out_nat[dest * width + half : (dest + 1) * width, :]
        packed[dest] = jnp.concatenate([first, second], axis=1).astype(BF)


def backward_last_kernel(
    own, meta, start_own, end_own, nat, tr, came, lse_own, delta_own, last_qk, last_v,
    q_rows, o_rows, pad_q, pad_o,
):
    rows = nat.shape[0]
    blocks = rows // TILE
    width = last_qk.shape[0]
    scale = 1.0 / math.sqrt(HEAD_DIM)
    base = pl.multiple_of(own[0], 16)

    q_rows[0:rows, :] = (nat[:, 0:128].astype(F32) * scale).astype(BF)
    q_rows[rows:, :] = jnp.zeros((q_rows.shape[0] - rows, 2 * HEAD_DIM), BF)
    for source in range(rows // width):
        o_rows[source * width : (source + 1) * width, :] = came[source, 0:width, :]
    o_rows[rows:, :] = jnp.zeros((o_rows.shape[0] - rows, 2 * HEAD_DIM), BF)

    pad_q[...] = jnp.zeros_like(pad_q)
    pad_o[...] = jnp.zeros_like(pad_o)
    pad_q[0:width, :] = pick_half(nat[pl.ds(base, width), 0:128], True, scale)
    pad_o[0:width, :] = pick_half(o_rows[pl.ds(base, width), :], True)
    limits = (start_own[...], base + lane_ids(TILE))

    begin_tile, end_tile = meta[2 * blocks], meta[2 * blocks + 1]

    def query_step(j, d_query):
        for tile in (begin_tile + 2 * j, begin_tile + 2 * j + 1):
            at = pl.multiple_of(jnp.minimum(tile, blocks - 1) * TILE, TILE)
            scores = contract(nat[pl.ds(at, TILE), 128:256], pad_q[...], 1, 1)
            scores = jnp.where(band(scores.shape, *limits, tile * TILE), scores, NEG)
            shares = jnp.exp(scores - lse_own[...])
            d_shares = contract(nat[pl.ds(at, TILE), 256:384], pad_o[...], 1, 1)
            d_scores = (shares * (d_shares - delta_own[...])).astype(BF)
            keys_t = tr[HEAD_DIM : 2 * HEAD_DIM, pl.ds(at, TILE)]
            d_query = d_query + contract(keys_t, d_scores, 1, 0)
        return d_query

    d_query = lax.fori_loop(
        0, (end_tile - begin_tile + 1) // 2, query_step, jnp.zeros((HEAD_DIM, TILE), F32)
    )
    last_qk[:, 0:HEAD_DIM] = (d_query.T[0:width, :] * scale).astype(BF)

    keys = pick_half(nat[pl.ds(base, width), 128:256], True)
    values = pick_half(nat[pl.ds(base, width), 256:384], True)
    key = base + lax.broadcasted_iota(jnp.int32, (width, TILE), 0)
    finish = jnp.broadcast_to(end_own[...].astype(F32), (128, TILE)).T[0:width, 0:1]
    finish = finish.astype(jnp.int32)
    lane = lane_ids(TILE)

    ways = rows // width

    def key_step(j, carry):
        d_key, d_value = carry
        for turn in range(2):
            query_source = begin_source + 2 * j + turn
            source = jnp.minimum(query_source, ways - 1)
            at = pl.multiple_of(source * width, 16)
            queries = q_rows[pl.ds(at, TILE), :]
            grads = o_rows[pl.ds(at, TILE), :]
            facts = came[source, width : width + 16, :].astype(F32)
            log_total = jnp.concatenate([facts[0:1] + facts[2:3], facts[1:2] + facts[3:4]], axis=1)
            delta = jnp.concatenate([facts[4:5] + facts[6:7], facts[5:6] + facts[7:8]], axis=1)
            query = query_source * width + lane
            keep = (key <= query) & (query < finish) & (lane < width)
            scores = jnp.where(keep, contract(keys, queries, 1, 1), NEG)
            shares = jnp.exp(scores - log_total)
            d_shares = contract(values, grads, 1, 1)
            d_scores = (shares * (d_shares - delta)).astype(BF)
            d_key = d_key + contract(d_scores, queries, 1, 0)
            d_value = d_value + contract(shares.astype(BF), grads, 1, 0)
        return d_key, d_value

    zero = jnp.zeros((width, 2 * HEAD_DIM), F32)
    begin_source, end_source = meta[2 * blocks + 2], meta[2 * blocks + 3]
    d_key, d_value = lax.fori_loop(
        0, (end_source - begin_source + 1) // 2, key_step, (zero, zero)
    )
    last_qk[:, HEAD_DIM:] = d_key[:, HEAD_DIM:].astype(BF)
    last_v[...] = d_value[:, HEAD_DIM:].astype(BF)


def backward_kernel(
    meta, start, nat, tr, came, out_nat, lse, packed, d_qk, d_v, o_rows, q_rows, acc_k, acc_v
):
    rows = nat.shape[0]
    blocks = rows // TILE
    width = rows // packed.shape[0]
    scale = 1.0 / math.sqrt(HEAD_DIM)

    q_rows[...] = (nat[:, 0:128].astype(F32) * scale).astype(BF)
    for source in range(rows // width):
        o_rows[source * width : (source + 1) * width, :] = came[source, 0:width, :]
    acc_k[...] = jnp.zeros_like(acc_k)
    acc_v[...] = jnp.zeros_like(acc_v)

    def one_block(qb, unused):
        at_q = pl.multiple_of(qb * TILE, TILE)
        pair = q_rows[pl.ds(at_q, TILE), :]
        queries = pick_half(pair, False)
        grads = o_rows[pl.ds(at_q, TILE), :]
        product = grads[:, 0:HEAD_DIM].astype(F32) * out_nat[pl.ds(at_q, TILE), :]
        delta = jnp.sum(product.T, axis=0, keepdims=True)
        grads_low = pick_half(grads, False)
        log_total = lse[:, pl.ds(at_q, TILE)]
        limits = (start[:, pl.ds(at_q, TILE)], at_q + lane_ids(TILE))

        def step(masked, low_tile, d_query):
            tiles = (low_tile, low_tile + 1)
            places = [pl.multiple_of(jnp.maximum(tile, 0) * TILE, TILE) for tile in tiles]
            scores = [contract(nat[pl.ds(at, TILE), 128:256], queries, 1, 1) for at in places]
            d_shares = [contract(nat[pl.ds(at, TILE), 256:384], grads_low, 1, 1) for at in places]
            if masked:
                scores = [
                    jnp.where(band(score.shape, *limits, tile * TILE), score, NEG)
                    for score, tile in zip(scores, tiles)
                ]
            shares = [jnp.exp(score - log_total) for score in scores]
            d_scores = [
                (share * (d_share - delta)).astype(BF) for share, d_share in zip(shares, d_shares)
            ]
            added_v = [contract(share.astype(BF), grads, 1, 0) for share in shares]
            added_k = [contract(d_score, pair, 1, 0) for d_score in d_scores]
            for at, d_score in zip(places, d_scores):
                d_query = d_query + contract(tr[0:HEAD_DIM, pl.ds(at, TILE)], d_score, 1, 0)
            for at, value, key in zip(places, added_v, added_k):
                acc_v[pl.ds(at, TILE), :] += value
                acc_k[pl.ds(at, TILE), :] += key
            return d_query

        plain, every = meta[qb], meta[blocks + qb]
        d_query = step(True, qb - 1, jnp.zeros((HEAD_DIM, TILE), F32))
        d_query = lax.fori_loop(0, plain, lambda j, c: step(False, qb - 3 - 2 * j, c), d_query)
        d_query = lax.fori_loop(plain, every, lambda j, c: step(True, qb - 3 - 2 * j, c), d_query)
        d_qk[pl.ds(at_q, TILE), 0:HEAD_DIM] = (d_query.T * scale).astype(BF)
        return unused

    lax.fori_loop(0, blocks, one_block, 0)
    d_qk[:, HEAD_DIM:] = acc_k[:, 0:HEAD_DIM].astype(BF)
    d_v[...] = acc_v[:, 0:HEAD_DIM].astype(BF)
    half = width // 2
    for dest in range(rows // width):
        low_rows = slice(dest * width, dest * width + half)
        high_rows = slice(dest * width + half, (dest + 1) * width)
        packed[dest, 0:width, :] = d_qk[dest * width : (dest + 1) * width, :]
        packed[dest, width:, :] = jnp.concatenate([d_v[low_rows, :], d_v[high_rows, :]], axis=1)


def kernel_call(kernel, scalars, operands, outs, scratch, work, smem_out=None):
    vmem = pl.BlockSpec(memory_space=pltpu.VMEM)
    smem = pl.BlockSpec(memory_space=pltpu.SMEM)
    out_shape = [jax.ShapeDtypeStruct(shape, kind) for shape, kind in outs]
    out_specs = [vmem] * len(outs)
    if smem_out is not None:
        out_shape.append(jax.ShapeDtypeStruct((smem_out,), jnp.int32))
        out_specs.append(smem)
    return pl.pallas_call(
        kernel,
        out_shape=tuple(out_shape),
        in_specs=[smem] * len(scalars) + [vmem] * len(operands),
        out_specs=tuple(out_specs),
        scratch_shapes=[pltpu.VMEM(shape, kind) for shape, kind in scratch],
        cost_estimate=pl.CostEstimate(flops=work, bytes_accessed=8 << 20, transcendentals=0),
    )(*scalars, *operands)


def attend_forward(own, seq_own, nat, tr, width):
    rows = nat.shape[0]
    pair = 2 * HEAD_DIM
    return kernel_call(
        forward_kernel,
        (own,),
        (seq_own, nat, tr),
        [
            ((rows // width, width // 2, pair), BF),
            ((rows, HEAD_DIM), F32),
            ((1, rows), F32),
            ((width, HEAD_DIM), F32),
            ((1, TILE), F32),
            ((1, rows), jnp.int32),
            ((1, TILE), jnp.int32),
            ((1, TILE), jnp.int32),
        ],
        [((TILE, pair), BF)],
        16 * rows * rows * HEAD_DIM,
        2 * (rows // TILE) + 4,
    )


def attend_backward_last(own, meta, start_own, end_own, nat, tr, came, lse_own, delta_own, width):
    rows = nat.shape[0]
    pair = 2 * HEAD_DIM
    return kernel_call(
        backward_last_kernel,
        (own, meta),
        (start_own, end_own, nat, tr, came, lse_own, delta_own),
        [((width, pair), BF), ((width, HEAD_DIM), BF)],
        [((rows + TILE - width, pair), BF)] * 2 + [((TILE, pair), BF)] * 2,
        4 * rows * rows * HEAD_DIM,
    )


def attend_backward(meta, start, nat, tr, came, out_nat, lse, width):
    rows = nat.shape[0]
    pair = 2 * HEAD_DIM
    return kernel_call(
        backward_kernel,
        (meta,),
        (start, nat, tr, came, out_nat, lse),
        [
            ((rows // width, width + width // 2, pair), BF),
            ((rows, pair), BF),
            ((rows, HEAD_DIM), BF),
        ],
        [((rows, pair), BF)] * 2 + [((rows, pair), F32)] * 2,
        40 * rows * rows * HEAD_DIM,
    )


def join_kernel(pieces, shared, weights, facts, joined, dots, dots_bias):
    heads = pieces.shape[0]
    running = [jnp.zeros((joined.shape[0], 2 * HEAD_DIM), F32)] * 2
    rest = [0.0, 0.0]
    units = 3 * (heads + 1)

    def unit(index):
        part, head = divmod(index, heads + 1)
        columns = slice(part * HEAD_DIM, (part + 1) * HEAD_DIM)
        return shared[:, columns] if head == heads else pieces[head, :, columns]

    facts_of = [facts[head].astype(F32) for head in range(heads)]
    sums = [fact[0:1, :] for fact in facts_of] + [sum(fact[1:2, :] for fact in facts_of)]

    def unit_sum(index):
        part, head = divmod(index, heads + 1)
        return sums[head][:, part * HEAD_DIM : (part + 1) * HEAD_DIM]

    for block in range((units + 1) // 2):
        paired = 2 * block + 1 < units
        if paired:
            values = jnp.concatenate([unit(2 * block), unit(2 * block + 1)], axis=1)
        else:
            values = unit(2 * block)
        at = slice(2 * block * HEAD_DIM, 2 * block * HEAD_DIM + values.shape[1])
        values = values.astype(F32)
        joined[:, at] = values
        weight = weights[:, at].astype(F32)
        row = [unit_sum(2 * block + i) for i in range(1 + paired)]
        products = [values * weight, weight * jnp.concatenate(row, axis=1)]
        if paired:
            running = [so_far + product for so_far, product in zip(running, products)]
        else:
            rest = [jnp.sum(product, axis=1, keepdims=True) for product in products]
    dots[...] = jnp.sum(running[0], axis=1, keepdims=True) + rest[0]
    dots_bias[...] = jnp.sum(running[1], axis=1, keepdims=True) + rest[1]


def join_heads(pieces, shared, weights):
    heads, _, columns = pieces.shape
    rows = weights.shape[0]
    step = 272 if rows % 272 == 0 else rows
    return pl.pallas_call(
        join_kernel,
        grid=(rows // step,),
        out_shape=(
            jax.ShapeDtypeStruct(weights.shape, F32),
            jax.ShapeDtypeStruct((rows, 1), F32),
            jax.ShapeDtypeStruct((rows, 1), F32),
        ),
        in_specs=[
            pl.BlockSpec((heads, step, columns), lambda i: (0, i, 0)),
            pl.BlockSpec((step, shared.shape[1]), lambda i: (i, 0)),
            pl.BlockSpec((step, weights.shape[1]), lambda i: (i, 0)),
            pl.BlockSpec((heads, 8, columns), lambda i: (0, pieces.shape[1] // 8 - 1, 0)),
        ],
        out_specs=(
            pl.BlockSpec((step, weights.shape[1]), lambda i: (i, 0)),
            pl.BlockSpec((step, 1), lambda i: (i, 0)),
            pl.BlockSpec((step, 1), lambda i: (i, 0)),
        ),
        cost_estimate=pl.CostEstimate(flops=1 << 20, bytes_accessed=14 << 20, transcendentals=0),
        name="join_heads",
    )(pieces, shared, weights, pieces)


def gelu_pair(pre):
    factor = math.sqrt(2.0 / math.pi)
    square = pre * pre
    bend = jnp.tanh(factor * (pre + 0.044715 * pre * square))
    value = 0.5 * pre * (1.0 + bend)
    slope = 0.5 * (1.0 + bend) + 0.5 * pre * (1.0 - bend * bend) * factor * (
        1.0 + 3.0 * 0.044715 * square
    )
    return value, slope


def feed_kernel(rows, d_hidden, up, hidden, d_pre, partial):
    value, slope = gelu_pair(jnp.dot(rows[...], up[...], preferred_element_type=F32))
    hidden[...] = value.astype(BF)
    grads = (d_hidden[...] * slope).astype(BF)
    d_pre[...] = grads
    partial[...] = contract(grads, up[...], 1, 1).astype(BF)


def turned_kernel(left, right, out):
    out[...] = contract(left[...], right[...], 1, 1).astype(BF)


def row_blocks(kernel, by_rows, whole, outs):
    count = by_rows[0].shape[0]
    step = count // 2

    def block(columns):
        return pl.BlockSpec((step, columns), lambda i: (i, 0))

    return pl.pallas_call(
        kernel,
        grid=(count // step,),
        out_shape=tuple(jax.ShapeDtypeStruct((count, columns), BF) for columns in outs),
        in_specs=[block(part.shape[1]) for part in by_rows]
        + [pl.BlockSpec(whole.shape, lambda i: (0, 0), pipeline_mode=pl.Buffered(1))],
        out_specs=tuple(block(columns) for columns in outs),
        cost_estimate=pl.CostEstimate(
            flops=2 * count * whole.size, bytes_accessed=8 << 20, transcendentals=0
        ),
    )(*by_rows, whole)


def split_two(values):
    high = values.astype(BF)
    low = (values - high.astype(F32)).astype(BF)
    return [high, low]


def round_up(value, step):
    return (value + step - 1) // step * step


def sum_tensor(partial, ways):
    rows = partial.shape[0] // ways
    got = lax.all_to_all(
        partial.astype(BF).reshape(ways, rows, partial.shape[1]), "tensor", 0, 0, tiled=True
    )
    return jnp.sum(got.astype(F32), axis=0)


def head_columns(matrix, head, width):
    return [
        lax.dynamic_slice_in_dim(matrix, part * width + head * HEAD_DIM, HEAD_DIM, 1)
        for part in range(3)
    ]


def shards(
    tokens, segments, w_qkv, w_out, ln1_gain, ln1_bias, ln2_gain, ln2_bias, w_up, w_down, out_grad
):
    rows, width = tokens.shape
    count = lax.axis_size("shard")
    ways_c = lax.axis_size("context")
    ways_t = lax.axis_size("tensor")
    ways = ways_c * ways_t
    part_rows = w_qkv.shape[0]
    device = lax.axis_index(GROUP)
    shared = HEADS - 1
    padded = round_up(width, 128)
    columns = 3 * HEAD_DIM

    vectors = gather_small(
        jnp.stack([ln1_gain, ln1_bias, ln2_gain, ln2_bias]), count, 1
    ).astype(F32)
    gain_one, bias_one, gain_two, bias_two = [vectors[i : i + 1] for i in range(4)]

    inputs = tokens.astype(F32)
    unit_one, inverse_one = norm_stats(inputs)
    low_one = (unit_one * gain_one + bias_one).astype(BF)
    seq_row = segments[0]
    wide_one = jnp.concatenate(
        [low_one, seq_row[:, None].astype(BF), jnp.zeros((rows, padded - width - 1), BF)], axis=1
    )
    rows_one = lax.all_gather(wide_one, GROUP, axis=0, tiled=True)

    mine = head_columns(w_qkv, device, width)
    last = [
        w_qkv[:, part * width + shared * HEAD_DIM : part * width + (shared + 1) * HEAD_DIM]
        for part in range(3)
    ]
    head_w = gather_small(
        jnp.concatenate([mine[0], last[0], mine[1], last[1], mine[2], last[2]], axis=1),
        count,
        0,
    )
    head_w = jnp.pad(head_w, ((0, padded - width), (0, 0)))
    mark = (jnp.arange(padded)[:, None] == width) & (jnp.arange(16)[None] == 0)
    turn_w = jnp.concatenate([head_w[:, 2 * HEAD_DIM :], mark.astype(BF)], axis=1)
    out_full = gather_large(w_out, count, 0)
    up_full = gather_large(w_up, count, 0)
    down_turned = gather_large(w_down.T, count, 0)
    qkv_full = gather_large(w_qkv, count, 0)
    grads_all = lax.all_gather(out_grad, "tensor", axis=0, tiled=True)
    split = ways * HEAD_DIM
    out_wide = jnp.concatenate(
        [
            out_full[:split].reshape(ways, HEAD_DIM, width),
            jnp.broadcast_to(out_full[None, split:], (ways, HEAD_DIM, width)),
        ],
        axis=1,
    ).reshape(2 * split, width)

    own = (device * rows).reshape(1).astype(jnp.int32)
    seq_own = jnp.concatenate(
        [seq_row, jnp.broadcast_to(seq_row[-1:], (TILE - rows,))]
    ).astype(F32)[None]
    nat = jnp.dot(rows_one, head_w, preferred_element_type=F32).astype(BF)
    tr = contract(turn_w, rows_one, 0, 1).astype(BF)
    packed, out_nat, lse, last_out, last_lse, start, start_own, end_own, meta = attend_forward(
        own, seq_own, nat, tr, rows
    )
    got = lax.all_to_all(packed, GROUP, 0, 0, tiled=True)
    half = rows // 2
    got = got.reshape(ways, half, 2, HEAD_DIM).transpose(2, 1, 0, 3).reshape(rows, split)
    attended = jnp.concatenate([got, last_out.astype(BF)], axis=1)

    resid = inputs + jnp.dot(attended, out_full, preferred_element_type=F32)
    unit_two, inverse_two = norm_stats(resid)
    low_two = (unit_two * gain_two + bias_two).astype(BF)

    d_hidden = jnp.dot(grads_all, down_turned, preferred_element_type=F32)
    rows_two = lax.all_gather(low_two, "tensor", axis=0, tiled=True)
    rows_two, d_hidden = lax.optimization_barrier((rows_two, d_hidden))
    units = up_full.shape[1]
    hidden, d_pre, partial = row_blocks(
        feed_kernel, (rows_two, d_hidden), up_full, (units, units, width)
    )
    d_normed_two = sum_tensor(partial, ways_t)

    grad_up = contract(rows_two, d_pre, 0, 0).astype(BF)
    grad_down = contract(grads_all, hidden, 0, 0).astype(BF)
    (mixed,) = row_blocks(turned_kernel, (hidden,), down_turned, (width,))

    grad_in = out_grad.astype(F32)
    d_resid = grad_in + norm_back(d_normed_two, unit_two, inverse_two, gain_two)
    d_branch = d_resid.astype(BF)

    d_wide = contract(d_branch, out_wide, 1, 1).astype(BF)
    last_grad = d_wide[:, HEAD_DIM : 2 * HEAD_DIM]
    last_delta = jnp.sum(last_grad.astype(F32) * last_out, axis=1)
    pieces = split_two(last_lse[0, :rows]) + split_two(last_delta)
    extra = jnp.pad(jnp.stack(pieces), ((0, 0), (0, TILE - rows))).reshape(8, 128)
    extra = jnp.pad(extra, ((0, 8), (0, 0)))
    payload = jnp.concatenate(
        [
            d_wide.reshape(rows, ways, 2 * HEAD_DIM).transpose(1, 0, 2),
            jnp.broadcast_to(extra[None], (ways,) + extra.shape),
        ],
        axis=1,
    )
    came = lax.all_to_all(payload, GROUP, 0, 0, tiled=True)
    mixed = lax.psum_scatter(
        after(mixed, came), "tensor", scatter_dimension=0, tiled=True
    )
    came_heads = came
    delta_own = jnp.pad(last_delta, (0, TILE - rows))[None]

    late_branch = after(d_branch, payload)

    grad_out_w = jnp.concatenate(
        [
            contract(attended, late_branch, 0, 0).astype(BF),
            jnp.sum(d_normed_two * unit_two, axis=0)[:, None].astype(BF),
            jnp.sum(d_normed_two, axis=0)[:, None].astype(BF),
            jnp.zeros((width, padded - width - 2), BF),
        ],
        axis=1,
    )
    last_qk, last_v = attend_backward_last(
        own, meta, start_own, end_own, nat, tr, came, last_lse, delta_own, rows
    )
    last_all = jnp.concatenate([last_qk, last_v], axis=1)
    chunk = padded // ways
    grad_last = contract(wide_one, last_all, 0, 0).astype(BF)
    grad_last = lax.all_to_all(
        grad_last.reshape(ways, chunk, columns), GROUP, 0, 0, tiled=True
    )

    packed, d_qk, d_v = attend_backward(meta, start, nat, tr, came, out_nat, lse, rows)
    came = lax.all_to_all(packed, GROUP, 0, 0, tiled=True)
    came_rows = came
    grad_last = jnp.sum(grad_last.astype(F32), axis=0)

    d_head = jnp.concatenate([d_qk, d_v], axis=1)
    grad_mine = contract(rows_one, d_head, 0, 0)[:width]
    wide = 256
    sums = jnp.stack(
        [jnp.sum(d_head.astype(F32), axis=0), jnp.sum(last_all.astype(F32), axis=0)]
    )
    extra = jnp.concatenate([grad_last, jnp.pad(sums, ((0, 6), (0, 0)))], axis=0)
    both = jnp.concatenate(
        [
            grad_mine.reshape(count, part_rows, columns),
            jnp.broadcast_to(extra[None], (count,) + extra.shape),
        ],
        axis=1,
    )
    both = jnp.pad(both, ((0, 0), (0, 0), (0, wide - columns)))
    both = sum_shard_rows(both.reshape(count * (part_rows + chunk + 8), wide), count)
    payload = both.astype(BF)

    pair = reduce_rows(
        jnp.concatenate([grad_up, grad_down], axis=1), count, ways_c, (grad_up, d_qk, came_rows)
    )
    grad_out_w = reduce_rows(grad_out_w, count, ways_c, (grad_out_w, came_heads, d_qk))
    piece = part_rows // ways_c
    deep = round_up(-(-piece // ways_t), 8)
    grad_out_w = jnp.pad(grad_out_w, ((0, deep * ways_t - piece), (0, 0)))
    grad_out_w = rotate(grad_out_w.reshape(ways_t, deep, padded), ways_t, last_qk)
    sent_pair = send_rows(pair, ways_c)
    grad_out_w = total([grad_out_w[0]] + [after(share, came_rows) for share in grad_out_w[1:]])
    grad_out_w = grad_out_w.astype(BF)
    pieces = lax.all_gather(payload, GROUP, axis=0, tiled=True)
    pieces = pieces.reshape((ways,) + payload.shape)
    shared_w = pieces[:, part_rows : part_rows + chunk, :columns].reshape(ways * chunk, columns)
    shared_w = lax.dynamic_slice_in_dim(
        shared_w, lax.axis_index("shard") * part_rows, part_rows, 0
    )
    grad_qkv, dots, dots_bias = join_heads(pieces, shared_w, w_qkv)
    grad_bias_one = dots_bias[:, 0]
    grad_gain_one = (dots[:, 0] - ln1_bias.astype(F32) * grad_bias_one) / ln1_gain.astype(F32)
    result = (resid + after(mixed, payload).astype(F32)).astype(BF)

    came_qk = came[:, :rows].reshape(ways, rows, 2, HEAD_DIM).transpose(1, 2, 0, 3)
    came_qk = came_qk.reshape(rows, 2, split)
    came_v = came[:, rows:].reshape(ways, half, 2, HEAD_DIM).transpose(2, 1, 0, 3)
    came_v = came_v.reshape(rows, 1, split)
    came = jnp.concatenate([came_qk, came_v], axis=1)
    d_projected = jnp.concatenate(
        [came, last_all.reshape(rows, 3, HEAD_DIM)], axis=2
    ).reshape(rows, 3 * width)
    d_normed_one = contract(d_projected, qkv_full, 1, 1)

    grad_out_w = gather_tensor(grad_out_w, ways_t, d_normed_one)[:piece]
    sent = send_rows(grad_out_w, ways_c)
    sent_pair = None if sent_pair is None else after(sent_pair, d_normed_one)
    pair = gather_rows(pair, sent_pair, ways_c).astype(F32)
    grad_up = pair[:, : up_full.shape[1]]
    grad_down = pair[:, up_full.shape[1] :].T
    grad_out_w = gather_rows(grad_out_w, sent, ways_c).astype(F32)

    input_grad = (d_resid + norm_back(d_normed_one, unit_one, inverse_one, gain_one)).astype(BF)
    return (
        result,
        input_grad,
        grad_qkv,
        grad_out_w[:, :width],
        grad_gain_one,
        grad_bias_one,
        grad_out_w[:, width],
        grad_out_w[:, width + 1],
        grad_up,
        grad_down,
    )


def solution(mesh):
    in_specs = (
        P(("shard", "context", "tensor"), None),
        P("shard", ("context", "tensor")),
        P("shard", None),
        P("shard", None),
        P("shard"),
        P("shard"),
        P("shard"),
        P("shard"),
        P("shard", "tensor"),
        P("tensor", "shard"),
        P(("shard", "context", "tensor"), None),
    )
    out_specs = (
        P(("shard", "context", "tensor"), None),
        P(("shard", "context", "tensor"), None),
        P("shard", None),
        P("shard", None),
        P("shard"),
        P("shard"),
        P("shard"),
        P("shard"),
        P("shard", "tensor"),
        P("tensor", "shard"),
    )
    return jax.shard_map(shards, mesh=mesh, in_specs=in_specs, out_specs=out_specs, check_vma=False)
```

```python
import math

import jax
import jax.numpy as jnp
from jax import lax
from jax.experimental import pallas as pl
from jax.experimental.pallas import tpu as pltpu
from jax.sharding import PartitionSpec as P


HEADS = 17
HEAD_DIM = 64
SEQS = 6
EPSILON = 1e-05
NEG = -1e30
GROUP = ("context", "tensor")
TILE = 256
BF = jnp.bfloat16
F32 = jnp.float32


def contract(left, right, left_dim, right_dim):
    return lax.dot_general(
        left, right, (((left_dim,), (right_dim,)), ((), ())), preferred_element_type=F32
    )


def norm_stats(values):
    average = jnp.mean(values, axis=-1, keepdims=True)
    centred = values - average
    variance = jnp.mean(centred * centred, axis=-1, keepdims=True)
    inverse = lax.rsqrt(variance + EPSILON)
    return centred * inverse, inverse


def norm_back(grad, unit, inverse, gain):
    scaled = grad * gain
    first = jnp.mean(scaled, axis=-1, keepdims=True)
    second = jnp.mean(scaled * unit, axis=-1, keepdims=True)
    return inverse * (scaled - first - unit * second)


def swap_shard(part):
    return lax.ppermute(part, "shard", [(0, 1), (1, 0)])


def in_order(mine, other, axis):
    index = lax.axis_index("shard")
    return jnp.where(
        index == 0,
        jnp.concatenate([mine, other], axis=axis),
        jnp.concatenate([other, mine], axis=axis),
    )


def gather_small(part, count, axis):
    if count != 2:
        return lax.all_gather(part, "shard", axis=axis, tiled=True)
    return in_order(part, swap_shard(part), axis)


def gather_large(part, count, axis):
    if count != 2:
        return lax.all_gather(part, "shard", axis=axis, tiled=True)
    ways = lax.axis_size("context")
    core = lax.rem(lax.axis_index("context"), 2)
    half = part.shape[axis] // 2
    mine = lax.dynamic_slice_in_dim(part, core * half, half, axis)
    fetched = swap_shard(mine)
    partner = lax.ppermute(fetched, "context", [(i, i ^ 1) for i in range(ways)])
    other = jnp.where(
        core == 0,
        jnp.concatenate([fetched, partner], axis=axis),
        jnp.concatenate([partner, fetched], axis=axis),
    )
    return in_order(part, other, axis)


def swap_half(blocks, bit, axis, axis_name, pairs):
    kept = lax.dynamic_index_in_dim(blocks, bit, axis, keepdims=False)
    away = lax.dynamic_index_in_dim(blocks, 1 - bit, axis, keepdims=False).astype(BF)
    came = lax.ppermute(away, axis_name, pairs)
    return kept, came


def add(kept, came):
    return kept.astype(F32) + came.astype(F32)


def sum_shard_rows(partial, count):
    if count != 2:
        return lax.psum_scatter(
            partial.astype(BF), "shard", scatter_dimension=0, tiled=True
        ).astype(F32)
    index = lax.axis_index("shard")
    blocks = partial.reshape((2, -1) + partial.shape[1:])
    return add(*swap_half(blocks, index, 0, "shard", [(0, 1), (1, 0)]))


def reduce_rows(partial, count, ways_c, gates):
    if count != 2 or ways_c != 4:
        return lax.psum_scatter(partial, ("shard", "context"), scatter_dimension=0, tiled=True)
    context = lax.axis_index("context")
    core, chip = lax.rem(context, 2), lax.div(context, 2)
    rows, columns = partial.shape
    blocks = partial.reshape(2, 2, 2, rows // 8, columns)
    kept, came = swap_half(blocks, core, 2, "context", [(i, i ^ 1) for i in range(4)])
    blocks = add(kept, after(came, gates[0])).astype(BF)
    kept, came = swap_half(blocks, chip, 1, "context", [(i, i ^ 2) for i in range(4)])
    blocks = add(kept, after(came, gates[1])).astype(BF)
    kept, came = swap_half(blocks, lax.axis_index("shard"), 0, "shard", [(0, 1), (1, 0)])
    return add(kept, after(came, gates[2])).astype(BF)


def send_rows(part, ways_c):
    if ways_c != 4:
        return None
    return lax.ppermute(part, "context", [(i, i ^ 2) for i in range(4)])


def gather_rows(part, sent, ways_c):
    if ways_c != 4:
        return lax.all_gather(part, "context", axis=0, tiled=True)
    context = lax.axis_index("context")
    core, chip = lax.rem(context, 2), lax.div(context, 2)
    both = jnp.where(chip == 0, jnp.stack([part, sent]), jnp.stack([sent, part]))
    came = lax.ppermute(both, "context", [(i, i ^ 1) for i in range(4)])
    all_rows = jnp.where(
        core == 0, jnp.stack([both, came], axis=1), jnp.stack([came, both], axis=1)
    )
    return all_rows.reshape((4 * part.shape[0],) + part.shape[1:])


def send_tensor(part, ways):
    return [part] + [
        lax.ppermute(part, "tensor", [(i, (i + turn) % ways) for i in range(ways)])
        for turn in range(1, ways)
    ]


def sum_ordered(parts, ways, gate):
    index = lax.axis_index("tensor")
    parts = jnp.stack([parts[0]] + [after(part, gate) for part in parts[1:]])
    return sum(
        lax.dynamic_index_in_dim(
            parts, lax.rem(index + ways - i, ways), 0, keepdims=False
        ).astype(F32)
        for i in range(ways)
    )


def after(value, *others):
    return lax.optimization_barrier((value,) + others)[0]


def pick_half(pair, high, scale=1.0):
    first = lax.broadcasted_iota(jnp.int32, pair.shape, 1) < HEAD_DIM
    values = pair.astype(F32) * scale
    return (jnp.where(first, 0.0, values) if high else jnp.where(first, values, 0.0)).astype(BF)


def lane_ids(count):
    return lax.broadcasted_iota(jnp.int32, (1, count), 1)


def band(shape, low, high, first_key):
    key = first_key + lax.broadcasted_iota(jnp.int32, shape, 0)
    return (key >= low) & (key <= high)


def forward_kernel(
    own, seq_own, nat, tr, packed, out_nat, lse, out_last, lse_last, start, start_own, end_own, meta,
    q_pad,
):
    rows = nat.shape[0]
    blocks = rows // TILE
    width = out_last.shape[0]
    scale = 1.0 / math.sqrt(HEAD_DIM)

    seq = tr[256:272, :].astype(F32)[0:1, :]
    mine = seq_own[...]
    begin = jnp.zeros_like(seq)
    begin_own = jnp.zeros_like(mine)
    finish_own = jnp.full_like(mine, float(rows))
    for number in range(1, SEQS):
        before = jnp.sum((seq < number).astype(F32), axis=1, keepdims=True)
        begin = jnp.where(seq >= number, before, begin)
        begin_own = jnp.where(mine >= number, before, begin_own)
        finish_own = jnp.where(mine == number - 1, before, finish_own)
    start[...] = begin.astype(jnp.int32)
    start_own[...] = begin_own.astype(jnp.int32)
    end_own[...] = finish_own.astype(jnp.int32)
    base = pl.multiple_of(own[0], 16)
    meta[2 * blocks] = jnp.min(begin_own).astype(jnp.int32) // TILE
    meta[2 * blocks + 1] = (base + width - 1) // TILE + 1
    meta[2 * blocks + 2] = base // width
    meta[2 * blocks + 3] = (jnp.max(finish_own).astype(jnp.int32) + width - 1) // width

    def step(queries, limits, v_row, low_tile, carry):
        top, total, acc = carry
        places, scores = [], []
        for tile in (low_tile, low_tile + 1):
            at = pl.multiple_of(jnp.clip(tile, 0, blocks - 1) * TILE, TILE)
            score = contract(nat[pl.ds(at, TILE), 128:256], queries, 1, 1)
            if limits is not None:
                score = jnp.where(band(score.shape, *limits, tile * TILE), score, NEG)
            places.append(at)
            scores.append(score)
        now = jnp.maximum(top, jnp.max(jnp.maximum(*scores), axis=0, keepdims=True))
        fade = jnp.exp(top - now)
        total, acc = total * fade, acc * fade
        for at, score in zip(places, scores):
            shares = jnp.exp(score - now)
            total = total + jnp.sum(shares, axis=0, keepdims=True)
            values = tr[v_row : v_row + HEAD_DIM, pl.ds(at, TILE)]
            acc = acc + contract(values, shares.astype(BF), 1, 0)
        return now, total, acc

    empty = (
        jnp.full((1, TILE), NEG, F32),
        jnp.zeros((1, TILE), F32),
        jnp.zeros((HEAD_DIM, TILE), F32),
    )

    def one_block(qb, unused):
        at = pl.multiple_of(qb * TILE, TILE)
        queries = pick_half(nat[pl.ds(at, TILE), 0:128], False, scale)
        low = start[:, pl.ds(at, TILE)]
        near = low.astype(F32)
        first = jnp.min(near).astype(jnp.int32) // TILE
        full = (jnp.max(near).astype(jnp.int32) + TILE - 1) // TILE
        plain = jnp.maximum(qb - 1 - full, 0) // 2
        every = (jnp.maximum(qb - 1 - first, 0) + 1) // 2
        meta[qb] = plain
        meta[blocks + qb] = every
        limits = (low, at + lane_ids(TILE))
        carry = step(queries, limits, 128, qb - 1, empty)
        carry = lax.fori_loop(
            0, plain, lambda j, c: step(queries, None, 128, qb - 3 - 2 * j, c), carry
        )
        carry = lax.fori_loop(
            plain, every, lambda j, c: step(queries, limits, 128, qb - 3 - 2 * j, c), carry
        )
        top, total, acc = carry
        lse[:, pl.ds(at, TILE)] = top + jnp.log(total)
        out_nat[pl.ds(at, TILE), :] = (acc / total).T
        return unused

    lax.fori_loop(0, blocks, one_block, 0)

    q_pad[...] = jnp.zeros_like(q_pad)
    q_pad[0:width, :] = pick_half(nat[pl.ds(base, width), 0:128], True, scale)
    limits = (start_own[...], base + lane_ids(TILE))
    begin_tile, end_tile = meta[2 * blocks], meta[2 * blocks + 1]
    top, total, acc = lax.fori_loop(
        0,
        (end_tile - begin_tile + 1) // 2,
        lambda j, c: step(q_pad[...], limits, 192, begin_tile + 2 * j, c),
        empty,
    )
    lse_last[...] = top + jnp.log(total)
    out_last[...] = (acc / total).T[0:width, :]

    half = width // 2
    for dest in range(rows // width):
        first = out_nat[dest * width : dest * width + half, :]
        second = out_nat[dest * width + half : (dest + 1) * width, :]
        packed[dest] = jnp.concatenate([first, second], axis=1).astype(BF)


def backward_last_kernel(
    own, meta, start_own, end_own, nat, tr, came, lse_own, delta_own, last_qk, last_v,
    q_rows, o_rows, pad_q, pad_o,
):
    rows = nat.shape[0]
    blocks = rows // TILE
    width = last_qk.shape[0]
    scale = 1.0 / math.sqrt(HEAD_DIM)
    base = pl.multiple_of(own[0], 16)

    q_rows[0:rows, :] = (nat[:, 0:128].astype(F32) * scale).astype(BF)
    q_rows[rows:, :] = jnp.zeros((q_rows.shape[0] - rows, 2 * HEAD_DIM), BF)
    for source in range(rows // width):
        o_rows[source * width : (source + 1) * width, :] = came[source, 0:width, :]
    o_rows[rows:, :] = jnp.zeros((o_rows.shape[0] - rows, 2 * HEAD_DIM), BF)

    pad_q[...] = jnp.zeros_like(pad_q)
    pad_o[...] = jnp.zeros_like(pad_o)
    pad_q[0:width, :] = pick_half(nat[pl.ds(base, width), 0:128], True, scale)
    pad_o[0:width, :] = pick_half(o_rows[pl.ds(base, width), :], True)
    limits = (start_own[...], base + lane_ids(TILE))

    begin_tile, end_tile = meta[2 * blocks], meta[2 * blocks + 1]

    def query_step(j, d_query):
        for tile in (begin_tile + 2 * j, begin_tile + 2 * j + 1):
            at = pl.multiple_of(jnp.minimum(tile, blocks - 1) * TILE, TILE)
            scores = contract(nat[pl.ds(at, TILE), 128:256], pad_q[...], 1, 1)
            scores = jnp.where(band(scores.shape, *limits, tile * TILE), scores, NEG)
            shares = jnp.exp(scores - lse_own[...])
            d_shares = contract(nat[pl.ds(at, TILE), 256:384], pad_o[...], 1, 1)
            d_scores = (shares * (d_shares - delta_own[...])).astype(BF)
            keys_t = tr[HEAD_DIM : 2 * HEAD_DIM, pl.ds(at, TILE)]
            d_query = d_query + contract(keys_t, d_scores, 1, 0)
        return d_query

    d_query = lax.fori_loop(
        0, (end_tile - begin_tile + 1) // 2, query_step, jnp.zeros((HEAD_DIM, TILE), F32)
    )
    last_qk[:, 0:HEAD_DIM] = (d_query.T[0:width, :] * scale).astype(BF)

    keys = pick_half(nat[pl.ds(base, width), 128:256], True)
    values = pick_half(nat[pl.ds(base, width), 256:384], True)
    key = base + lax.broadcasted_iota(jnp.int32, (width, TILE), 0)
    finish = jnp.broadcast_to(end_own[...].astype(F32), (128, TILE)).T[0:width, 0:1]
    finish = finish.astype(jnp.int32)
    lane = lane_ids(TILE)

    ways = rows // width

    def key_step(j, carry):
        d_key, d_value = carry
        for turn in range(2):
            query_source = begin_source + 2 * j + turn
            source = jnp.minimum(query_source, ways - 1)
            at = pl.multiple_of(source * width, 16)
            queries = q_rows[pl.ds(at, TILE), :]
            grads = o_rows[pl.ds(at, TILE), :]
            facts = came[source, width : width + 16, :].astype(F32)
            log_total = jnp.concatenate([facts[0:1] + facts[2:3], facts[1:2] + facts[3:4]], axis=1)
            delta = jnp.concatenate([facts[4:5] + facts[6:7], facts[5:6] + facts[7:8]], axis=1)
            query = query_source * width + lane
            keep = (key <= query) & (query < finish) & (lane < width)
            scores = jnp.where(keep, contract(keys, queries, 1, 1), NEG)
            shares = jnp.exp(scores - log_total)
            d_shares = contract(values, grads, 1, 1)
            d_scores = (shares * (d_shares - delta)).astype(BF)
            d_key = d_key + contract(d_scores, queries, 1, 0)
            d_value = d_value + contract(shares.astype(BF), grads, 1, 0)
        return d_key, d_value

    zero = jnp.zeros((width, 2 * HEAD_DIM), F32)
    begin_source, end_source = meta[2 * blocks + 2], meta[2 * blocks + 3]
    d_key, d_value = lax.fori_loop(
        0, (end_source - begin_source + 1) // 2, key_step, (zero, zero)
    )
    last_qk[:, HEAD_DIM:] = d_key[:, HEAD_DIM:].astype(BF)
    last_v[...] = d_value[:, HEAD_DIM:].astype(BF)


def backward_kernel(
    meta, start, nat, tr, came, out_nat, lse, packed, d_qk, d_v, o_rows, q_rows, acc_k, acc_v
):
    rows = nat.shape[0]
    blocks = rows // TILE
    width = rows // packed.shape[0]
    scale = 1.0 / math.sqrt(HEAD_DIM)

    q_rows[...] = (nat[:, 0:128].astype(F32) * scale).astype(BF)
    for source in range(rows // width):
        o_rows[source * width : (source + 1) * width, :] = came[source, 0:width, :]
    acc_k[...] = jnp.zeros_like(acc_k)
    acc_v[...] = jnp.zeros_like(acc_v)

    def one_block(qb, unused):
        at_q = pl.multiple_of(qb * TILE, TILE)
        pair = q_rows[pl.ds(at_q, TILE), :]
        queries = pick_half(pair, False)
        grads = o_rows[pl.ds(at_q, TILE), :]
        product = grads[:, 0:HEAD_DIM].astype(F32) * out_nat[pl.ds(at_q, TILE), :]
        delta = jnp.sum(product.T, axis=0, keepdims=True)
        grads_low = pick_half(grads, False)
        log_total = lse[:, pl.ds(at_q, TILE)]
        limits = (start[:, pl.ds(at_q, TILE)], at_q + lane_ids(TILE))

        def step(masked, low_tile, d_query):
            tiles = (low_tile, low_tile + 1)
            places = [pl.multiple_of(jnp.maximum(tile, 0) * TILE, TILE) for tile in tiles]
            scores = [contract(nat[pl.ds(at, TILE), 128:256], queries, 1, 1) for at in places]
            d_shares = [contract(nat[pl.ds(at, TILE), 256:384], grads_low, 1, 1) for at in places]
            if masked:
                scores = [
                    jnp.where(band(score.shape, *limits, tile * TILE), score, NEG)
                    for score, tile in zip(scores, tiles)
                ]
            shares = [jnp.exp(score - log_total) for score in scores]
            d_scores = [
                (share * (d_share - delta)).astype(BF) for share, d_share in zip(shares, d_shares)
            ]
            added_v = [contract(share.astype(BF), grads, 1, 0) for share in shares]
            added_k = [contract(d_score, pair, 1, 0) for d_score in d_scores]
            for at, d_score in zip(places, d_scores):
                d_query = d_query + contract(tr[0:HEAD_DIM, pl.ds(at, TILE)], d_score, 1, 0)
            for at, value, key in zip(places, added_v, added_k):
                acc_v[pl.ds(at, TILE), :] += value
                acc_k[pl.ds(at, TILE), :] += key
            return d_query

        plain, every = meta[qb], meta[blocks + qb]
        d_query = step(True, qb - 1, jnp.zeros((HEAD_DIM, TILE), F32))
        d_query = lax.fori_loop(0, plain, lambda j, c: step(False, qb - 3 - 2 * j, c), d_query)
        d_query = lax.fori_loop(plain, every, lambda j, c: step(True, qb - 3 - 2 * j, c), d_query)
        d_qk[pl.ds(at_q, TILE), 0:HEAD_DIM] = (d_query.T * scale).astype(BF)
        return unused

    lax.fori_loop(0, blocks, one_block, 0)
    d_qk[:, HEAD_DIM:] = acc_k[:, 0:HEAD_DIM].astype(BF)
    d_v[...] = acc_v[:, 0:HEAD_DIM].astype(BF)
    half = width // 2
    for dest in range(rows // width):
        low_rows = slice(dest * width, dest * width + half)
        high_rows = slice(dest * width + half, (dest + 1) * width)
        packed[dest, 0:width, :] = d_qk[dest * width : (dest + 1) * width, :]
        packed[dest, width:, :] = jnp.concatenate([d_v[low_rows, :], d_v[high_rows, :]], axis=1)


def kernel_call(kernel, scalars, operands, outs, scratch, work, smem_out=None):
    vmem = pl.BlockSpec(memory_space=pltpu.VMEM)
    smem = pl.BlockSpec(memory_space=pltpu.SMEM)
    out_shape = [jax.ShapeDtypeStruct(shape, kind) for shape, kind in outs]
    out_specs = [vmem] * len(outs)
    if smem_out is not None:
        out_shape.append(jax.ShapeDtypeStruct((smem_out,), jnp.int32))
        out_specs.append(smem)
    return pl.pallas_call(
        kernel,
        out_shape=tuple(out_shape),
        in_specs=[smem] * len(scalars) + [vmem] * len(operands),
        out_specs=tuple(out_specs),
        scratch_shapes=[pltpu.VMEM(shape, kind) for shape, kind in scratch],
        cost_estimate=pl.CostEstimate(flops=work, bytes_accessed=8 << 20, transcendentals=0),
    )(*scalars, *operands)


def attend_forward(own, seq_own, nat, tr, width):
    rows = nat.shape[0]
    pair = 2 * HEAD_DIM
    return kernel_call(
        forward_kernel,
        (own,),
        (seq_own, nat, tr),
        [
            ((rows // width, width // 2, pair), BF),
            ((rows, HEAD_DIM), F32),
            ((1, rows), F32),
            ((width, HEAD_DIM), F32),
            ((1, TILE), F32),
            ((1, rows), jnp.int32),
            ((1, TILE), jnp.int32),
            ((1, TILE), jnp.int32),
        ],
        [((TILE, pair), BF)],
        16 * rows * rows * HEAD_DIM,
        2 * (rows // TILE) + 4,
    )


def attend_backward_last(own, meta, start_own, end_own, nat, tr, came, lse_own, delta_own, width):
    rows = nat.shape[0]
    pair = 2 * HEAD_DIM
    return kernel_call(
        backward_last_kernel,
        (own, meta),
        (start_own, end_own, nat, tr, came, lse_own, delta_own),
        [((width, pair), BF), ((width, HEAD_DIM), BF)],
        [((rows + TILE - width, pair), BF)] * 2 + [((TILE, pair), BF)] * 2,
        4 * rows * rows * HEAD_DIM,
    )


def attend_backward(meta, start, nat, tr, came, out_nat, lse, width):
    rows = nat.shape[0]
    pair = 2 * HEAD_DIM
    return kernel_call(
        backward_kernel,
        (meta,),
        (start, nat, tr, came, out_nat, lse),
        [
            ((rows // width, width + width // 2, pair), BF),
            ((rows, pair), BF),
            ((rows, HEAD_DIM), BF),
        ],
        [((rows, pair), BF)] * 2 + [((rows, pair), F32)] * 2,
        40 * rows * rows * HEAD_DIM,
    )


def join_kernel(pieces, shared, weights, facts, joined, dots, dots_bias):
    heads = pieces.shape[0]
    running = [jnp.zeros((joined.shape[0], 2 * HEAD_DIM), F32)] * 2
    rest = [0.0, 0.0]
    units = 3 * (heads + 1)

    def unit(index):
        part, head = divmod(index, heads + 1)
        columns = slice(part * HEAD_DIM, (part + 1) * HEAD_DIM)
        return shared[:, columns] if head == heads else pieces[head, :, columns]

    facts_of = [facts[head].astype(F32) for head in range(heads)]
    sums = [fact[0:1, :] for fact in facts_of] + [sum(fact[1:2, :] for fact in facts_of)]

    def unit_sum(index):
        part, head = divmod(index, heads + 1)
        return sums[head][:, part * HEAD_DIM : (part + 1) * HEAD_DIM]

    for block in range((units + 1) // 2):
        paired = 2 * block + 1 < units
        if paired:
            values = jnp.concatenate([unit(2 * block), unit(2 * block + 1)], axis=1)
        else:
            values = unit(2 * block)
        at = slice(2 * block * HEAD_DIM, 2 * block * HEAD_DIM + values.shape[1])
        values = values.astype(F32)
        joined[:, at] = values
        weight = weights[:, at].astype(F32)
        row = [unit_sum(2 * block + i) for i in range(1 + paired)]
        products = [values * weight, weight * jnp.concatenate(row, axis=1)]
        if paired:
            running = [so_far + product for so_far, product in zip(running, products)]
        else:
            rest = [jnp.sum(product, axis=1, keepdims=True) for product in products]
    dots[...] = jnp.sum(running[0], axis=1, keepdims=True) + rest[0]
    dots_bias[...] = jnp.sum(running[1], axis=1, keepdims=True) + rest[1]


def join_heads(pieces, shared, weights):
    heads, _, columns = pieces.shape
    rows = weights.shape[0]
    step = 272 if rows % 272 == 0 else rows
    return pl.pallas_call(
        join_kernel,
        grid=(rows // step,),
        out_shape=(
            jax.ShapeDtypeStruct(weights.shape, F32),
            jax.ShapeDtypeStruct((rows, 1), F32),
            jax.ShapeDtypeStruct((rows, 1), F32),
        ),
        in_specs=[
            pl.BlockSpec((heads, step, columns), lambda i: (0, i, 0)),
            pl.BlockSpec((step, shared.shape[1]), lambda i: (i, 0)),
            pl.BlockSpec((step, weights.shape[1]), lambda i: (i, 0)),
            pl.BlockSpec((heads, 8, columns), lambda i: (0, pieces.shape[1] // 8 - 1, 0)),
        ],
        out_specs=(
            pl.BlockSpec((step, weights.shape[1]), lambda i: (i, 0)),
            pl.BlockSpec((step, 1), lambda i: (i, 0)),
            pl.BlockSpec((step, 1), lambda i: (i, 0)),
        ),
        cost_estimate=pl.CostEstimate(flops=1 << 20, bytes_accessed=14 << 20, transcendentals=0),
        name="join_heads",
    )(pieces, shared, weights, pieces)


def gelu_pair(pre):
    factor = math.sqrt(2.0 / math.pi)
    square = pre * pre
    bend = jnp.tanh(factor * (pre + 0.044715 * pre * square))
    value = 0.5 * pre * (1.0 + bend)
    slope = 0.5 * (1.0 + bend) + 0.5 * pre * (1.0 - bend * bend) * factor * (
        1.0 + 3.0 * 0.044715 * square
    )
    return value, slope


def feed_kernel(rows, d_hidden, up, hidden, d_pre, partial):
    value, slope = gelu_pair(jnp.dot(rows[...], up[...], preferred_element_type=F32))
    hidden[...] = value.astype(BF)
    grads = (d_hidden[...] * slope).astype(BF)
    d_pre[...] = grads
    partial[...] = contract(grads, up[...], 1, 1).astype(BF)


def turned_kernel(left, right, out):
    out[...] = contract(left[...], right[...], 1, 1).astype(BF)


def row_blocks(kernel, by_rows, whole, outs):
    count = by_rows[0].shape[0]
    step = count // 2

    def block(columns):
        return pl.BlockSpec((step, columns), lambda i: (i, 0))

    return pl.pallas_call(
        kernel,
        grid=(count // step,),
        out_shape=tuple(jax.ShapeDtypeStruct((count, columns), BF) for columns in outs),
        in_specs=[block(part.shape[1]) for part in by_rows]
        + [pl.BlockSpec(whole.shape, lambda i: (0, 0), pipeline_mode=pl.Buffered(1))],
        out_specs=tuple(block(columns) for columns in outs),
        cost_estimate=pl.CostEstimate(
            flops=2 * count * whole.size, bytes_accessed=8 << 20, transcendentals=0
        ),
    )(*by_rows, whole)


def split_two(values):
    high = values.astype(BF)
    low = (values - high.astype(F32)).astype(BF)
    return [high, low]


def round_up(value, step):
    return (value + step - 1) // step * step


def sum_tensor(partial, ways):
    rows = partial.shape[0] // ways
    got = lax.all_to_all(
        partial.astype(BF).reshape(ways, rows, partial.shape[1]), "tensor", 0, 0, tiled=True
    )
    return jnp.sum(got.astype(F32), axis=0)


def head_columns(matrix, head, width):
    return [
        lax.dynamic_slice_in_dim(matrix, part * width + head * HEAD_DIM, HEAD_DIM, 1)
        for part in range(3)
    ]


def shards(
    tokens, segments, w_qkv, w_out, ln1_gain, ln1_bias, ln2_gain, ln2_bias, w_up, w_down, out_grad
):
    rows, width = tokens.shape
    count = lax.axis_size("shard")
    ways_c = lax.axis_size("context")
    ways_t = lax.axis_size("tensor")
    ways = ways_c * ways_t
    part_rows = w_qkv.shape[0]
    device = lax.axis_index(GROUP)
    shared = HEADS - 1
    padded = round_up(width, 128)
    columns = 3 * HEAD_DIM

    vectors = gather_small(
        jnp.stack([ln1_gain, ln1_bias, ln2_gain, ln2_bias]), count, 1
    ).astype(F32)
    gain_one, bias_one, gain_two, bias_two = [vectors[i : i + 1] for i in range(4)]

    inputs = tokens.astype(F32)
    unit_one, inverse_one = norm_stats(inputs)
    low_one = (unit_one * gain_one + bias_one).astype(BF)
    seq_row = segments[0]
    wide_one = jnp.concatenate(
        [low_one, seq_row[:, None].astype(BF), jnp.zeros((rows, padded - width - 1), BF)], axis=1
    )
    rows_one = lax.all_gather(wide_one, GROUP, axis=0, tiled=True)

    mine = head_columns(w_qkv, device, width)
    last = [
        w_qkv[:, part * width + shared * HEAD_DIM : part * width + (shared + 1) * HEAD_DIM]
        for part in range(3)
    ]
    head_w = gather_small(
        jnp.concatenate([mine[0], last[0], mine[1], last[1], mine[2], last[2]], axis=1),
        count,
        0,
    )
    head_w = jnp.pad(head_w, ((0, padded - width), (0, 0)))
    mark = (jnp.arange(padded)[:, None] == width) & (jnp.arange(16)[None] == 0)
    turn_w = jnp.concatenate([head_w[:, 2 * HEAD_DIM :], mark.astype(BF)], axis=1)
    out_full = gather_large(w_out, count, 0)
    up_full = gather_large(w_up, count, 0)
    down_turned = gather_large(w_down.T, count, 0)
    qkv_full = gather_large(w_qkv, count, 0)
    grads_all = lax.all_gather(out_grad, "tensor", axis=0, tiled=True)
    split = ways * HEAD_DIM
    out_wide = jnp.concatenate(
        [
            out_full[:split].reshape(ways, HEAD_DIM, width),
            jnp.broadcast_to(out_full[None, split:], (ways, HEAD_DIM, width)),
        ],
        axis=1,
    ).reshape(2 * split, width)

    own = (device * rows).reshape(1).astype(jnp.int32)
    seq_own = jnp.concatenate(
        [seq_row, jnp.broadcast_to(seq_row[-1:], (TILE - rows,))]
    ).astype(F32)[None]
    nat = jnp.dot(rows_one, head_w, preferred_element_type=F32).astype(BF)
    tr = contract(turn_w, rows_one, 0, 1).astype(BF)
    packed, out_nat, lse, last_out, last_lse, start, start_own, end_own, meta = attend_forward(
        own, seq_own, nat, tr, rows
    )
    got = lax.all_to_all(packed, GROUP, 0, 0, tiled=True)
    half = rows // 2
    got = got.reshape(ways, half, 2, HEAD_DIM).transpose(2, 1, 0, 3).reshape(rows, split)
    attended = jnp.concatenate([got, last_out.astype(BF)], axis=1)

    resid = inputs + jnp.dot(attended, out_full, preferred_element_type=F32)
    unit_two, inverse_two = norm_stats(resid)
    low_two = (unit_two * gain_two + bias_two).astype(BF)

    d_hidden = jnp.dot(grads_all, down_turned, preferred_element_type=F32)
    rows_two = lax.all_gather(low_two, "tensor", axis=0, tiled=True)
    rows_two, d_hidden = lax.optimization_barrier((rows_two, d_hidden))
    units = up_full.shape[1]
    hidden, d_pre, partial = row_blocks(
        feed_kernel, (rows_two, d_hidden), up_full, (units, units, width)
    )
    d_normed_two = sum_tensor(partial, ways_t)

    grad_up = contract(rows_two, d_pre, 0, 0).astype(BF)
    grad_down = contract(grads_all, hidden, 0, 0).astype(BF)
    (mixed,) = row_blocks(turned_kernel, (hidden,), down_turned, (width,))

    grad_in = out_grad.astype(F32)
    d_resid = grad_in + norm_back(d_normed_two, unit_two, inverse_two, gain_two)
    d_branch = d_resid.astype(BF)

    d_wide = contract(d_branch, out_wide, 1, 1).astype(BF)
    last_grad = d_wide[:, HEAD_DIM : 2 * HEAD_DIM]
    last_delta = jnp.sum(last_grad.astype(F32) * last_out, axis=1)
    pieces = split_two(last_lse[0, :rows]) + split_two(last_delta)
    extra = jnp.pad(jnp.stack(pieces), ((0, 0), (0, TILE - rows))).reshape(8, 128)
    extra = jnp.pad(extra, ((0, 8), (0, 0)))
    payload = jnp.concatenate(
        [
            d_wide.reshape(rows, ways, 2 * HEAD_DIM).transpose(1, 0, 2),
            jnp.broadcast_to(extra[None], (ways,) + extra.shape),
        ],
        axis=1,
    )
    came = lax.all_to_all(payload, GROUP, 0, 0, tiled=True)
    mixed = lax.psum_scatter(
        after(mixed, came), "tensor", scatter_dimension=0, tiled=True
    )
    came_heads = came
    delta_own = jnp.pad(last_delta, (0, TILE - rows))[None]

    late_branch = after(d_branch, payload)

    grad_out_w = jnp.concatenate(
        [
            contract(attended, late_branch, 0, 0).astype(BF),
            jnp.sum(d_normed_two * unit_two, axis=0)[:, None].astype(BF),
            jnp.sum(d_normed_two, axis=0)[:, None].astype(BF),
            jnp.zeros((width, padded - width - 2), BF),
        ],
        axis=1,
    )
    last_qk, last_v = attend_backward_last(
        own, meta, start_own, end_own, nat, tr, came, last_lse, delta_own, rows
    )
    last_all = jnp.concatenate([last_qk, last_v], axis=1)
    chunk = padded // ways
    grad_last = contract(wide_one, last_all, 0, 0).astype(BF)
    grad_last = lax.all_to_all(
        grad_last.reshape(ways, chunk, columns), GROUP, 0, 0, tiled=True
    )

    packed, d_qk, d_v = attend_backward(meta, start, nat, tr, came, out_nat, lse, rows)
    came = lax.all_to_all(packed, GROUP, 0, 0, tiled=True)
    came_rows = came
    grad_last = jnp.sum(grad_last.astype(F32), axis=0)

    d_head = jnp.concatenate([d_qk, d_v], axis=1)
    grad_mine = contract(rows_one, d_head, 0, 0)[:width]
    wide = 256
    sums = jnp.stack(
        [jnp.sum(d_head.astype(F32), axis=0), jnp.sum(last_all.astype(F32), axis=0)]
    )
    extra = jnp.concatenate([grad_last, jnp.pad(sums, ((0, 6), (0, 0)))], axis=0)
    both = jnp.concatenate(
        [
            grad_mine.reshape(count, part_rows, columns),
            jnp.broadcast_to(extra[None], (count,) + extra.shape),
        ],
        axis=1,
    )
    both = jnp.pad(both, ((0, 0), (0, 0), (0, wide - columns)))
    both = sum_shard_rows(both.reshape(count * (part_rows + chunk + 8), wide), count)
    payload = both.astype(BF)

    pair = reduce_rows(
        jnp.concatenate([grad_up, grad_down], axis=1), count, ways_c, (grad_up, d_qk, came_rows)
    )
    grad_out_w = reduce_rows(grad_out_w, count, ways_c, (grad_out_w, came_heads, d_qk))
    grad_out_w = send_tensor(grad_out_w, ways_t)
    sent_pair = send_rows(pair, ways_c)
    grad_out_w = sum_ordered(grad_out_w, ways_t, came_rows).astype(BF)
    sent_out = send_rows(grad_out_w, ways_c)
    pieces = lax.all_gather(payload, GROUP, axis=0, tiled=True)
    pieces = pieces.reshape((ways,) + payload.shape)
    shared_w = pieces[:, part_rows : part_rows + chunk, :columns].reshape(ways * chunk, columns)
    shared_w = lax.dynamic_slice_in_dim(
        shared_w, lax.axis_index("shard") * part_rows, part_rows, 0
    )
    grad_qkv, dots, dots_bias = join_heads(pieces, shared_w, w_qkv)
    grad_bias_one = dots_bias[:, 0]
    grad_gain_one = (dots[:, 0] - ln1_bias.astype(F32) * grad_bias_one) / ln1_gain.astype(F32)
    result = (resid + after(mixed, payload).astype(F32)).astype(BF)

    came_qk = came[:, :rows].reshape(ways, rows, 2, HEAD_DIM).transpose(1, 2, 0, 3)
    came_qk = came_qk.reshape(rows, 2, split)
    came_v = came[:, rows:].reshape(ways, half, 2, HEAD_DIM).transpose(2, 1, 0, 3)
    came_v = came_v.reshape(rows, 1, split)
    came = jnp.concatenate([came_qk, came_v], axis=1)
    d_projected = jnp.concatenate(
        [came, last_all.reshape(rows, 3, HEAD_DIM)], axis=2
    ).reshape(rows, 3 * width)
    d_normed_one = contract(d_projected, qkv_full, 1, 1)

    sent_pair = None if sent_pair is None else after(sent_pair, d_normed_one)
    pair = gather_rows(pair, sent_pair, ways_c).astype(F32)
    grad_up = pair[:, : up_full.shape[1]]
    grad_down = pair[:, up_full.shape[1] :].T
    sent_out = None if sent_out is None else after(sent_out, d_normed_one)
    grad_out_w = gather_rows(grad_out_w, sent_out, ways_c).astype(F32)

    input_grad = (d_resid + norm_back(d_normed_one, unit_one, inverse_one, gain_one)).astype(BF)
    return (
        result,
        input_grad,
        grad_qkv,
        grad_out_w[:, :width],
        grad_gain_one,
        grad_bias_one,
        grad_out_w[:, width],
        grad_out_w[:, width + 1],
        grad_up,
        grad_down,
    )


def solution(mesh):
    in_specs = (
        P(("shard", "context", "tensor"), None),
        P("shard", ("context", "tensor")),
        P("shard", None),
        P("shard", None),
        P("shard"),
        P("shard"),
        P("shard"),
        P("shard"),
        P("shard", "tensor"),
        P("tensor", "shard"),
        P(("shard", "context", "tensor"), None),
    )
    out_specs = (
        P(("shard", "context", "tensor"), None),
        P(("shard", "context", "tensor"), None),
        P("shard", None),
        P("shard", None),
        P("shard"),
        P("shard"),
        P("shard"),
        P("shard"),
        P("shard", "tensor"),
        P("tensor", "shard"),
    )
    return jax.shard_map(shards, mesh=mesh, in_specs=in_specs, out_specs=out_specs, check_vma=False)
```
